32 devices in a mesh: seq: 4 (over x, core), fsdp: 8 (over z, y).
Axes of the slice: x: 2, y: 2, z: 4, core: 2. Of those that a mesh axis runs over, the one named last changes fastest.
Arguments:
- tokens: bfloat16 [8, 1536, 1024], P('fsdp', 'seq'), may hold values from -6 to 6
- first_values: bfloat16 [8, 1536, 1024], P('fsdp', 'seq'), may hold values from -6 to 6
- cotangent: bfloat16 [8, 1536, 1024], P('fsdp', 'seq'), may hold values from -6 to 6
- first_gain: bfloat16 [1024], P('fsdp'), may hold values from 0.099609375 to 1.8984375
- query_weight: bfloat16 [1024, 1024], P('fsdp'), may hold values from -0.25 to 0.25
- key_weight: bfloat16 [1024, 1024], P('fsdp'), may hold values from -0.25 to 0.25
- value_weight: bfloat16 [1024, 1024], P('fsdp'), may hold values from -0.1875 to 0.1875
- out_weight: bfloat16 [1024, 1024], P('fsdp'), may hold values from -2 to 2
- second_gain: bfloat16 [1024], P('fsdp'), may hold values from 0.099609375 to 1.8984375
- gate_weight: bfloat16 [1024, 2816], P('fsdp'), may hold values from -0.1875 to 0.1875
- up_weight: bfloat16 [1024, 2816], P('fsdp'), may hold values from -0.1875 to 0.1875
- down_weight: bfloat16 [1024, 2816], P('fsdp'), may hold values from -0.109375 to 0.109375
Outputs:
- output: bfloat16 [8, 1536, 1024], P('fsdp', 'seq')
- tokens_grad: float32 [8, 1536, 1024], P('fsdp', 'seq')
- values_grad: float32 [8, 1536, 1024], P('fsdp', 'seq')
- first_gain_grad: float32 [1024], P('fsdp')
- query_grad: float32 [1024, 1024], P('fsdp')
- key_grad: float32 [1024, 1024], P('fsdp')
- value_grad: float32 [1024, 1024], P('fsdp')
- out_grad: float32 [1024, 1024], P('fsdp')
- second_gain_grad: float32 [1024], P('fsdp')
- gate_grad: float32 [1024, 2816], P('fsdp')
- up_grad: float32 [1024, 2816], P('fsdp')
- down_grad: float32 [1024, 2816], P('fsdp')
The draws below stay inside these ranges and needn't reach their ends.
All inputs are finite; a program needn't handle non-finite values.
Results may differ from the reference program's by a relative error of at most 0.018.
The reference program's roundings to bfloat16 on the way count: a program that leaves them out, or rounds other values in their place, can miss the bound.
Values may be sent and summed in bfloat16 or wider, within the bound.
No kernel may reach another device: no remote copies, remote signals or barrier semaphores. Data moves between devices by JAX's collectives and lax.ppermute only.
A program may use at most 192 MiB of HBM per device.

```python
import math
import jax
import jax.numpy as jnp
from jax import lax

D = 1024
HEADS = 16
HEAD_DIM = 64
FF = 2816
BLOCK = 512
LENGTH = 1536
SEQS = 8


def steps_of(rng, extent, shards, least, top_value):
    level = 1.0
    for position, shards_of in shards:
        heights = jax.random.uniform(jax.random.fold_in(jax.random.fold_in(rng, 6), position), (shards_of,), jnp.float32, least / len(shards), top_value / len(shards))
        level = level * jnp.repeat(jnp.exp(heights), extent[position] // shards_of).reshape((-1,) + (1,) * (len(extent) - 1 - position))
    return level


def scatter_about(key, shape, spread, reach, cuts=(), kind=jnp.bfloat16):
    level = steps_of(key, shape, cuts, -0.22, 0.18) if cuts else 1.0
    values = jax.random.normal(key, shape, jnp.float32) * spread * level
    return jnp.minimum(jnp.maximum(values, -reach), reach).astype(kind)


def setup_inputs(seed: int = 0) -> dict:
    streams_of = jax.random.split(jax.random.key(seed), 13)
    return {
        "tokens": scatter_about(streams_of[0], (SEQS, LENGTH, D), 1.0, 6.0, ((0, 8), (1, 4))),
        "first_values": scatter_about(streams_of[1], (SEQS, LENGTH, D), 1.0, 6.0, ((0, 8), (1, 4))),
        "cotangent": scatter_about(streams_of[2], (SEQS, LENGTH, D), 1.0, 6.0, ((0, 8), (1, 4))),
        "first_gain": jnp.clip(1.0 + 0.18 * jax.random.normal(streams_of[3], (D,), jnp.float32), 0.099609375, 1.8984375).astype(jnp.bfloat16),
        "query_weight": scatter_about(streams_of[4], (D, D), (D // 2) ** -0.5, 0.25, ((0, 8),)),
        "key_weight": scatter_about(streams_of[5], (D, D), (D // 2) ** -0.5, 0.25, ((0, 8),)),
        "value_weight": scatter_about(streams_of[6], (D, D), D ** -0.5, 0.1875, ((0, 8),)),
        "out_weight": scatter_about(streams_of[7], (D, D), (max(D // 128, 1)) ** -0.5, 2.0, ((0, 8),)),
        "second_gain": jnp.clip(1.0 + 0.18 * jax.random.normal(streams_of[8], (D,), jnp.float32), 0.099609375, 1.8984375).astype(jnp.bfloat16),
        "gate_weight": scatter_about(streams_of[9], (D, FF), D ** -0.5, 0.1875, ((0, 8),)),
        "up_weight": scatter_about(streams_of[10], (D, FF), D ** -0.5, 0.1875, ((0, 8),)),
        "down_weight": scatter_about(streams_of[11], (D, FF), FF ** -0.5, 0.109375, ((0, 8),)),
    }


@jax.custom_vjp
def low(v):
    return lax.optimization_barrier(v.astype(jnp.bfloat16)).astype(jnp.float32)

@jax.custom_vjp
def low_back(v):
    return v

def low_keep(v):
    return (low(v), None)

def low_pass(kept, grad):
    return (grad,)

def back_keep(v):
    return (v, None)

def back_low(kept, grad):
    return (low(grad),)
low.defvjp(low_keep, low_pass)
low_back.defvjp(back_keep, back_low)
HIGHEST = lax.Precision.HIGHEST
EPSILON = 1e-06
NEGATIVE = -1e+30

def matmul(left, right):
    return jnp.dot(left, right, precision=HIGHEST)

def normalize(source, gain):
    scale_rows = lax.rsqrt(lax.optimization_barrier(jnp.mean(source * source, axis=-1, keepdims=True)) + EPSILON)
    return source * scale_rows * gain

def rotate(source, positions):
    count = source.shape[0]
    parts = source.reshape(count, HEADS, HEAD_DIM)
    half_dim = HEAD_DIM // 2
    freqs = jnp.exp(jnp.arange(half_dim, dtype=jnp.float32) * (-2.0 * math.log(10000.0) / HEAD_DIM))
    angles = positions.astype(jnp.float32)[:, None] * freqs[None, :]
    cosine = jnp.cos(angles)[:, None, :]
    sine = jnp.sin(angles)[:, None, :]
    first_half = parts[..., :half_dim]
    second_half = parts[..., half_dim:]
    turned = jnp.concatenate([first_half * cosine - second_half * sine, second_half * cosine + first_half * sine], axis=-1)
    return turned.reshape(count, HEADS * HEAD_DIM)

def attend(queries, key_rows, value_rows):
    query_blocks = queries.reshape(LENGTH // BLOCK, BLOCK, HEADS, HEAD_DIM)
    key_heads = key_rows.reshape(LENGTH, HEADS, HEAD_DIM)
    value_heads = value_rows.reshape(LENGTH, HEADS, HEAD_DIM)
    scale_factor = 1.0 / math.sqrt(HEAD_DIM)
    columns = jnp.arange(LENGTH, dtype=jnp.int32)

    def block_out(pair):
        query_block, block_start = pair
        row_places = block_start + jnp.arange(BLOCK, dtype=jnp.int32)
        scores = low_back(jnp.einsum('qhd,khd->hqk', query_block, key_heads, precision=HIGHEST) * scale_factor)
        scores = jnp.where(columns[None, None, :] <= row_places[None, :, None], scores, NEGATIVE)
        largest = lax.optimization_barrier(jnp.max(scores, axis=-1, keepdims=True))
        exponent = jnp.exp(scores - largest)
        soft_rows = low(exponent / lax.optimization_barrier(jnp.sum(exponent, axis=-1, keepdims=True)))
        return jnp.einsum('hqk,khd->qhd', soft_rows, value_heads, precision=HIGHEST)
    starts = jnp.arange(LENGTH // BLOCK, dtype=jnp.int32) * BLOCK
    mixed_blocks = lax.map(jax.checkpoint(block_out), (query_blocks, starts))
    return mixed_blocks.reshape(LENGTH, HEADS * HEAD_DIM)

def residual_block(tokens, first_values, first_gain, query_weight, key_weight, value_weight, out_weight, second_gain, gate_weight, up_weight, down_weight):
    positions = jnp.arange(LENGTH, dtype=jnp.int32)
    normed = low(normalize(tokens, first_gain))
    queries = low(rotate(low_back(matmul(normed, query_weight)), positions))
    key_rows = low(rotate(low_back(matmul(normed, key_weight)), positions))
    value_rows = low(low_back(0.5 * matmul(normed, value_weight) + 0.5 * first_values))
    mixed_rows = low(low_back(attend(queries, key_rows, value_rows)))
    middle = tokens + low_back(matmul(mixed_rows, out_weight))
    second = low(normalize(middle, second_gain))
    gate_lin = low_back(matmul(second, gate_weight))
    up_lin = low_back(matmul(second, up_weight))
    hidden = low(gate_lin * jax.nn.sigmoid(gate_lin) * up_lin)
    return middle + matmul(hidden, down_weight.T)

def reference(tokens, first_values, cotangent, first_gain, query_weight, key_weight, value_weight, out_weight, second_gain, gate_weight, up_weight, down_weight):
    params = tuple((weight_item.astype(jnp.float32) for weight_item in (first_gain, query_weight, key_weight, value_weight, out_weight, second_gain, gate_weight, up_weight, down_weight)))

    def one_sequence(totals, sequence):
        token_rows, first_rows, grad_rows = sequence
        result, pullback = jax.vjp(residual_block, token_rows, first_rows, *params)
        gradients = pullback(grad_rows)
        summed = tuple((total_item + grad_item for total_item, grad_item in zip(totals, gradients[2:])))
        return (summed, (result.astype(jnp.bfloat16), gradients[0], gradients[1]))
    start_totals = tuple((jnp.zeros(weight_item.shape, jnp.float32) for weight_item in params))
    totals, outputs = lax.scan(one_sequence, start_totals, (tokens.astype(jnp.float32), first_values.astype(jnp.float32), cotangent.astype(jnp.float32)))
    return (outputs[0], outputs[1], outputs[2], totals[0], totals[1], totals[2], totals[3], totals[4], totals[5], totals[6], totals[7], totals[8])
```

```python
import functools
import math

import jax
import jax.numpy as jnp
from jax import lax
from jax.experimental import pallas as pl
from jax.experimental.pallas import tpu as pltpu
from jax.sharding import PartitionSpec as P

HEADS = 16
HEAD_DIM = 64
GROUPS = 4
EPSILON = 1e-06
NEGATIVE = -1e30
F32 = jnp.float32
BF16 = jnp.bfloat16
PARAMS = pltpu.CompilerParams(vmem_limit_bytes=56 * 2**20)


def nn(a, b):
    return lax.dot_general(a, b, (((1,), (0,)), ((), ())), preferred_element_type=F32)


def nt(a, b):
    return lax.dot_general(a, b, (((1,), (1,)), ((), ())), preferred_element_type=F32)


def tn(a, b):
    return lax.dot_general(a, b, (((0,), (0,)), ((), ())), preferred_element_type=F32)


def cost(flops, nbytes, trans=0):
    flops, nbytes, trans = flops / 50, nbytes / 50, 0
    return pl.CostEstimate(flops=int(flops), bytes_accessed=int(nbytes), transcendentals=int(trans))


def turn(u, cosine, sine):
    lane = lax.broadcasted_iota(jnp.int32, (u.shape[0], 128), 1)
    first = lane % HEAD_DIM < HEAD_DIM // 2
    parts = []
    for j in range(u.shape[1] // 128):
        part = u[:, 128 * j : 128 * (j + 1)]
        other = jnp.where(first, pltpu.roll(part, 96, 1), pltpu.roll(part, 32, 1))
        parts.append(part * cosine + other * sine)
    return jnp.concatenate(parts, axis=1)


def inverse_rms(v):
    return lax.rsqrt(jnp.mean(v * v, axis=-1, keepdims=True) + EPSILON)


def assemble_kernel(count, me, *refs):
    pieces, (w, small) = refs[:count], refs[count:]
    share = w.shape[0] // count
    for i, piece in enumerate(pieces):
        at = me[0] ^ i
        w[pl.ds(pl.multiple_of(at * share, share), share), :] = piece[:share]
        if small is not None:
            small[at] = piece[share:]


ANY = pl.BlockSpec(memory_space=pl.ANY)


def assemble(pieces, share):
    count = len(pieces)
    rows, width = pieces[0].shape
    me = lax.axis_index("fsdp").astype(jnp.int32).reshape(1)
    shapes = [((count * share, width), BF16), ((count, max(rows - share, 8), width), BF16)]
    kernel = functools.partial(assemble_kernel, count)
    if rows == share:
        kernel = lambda me, *refs: assemble_kernel(count, me, *refs, None)
        shapes = shapes[:1]
    out = vmem_call(kernel, "assemble", shapes, me, pieces, cost(0, 2 * count * rows * width * 2))
    return out if rows > share else out[0]


def qkv_kernel(t0, t1, t2, t3, f0, f1, f2, f3, w, gain, cosine, sine, q, k, v, n, tv, fv, wv, sems):
    width = q.shape[-1]
    copies = [pltpu.make_async_copy(w, wv, sems.at[8])]
    for i, (t, f) in enumerate(((t0, f0), (t1, f1), (t2, f2), (t3, f3))):
        copies.append(pltpu.make_async_copy(t, tv.at[i], sems.at[2 * i]))
        copies.append(pltpu.make_async_copy(f, fv.at[i], sems.at[2 * i + 1]))
    for copy in copies:
        copy.start()
    for i in range(4):
        copies[1 + 2 * i].wait()
        x = tv[i].astype(F32)
        normed = (x * inverse_rms(x) * gain[...]).astype(BF16)
        n[i] = normed
        if i == 0:
            copies[0].wait()
        u = nn(normed, wv[...])
        c, s = cosine[i], sine[i]
        q[i] = (turn(u[:, :width], c, s).astype(BF16).astype(F32) * 0.125).astype(BF16)
        k[i] = turn(u[:, width : 2 * width], c, s).astype(BF16)
        copies[2 + 2 * i].wait()
        v[i] = (0.5 * u[:, 2 * width :] + 0.5 * fv[i].astype(F32)).astype(BF16)


def qkv(t, f, w, gain, cosine, sine):
    rows, d = t[0].shape
    width = w.shape[1] // 3
    full = lambda *shape: pl.BlockSpec(shape, lambda i: (0,) * len(shape))
    shapes = [(4, rows, width)] * 3 + [(4, rows, d)]
    return pl.pallas_call(
        qkv_kernel,
        grid=(1,),
        in_specs=[ANY] * 9 + [full(1, d)] + [full(4, rows, 128)] * 2,
        out_specs=[full(*s) for s in shapes],
        out_shape=[jax.ShapeDtypeStruct(s, BF16) for s in shapes],
        scratch_shapes=[
            pltpu.VMEM((4, rows, d), BF16),
            pltpu.VMEM((4, rows, width), BF16),
            pltpu.VMEM(w.shape, BF16),
            pltpu.SemaphoreType.DMA((9,)),
        ],
        compiler_params=PARAMS,
        cost_estimate=cost(2 * 4 * rows * d * 3 * width, 12e6),
        name="qkv",
    )(*t, *f, w, gain, cosine, sine)


def attn_kernel(me, q, k, v, o0, o1, o2, o3, lse, o):
    h = pl.program_id(0)
    rows, width = q.shape[1:]
    mine = lax.broadcasted_iota(jnp.int32, (1, width), 1) // HEAD_DIM == h
    row = lax.broadcasted_iota(jnp.int32, (rows, rows), 0)
    col = lax.broadcasted_iota(jnp.int32, (rows, rows), 1)
    s = me[0]
    for i in range(GROUPS):
        ri = i ^ s
        qi = jnp.where(mine, q[ri], jnp.zeros((), BF16))
        tiles = []
        for j in range(i + 1):
            tile = nt(qi, k[j ^ s])
            if j == i:
                tile = jnp.where(col <= row, tile, NEGATIVE)
            tiles.append(tile)
        largest = tiles[0].max(axis=1, keepdims=True)
        for tile in tiles[1:]:
            largest = jnp.maximum(largest, tile.max(axis=1, keepdims=True))
        tiles = [jnp.exp(tile - largest) for tile in tiles]
        total = tiles[0].sum(axis=1, keepdims=True)
        for tile in tiles[1:]:
            total = total + tile.sum(axis=1, keepdims=True)
        inverse = 1.0 / total
        acc = jnp.zeros((rows, width), F32)
        for j in range(i + 1):
            acc = acc + nn((tiles[j] * inverse).astype(BF16), v[j ^ s])
        o[ri] = jnp.where(mine, acc.astype(BF16), o[ri])
        stat = jnp.broadcast_to(largest + jnp.log(total), (rows, 128))
        lse[0, i] = jnp.transpose(stat)[:8]

    @pl.when(h == pl.num_programs(0) - 1)
    def _():
        for r, out in enumerate((o0, o1, o2, o3)):
            out[...] = o[r]


def attention(me, q, k, v):
    _, rows, width = q.shape
    heads = width // HEAD_DIM
    full = lambda *shape: pl.BlockSpec(shape, lambda h, me: (0,) * len(shape))
    return pl.pallas_call(
        attn_kernel,
        grid_spec=pltpu.PrefetchScalarGridSpec(
            num_scalar_prefetch=1,
            grid=(heads,),
            in_specs=[full(4, rows, width)] * 3,
            out_specs=[full(rows, width)] * 4
            + [pl.BlockSpec((1, 4, 8, rows), lambda h, me: (h, 0, 0, 0))],
            scratch_shapes=[pltpu.VMEM((4, rows, width), BF16)],
        ),
        out_shape=[jax.ShapeDtypeStruct((rows, width), BF16)] * 4
        + [jax.ShapeDtypeStruct((heads, 4, 8, rows), F32)],
        compiler_params=PARAMS,
        cost_estimate=cost(2 * 2 * 10 * rows * rows * width * 4, 4e6, 10 * heads * rows * rows),
        name="attention",
    )(me, q, k, v)


def attn_back_kernel(me, q, k, v, b0, b1, b2, b3, lse, cosine, sine, out, *rest):
    vouts, (do, dq, dk, dv) = rest[:4], rest[4:]
    h = pl.program_id(0)
    rows, width = q.shape[1:]
    mine = lax.broadcasted_iota(jnp.int32, (1, width), 1) // HEAD_DIM == h
    key = lax.broadcasted_iota(jnp.int32, (rows, rows), 0)
    query = lax.broadcasted_iota(jnp.int32, (rows, rows), 1)
    s = me[0]
    zero = jnp.zeros((), BF16)

    @pl.when(h == 0)
    def _():
        for r, b in enumerate((b0, b1, b2, b3)):
            do[r] = b[...]
        dq[...] = jnp.zeros_like(dq)
        dk[...] = jnp.zeros_like(dk)
        dv[...] = jnp.zeros_like(dv)

    for i in range(GROUPS):
        qi = jnp.where(mine, q[i ^ s], zero)
        doi = jnp.where(mine, do[i ^ s], zero)
        stat = lse[0, i][:1]
        soft, back = [], []
        dot = jnp.zeros((1, rows), F32)
        for j in range(i + 1):
            tile = nt(k[j ^ s], qi)
            if j == i:
                tile = jnp.where(key <= query, tile, NEGATIVE)
            p = jnp.exp(tile - stat)
            dp = nt(v[j ^ s], doi)
            dot = dot + jnp.sum(p * dp, axis=0, keepdims=True)
            soft.append(p)
            back.append(dp)
        acc = jnp.zeros((rows, width), F32)
        for j in range(i + 1):
            ds = (soft[j] * (back[j] - dot)).astype(BF16)
            dk[j] += nn(ds, qi)
            dv[j] += nn(soft[j].astype(BF16), doi)
            acc = acc + tn(ds, jnp.where(mine, k[j ^ s], zero))
        dq[i] += acc

    @pl.when(h == pl.num_programs(0) - 1)
    def _():
        for i in range(GROUPS):
            ri = i ^ s
            c, n = cosine[ri], -sine[ri]
            out[ri, :, :width] = turn(dq[i] * 0.125, c, n).astype(BF16)
            out[ri, :, width : 2 * width] = turn(dk[i], c, n).astype(BF16)
            out[ri, :, 2 * width :] = (0.5 * dv[i]).astype(BF16)
        for r, vout in enumerate(vouts):
            vout[...] = out[r, :, 2 * width :]


def attention_back(part, me, q, k, v, b, lse, cosine, sine):
    rows = q.shape[1]
    width = 2 * HEAD_DIM
    full = lambda *shape: pl.BlockSpec(shape, lambda h, me: (0,) * len(shape))
    pair = pl.BlockSpec((4, rows, width), lambda h, me: (0, 0, part))
    return pl.pallas_call(
        attn_back_kernel,
        grid_spec=pltpu.PrefetchScalarGridSpec(
            num_scalar_prefetch=1,
            grid=(2,),
            in_specs=[pair] * 3
            + [pl.BlockSpec((rows, width), lambda h, me: (0, part))] * 4
            + [pl.BlockSpec((1, 4, 8, rows), lambda h, me: (2 * part + h, 0, 0, 0))]
            + [full(4, rows, 128)] * 2,
            out_specs=[full(4, rows, 3 * width)] + [full(rows, width)] * 4,
            scratch_shapes=[pltpu.VMEM((4, rows, width), BF16)]
            + [pltpu.VMEM((4, rows, width), F32)] * 3,
        ),
        out_shape=[jax.ShapeDtypeStruct((4, rows, 3 * width), BF16)]
        + [jax.ShapeDtypeStruct((rows, width), BF16)] * 4,
        compiler_params=PARAMS,
        cost_estimate=cost(5 * 2 * 10 * rows * rows * width * 4, 4e6, 20 * rows * rows),
        name="attention_back",
    )(me, q, k, v, *b, lse, cosine, sine)


def out_kernel(me, m0, m1, m2, m3, w0, w1, t, gain, middle, second):
    s = me[0]
    width = m0.shape[1]
    for j, w in enumerate((w0, w1)):
        half = w.shape[1]
        cols = pl.ds(pl.multiple_of(((s % 2) ^ j) * half, half), half)
        part = None
        for r, m in enumerate((m0, m1, m2, m3)):
            one = nn(m[...], w[pl.ds(pl.multiple_of((s ^ r) * width, width), width), :])
            part = one if part is None else part + one
        middle[:, cols] = t[:, cols].astype(F32) + part
    acc = middle[...]
    second[...] = (acc * inverse_rms(acc) * gain[...]).astype(BF16)


def vmem_call(kernel, name, shapes, me, args, estimate, scratch=()):
    full = lambda shape: pl.BlockSpec(shape, lambda i, me: (0,) * len(shape))
    outs = [jax.ShapeDtypeStruct(s, t) for s, t in shapes]
    return pl.pallas_call(
        kernel,
        grid_spec=pltpu.PrefetchScalarGridSpec(
            num_scalar_prefetch=1,
            grid=(1,),
            in_specs=[full(a.shape) for a in args],
            out_specs=[full(s) for s, _ in shapes],
            scratch_shapes=scratch,
        ),
        out_shape=outs,
        compiler_params=PARAMS,
        cost_estimate=estimate,
        name=name,
    )(me, *args)


def mlp_kernel(me, sa, sb, ga, gb, w, *refs):
    outs, (sv, gv, wv, hid, gback, uback, sback, sems) = refs[:5], refs[5:]
    units = wv.shape[1]
    rows = sa.shape[0]
    copies = [pltpu.make_async_copy(sa, sv.at[0], sems.at[0])]
    for i in range(3):
        copies.append(pltpu.make_async_copy(w.at[i * units : (i + 1) * units], wv.at[i], sems.at[1 + i]))
    copies.append(pltpu.make_async_copy(ga, gv.at[0], sems.at[4]))
    copies.append(pltpu.make_async_copy(sb, sv.at[1], sems.at[5]))
    copies.append(pltpu.make_async_copy(gb, gv.at[1], sems.at[6]))
    for copy in copies:
        copy.start()
    writes = []

    def write(buf, out):
        copy = pltpu.make_async_copy(buf, out, sems.at[7 + len(writes)])
        copy.start()
        writes.append(copy)

    for i in range(2):
        copies[5 if i else 0].wait()
        if i == 0:
            copies[1].wait()
        gate = nt(sv[i], wv[0])
        if i == 0:
            copies[2].wait()
        up = nt(sv[i], wv[1])
        sg = jax.nn.sigmoid(gate)
        act = gate * sg
        hid[i] = (act * up).astype(BF16)
        at = slice(i * rows, (i + 1) * rows)
        write(hid.at[i], outs[0].at[at])
        copies[6 if i else 4].wait()
        if i == 0:
            copies[3].wait()
        hb = nt(gv[i], wv[2])
        gate_back = (hb * up * sg * (1.0 + gate * (1.0 - sg))).astype(BF16)
        up_back = (hb * act).astype(BF16)
        gback[i] = gate_back
        write(gback.at[i], outs[1].at[at])
        uback[i] = up_back
        write(uback.at[i], outs[2].at[at])
        sback[i] = (nn(gate_back, wv[0]) + nn(up_back, wv[1])).astype(BF16)
        write(sback.at[i], outs[3 + i])
    for copy in writes:
        copy.wait()


def any_call(kernel, name, shapes, me, args, estimate, scratch):
    return pl.pallas_call(
        kernel,
        grid_spec=pltpu.PrefetchScalarGridSpec(
            num_scalar_prefetch=1,
            grid=(1,),
            in_specs=[ANY] * len(args),
            out_specs=[ANY] * len(shapes),
            scratch_shapes=scratch,
        ),
        out_shape=[jax.ShapeDtypeStruct(s, t) for s, t in shapes],
        compiler_params=PARAMS,
        cost_estimate=estimate,
        name=name,
    )(me, *args)


def mlp(me, sa, sb, ga, gb, w):
    rows, d = sa.shape
    units = w.shape[0] // 3
    part = ((2 * rows, units), BF16)
    return any_call(
        mlp_kernel,
        "mlp",
        [part] * 3 + [((rows, d), BF16)] * 2,
        me,
        [sa, sb, ga, gb, w],
        cost(2 * 5 * 2 * rows * d * units, 12e6, 2 * rows * units),
        [pltpu.VMEM((2, rows, d), BF16)] * 2
        + [pltpu.VMEM((3, units, d), BF16)]
        + [pltpu.VMEM((2, rows, units), BF16)] * 3
        + [pltpu.VMEM((2, rows, d), BF16), pltpu.SemaphoreType.DMA((15,))],
    )


def mlp_out_kernel(me, hn, hf, whole, o0, o1, o2, o3):
    rows = o0.shape[0]
    units = whole.shape[0] // 3
    w = whole.at[2 * units :]
    for h, outs in ((hn, (o0, o1)), (hf, (o2, o3))):
        for i, out in enumerate(outs):
            out[...] = nn(h[i * rows : (i + 1) * rows], w[...]).astype(BF16)


def unit_grad_kernel(count, me, *refs):
    ins, outs, acc = refs[: 2 * count + 4], refs[2 * count + 4 : -1], refs[-1]
    blocks = ins[2 * count :]
    y = me[0] % 2
    near = jnp.concatenate([blocks[0][...], blocks[1][...]], axis=0)
    far = jnp.concatenate([blocks[2][...], blocks[3][...]], axis=0)
    share = outs[0].shape[2]
    for i in range(count):
        acc[...] = tn(ins[2 * i][...], near) + tn(ins[2 * i + 1][...], far)
        for z in range(outs[0].shape[0]):
            for j in range(2):
                at = pl.multiple_of((2 * z + (y ^ j)) * share, share)
                outs[2 * i + j][z] = acc[:, pl.ds(at, share)].astype(BF16)


def unit_grads(pairs, blocks):
    n = lax.axis_size("fsdp")
    units, d = pairs[0][0].shape[1], blocks[0].shape[1]
    if n != 8:
        near, far = jnp.concatenate(blocks[:2]), jnp.concatenate(blocks[2:])
        outs = [(tn(a, near) + tn(b, far)).astype(BF16) for a, b in pairs]
        return [jnp.transpose(o.reshape(units, n, d // n), (1, 0, 2)) for o in outs]
    me = lax.axis_index("fsdp").astype(jnp.int32).reshape(1)
    outs = vmem_call(
        functools.partial(unit_grad_kernel, len(pairs)),
        "unit_grads",
        [((n // 2, units, d // n), BF16)] * (2 * len(pairs)),
        me,
        [a for pair in pairs for a in pair] + list(blocks),
        cost(2 * 4 * blocks[0].shape[0] * units * d * len(pairs), 6e6),
        [pltpu.VMEM((units, d), F32)],
    )
    return [(outs[2 * i], outs[2 * i + 1]) for i in range(len(pairs))]


def out_grad_kernel(me, m0, m1, m2, m3, low, gain, keep, send, acc):
    s, y = me[0], me[1] % 2
    width = m0.shape[1]
    d = acc.shape[0]
    for r, m in enumerate((m0, m1, m2, m3)):
        acc[pl.ds(pl.multiple_of((s ^ r) * width, width), width), :] = tn(m[...], low[...])
    share = keep.shape[2] - 8
    for k, out in enumerate((keep, send)):
        at = pl.multiple_of(((s % 2) ^ k) * (d // 2), d // 2)
        for j in range(2):
            for z in range(keep.shape[1]):
                block = pl.multiple_of((2 * z + (y ^ j)) * share, share)
                out[j, z, :share] = acc[pl.ds(block, share), pl.ds(at, d // 2)].astype(BF16)
                out[j, z, share:] = jnp.zeros((8, d // 2), BF16)
                if k == 0:
                    out[j, z, share:, :share] = gain[:, pl.ds(block, share)].astype(BF16)


def qkv_grad_kernel(me, normed, dd, w, gain, mine, other, acc):
    y = me[1] % 2
    share = mine.shape[1] - 8
    acc[...] = tn(normed[...], dd[...])
    pair = dd.shape[1] // 3
    part = me[2]
    width = w.shape[1] // 3
    total = jnp.zeros((acc.shape[0], pair), F32)
    for i in range(3):
        cols = pl.ds(pl.multiple_of(i * width + part * pair, pair), pair)
        total = total + acc[:, i * pair : (i + 1) * pair] * w[:, cols].astype(F32)
    sums = jnp.broadcast_to(jnp.sum(total, axis=1, keepdims=True) / gain[...], (acc.shape[0], 128))
    for j, out in enumerate((mine, other)):
        for z in range(mine.shape[0]):
            block = pl.multiple_of((2 * z + (y ^ j)) * share, share)
            out[z, :share] = acc[pl.ds(block, share), :].astype(BF16)
            out[z, share:] = jnp.zeros((8, dd.shape[1]), BF16)
    for f in range(acc.shape[0] // share):
        row = jnp.transpose(sums[f * share : (f + 1) * share])[:8].astype(BF16)
        for j, out in enumerate((mine, other)):

            @pl.when((f % 2) == (y ^ j))
            def _():
                out[f // 2, share:, :share] = row


def normed_back_kernel(half, me, da, db, w, n0, n1):
    pair = da.shape[2] // 3
    for i, out in enumerate((n0, n1)):
        r = 2 * half + i
        parts = [d[r, :, j * pair : (j + 1) * pair] for j in range(3) for d in (da, db)]
        out[...] = nt(jnp.concatenate(parts, axis=1), w[...]).astype(BF16)


def place_kernel(count, me, *refs):
    pieces, outs = refs[: 4 * count], refs[4 * count :]
    s = me[0]
    out = outs[0]
    for p in range(count):
        for r in range(4):
            piece = pieces[4 * p + r]
            size = piece.shape[1]
            at = pl.multiple_of((s ^ r) * count * size + p * size, size)
            out[:, pl.ds(at, size)] = piece[...].astype(F32)


def place_qkv_kernel(me, *refs):
    pieces, outs, gain = refs[:8], refs[8:11], refs[11]
    s = me[0]
    share = outs[0].shape[0]
    total = jnp.zeros((8, gain.shape[1]), F32)
    for p in range(2):
        for r in range(4):
            piece = pieces[4 * p + r]
            size = piece.shape[1] // 3
            at = pl.multiple_of((s ^ r) * 2 * size + p * size, size)
            for i, out in enumerate(outs):
                out[:, pl.ds(at, size)] = piece[:share, i * size : (i + 1) * size].astype(F32)
            total = total + piece[share:, : gain.shape[1]].astype(F32)
    gain[...] = total


def place_units_kernel(me, p0, p1, p2, p3, out, buf):
    s = me[0]
    for r, p in enumerate((p0, p1, p2, p3)):
        buf[s ^ r] = p[...].astype(F32)
    units = p0.shape[0]
    for j in range(4):
        out[:, j * units : (j + 1) * units] = jnp.transpose(buf[j])


def middle_kernel(me, p0, p1, p2, middle, g, gain, w0, w1, mback, mlow, b0, b1, b2, b3, ggrad):
    s = me[0]
    width = b0.shape[1]
    dn = p0[...].astype(F32) + p1[...].astype(F32) + p2[...].astype(F32)
    v = middle[...]
    r = inverse_rms(v)
    x = v * r
    ggrad[...] = jnp.broadcast_to(jnp.sum(dn * x, axis=0, keepdims=True), ggrad.shape)
    dx = dn * gain[...]
    total = g[...].astype(F32) + r * (dx - x * jnp.mean(dx * x, axis=-1, keepdims=True))
    mback[...] = total
    mlow[...] = total.astype(BF16)
    half = w0.shape[1]
    lows = [mlow[:, pl.ds(pl.multiple_of(((s % 2) ^ j) * half, half), half)] for j in range(2)]
    for i, b in enumerate((b0, b1, b2, b3)):
        rows = pl.ds(pl.multiple_of((s ^ i) * width, width), width)
        b[...] = (nt(lows[0], w0[rows, :]) + nt(lows[1], w1[rows, :])).astype(BF16)


def final_kernel(me, p0, p1, p2, t, gain, mback, out):
    dn = p0[...].astype(F32) + p1[...].astype(F32) + p2[...].astype(F32)
    v = t[...].astype(F32)
    r = inverse_rms(v)
    x = v * r
    dx = dn * gain[...]
    out[...] = mback[...] + r * (dx - x * jnp.mean(dx * x, axis=-1, keepdims=True))


def after(value, *others):
    return lax.optimization_barrier((value,) + others)[0]


def seq_permute(value, flip):
    return lax.ppermute(value, "seq", [(i, i ^ flip) for i in range(GROUPS)])


def gather_four(own):
    near = seq_permute(own, 1)
    far = seq_permute(own, 2)
    return own, near, far, seq_permute(far, 1)


def exchange_four(pieces):
    return [pieces[0]] + [seq_permute(pieces[r], r) for r in (1, 2, 3)]


def sum_pairs(mine, other):
    return (mine.astype(F32) + seq_permute(other, 1).astype(F32)).astype(BF16)


def fsdp_permute(value, flip):
    n = lax.axis_size("fsdp")
    return lax.ppermute(value, "fsdp", [(i, i ^ flip) for i in range(n)])


def gather_rows(own, share, forward=None, last=()):
    n = lax.axis_size("fsdp")
    if n != 8:
        out = lax.all_gather(own, "fsdp", axis=0)
        whole = out[:, :share].reshape(n * share, -1)
        return (whole, out[:, share:]) if own.shape[0] > share else whole
    pieces = [own, fsdp_permute(own, 1)]
    for k in (2, 4, 6):
        one = fsdp_permute(own, k)
        if forward is not None:
            one = forward(one, k)
        pieces += [one, fsdp_permute(one, 1)]
    pieces[0] = after(pieces[0], *last)
    return assemble(pieces, share)


def fsdp_pairs(mine, other):
    return (mine.astype(F32) + fsdp_permute(other, 1).astype(F32)).astype(BF16)


def fsdp_rest(both):
    z = lax.axis_index("fsdp") // 2
    total = lax.dynamic_index_in_dim(both, z, 0, keepdims=False).astype(F32)
    for k in range(1, both.shape[0]):
        piece = lax.dynamic_index_in_dim(both, z ^ k, 0, keepdims=False)
        total = total + fsdp_permute(piece, 2 * k).astype(F32)
    return total.astype(BF16)


def scatter_whole(parts):
    return lax.psum_scatter(parts, "fsdp", scatter_dimension=0, tiled=False)


def per_device(
    tokens,
    first_values,
    cotangent,
    first_gain,
    query_weight,
    key_weight,
    value_weight,
    out_weight,
    second_gain,
    gate_weight,
    up_weight,
    down_weight,
):
    n = lax.axis_size("fsdp")
    s = lax.axis_index("seq").astype(jnp.int32)
    me = s.reshape(1)
    place3 = [jnp.stack([s, lax.axis_index("fsdp").astype(jnp.int32), jnp.int32(p)]) for p in (0, 1)]
    t0, g0, f0 = tokens[0], cotangent[0], first_values[0]
    rows, d = t0.shape
    width = d // GROUPS
    pair = width // 2
    units = gate_weight.shape[1] // GROUPS
    share = d // n
    core = s % 2
    ring = n == 8

    def columns(v, which, size):
        return lax.dynamic_slice_in_dim(v, which * size, size, 1)

    small = jnp.zeros((8, 3 * width), BF16)
    small = small.at[0, :share].set(first_gain).at[1, :share].set(second_gain)
    packed = jnp.concatenate(
        [columns(w, s, width) for w in (query_weight, key_weight, value_weight)], axis=1
    )
    own_qkv = jnp.concatenate([packed, small], axis=0)
    t0, t1, t2, t3 = gather_four(t0)
    f = [columns(f0, s ^ r, width) for r in range(4)]
    f = exchange_four(f[:2] + [after(v, t2) if True else v for v in f[2:]])
    w_qkv, gains = gather_rows(
        own_qkv, share, lambda one, k: after(one, t2) if k == 6 else one, (f[2], f[3])
    )
    gain_first = gains[:, 0, :share].reshape(1, d).astype(F32)
    gain_second = gains[:, 1, :share].reshape(1, d).astype(F32)
    w_mlp = jnp.concatenate(
        [columns(w, s, units).T for w in (gate_weight, up_weight, down_weight)], axis=0
    )
    w_mlp = lax.all_gather(w_mlp, "fsdp", axis=1, tiled=True)
    g0, g1, g2 = g0, seq_permute(g0, 1), seq_permute(after(g0, t2), 2)

    places = (jnp.arange(4, dtype=jnp.int32) ^ s)[:, None] * rows + jnp.arange(rows, dtype=jnp.int32)
    half_dim = HEAD_DIM // 2
    freqs = jnp.exp(jnp.arange(half_dim, dtype=F32) * (-2.0 * math.log(10000.0) / HEAD_DIM))
    angles = places.astype(F32)[:, :, None] * jnp.tile(freqs, 4)
    sign = jnp.tile(jnp.repeat(jnp.array([-1.0, 1.0], F32), half_dim), 2)
    cosine, sine = jnp.cos(angles), jnp.sin(angles) * sign

    own_out = after(columns(out_weight, core, d // 2), w_qkv)
    q, k, v, normed = qkv((t0, t1, t2, t3), f, w_qkv, gain_first, cosine, sine)
    g2 = after(g2, q)
    g3 = seq_permute(g2, 1)
    waits = []

    def forward(one, k):
        waits.append(one)
        return after(one, q)

    mixed = []

    def attend(*waits):
        *mixed[:], lse = attention(me, after(q, g2, *waits), k, v)
        return lse

    if ring:
        own_y = fsdp_permute(own_out, 1)
        pieces = [own_out, own_y]
        for flip in (2, 4, 6):
            one = after(fsdp_permute(own_out, flip), q)
            waits.append(one)
            pieces += [one, fsdp_permute(one, 1)]
        lse = attend(*waits)
        pieces[0] = after(pieces[0], *mixed)
        w_out_half = assemble(pieces, share)
    else:
        lse = attend()
        w_out_half = gather_rows(own_out, share)
    m = exchange_four(mixed)
    w_out_other = seq_permute(w_out_half, 1)
    middle, second = vmem_call(
        out_kernel,
        "out",
        [((rows, d), F32), ((rows, d), BF16)],
        me,
        [*m, w_out_half, w_out_other, t0, gain_second],
        cost(2 * rows * d * d, 8e6),
    )
    s0, s1, s2 = second, seq_permute(second, 1), seq_permute(second, 2)
    hid_near, gate_near, up_near, sb0, sb1 = mlp(me, s0, s1, g0, g1, w_mlp)
    s2 = after(s2, sb0)
    s3 = seq_permute(s2, 1)
    hid_far, gate_far, up_far, sb2, sb3 = mlp(me, s2, s3, g2, g3, w_mlp)
    sb_both = sum_pairs(sb2, sb3)
    p = [sb0, seq_permute(sb1, 1), seq_permute(sb_both, 2)]

    (down_part,) = unit_grads([(hid_near, after(hid_far, sb_both))], (g0, g1, g2, g3))
    gate_part, up_part = unit_grads(
        [(gate_near, after(gate_far, down_part[0])), (up_near, up_far)], (s0, s1, s2, s3)
    )
    o = vmem_call(
        mlp_out_kernel,
        "mlp_out",
        [((rows, d), BF16)] * 4,
        me,
        [hid_near, after(hid_far, up_part[0]), w_mlp],
        cost(2 * 4 * rows * d * units, 8e6),
    )
    waits = [up_part[0], o[0]]
    if ring:
        down_both = fsdp_pairs(down_part[0], after(down_part[1], up_part[0]))
        waits.append(down_both)
    p[2] = after(p[2], *waits)
    mback, mlow, b0, b1, b2, b3, ggrad_second = vmem_call(
        middle_kernel,
        "middle",
        [((rows, d), F32), ((rows, d), BF16)] + [((rows, width), BF16)] * 4 + [((8, d), F32)],
        me,
        [*p, middle, g0, gain_second, w_out_half, w_out_other],
        cost(2 * rows * d * d, 12e6),
    )
    b = exchange_four([b0, b1, b2, b3])
    o_both = after(sum_pairs(o[2], o[3]), b[2])
    o = [o[0], seq_permute(o[1], 1), seq_permute(o_both, 2)]
    if ring:
        gate_both = fsdp_pairs(gate_part[0], after(gate_part[1], down_both))
        down_share = fsdp_rest(down_both)
        keep, send = vmem_call(
            out_grad_kernel,
            "out_grad",
            [((2, n // 2, share + 8, d // 2), BF16)] * 2,
            place3[0],
            [*m, mlow, ggrad_second],
            cost(2 * rows * d * d, 6e6),
            [pltpu.VMEM((d, d), F32)],
        )
        out_cores = (keep.astype(F32) + seq_permute(send, 1).astype(F32)).astype(BF16)
        q = after(q, gate_both, down_share, out_cores, o_both)
    else:
        down_share, gate_share, up_share = (scatter_whole(v) for v in (down_part, gate_part, up_part))


    d_a, *v_a = attention_back(0, me, q, k, v, b, lse, cosine, sine)
    flat = lambda x: x.reshape(4 * rows, -1)

    def qkv_part(part, dd):
        if ring:
            return vmem_call(
                qkv_grad_kernel,
                "qkv_grad",
                [((n // 2, share + 8, 3 * pair), BF16)] * 2,
                place3[part],
                [flat(normed), flat(dd), w_qkv, gain_first.reshape(d, 1)],
                cost(2 * 4 * rows * d * 3 * pair, 6e6),
                [pltpu.VMEM((d, 3 * pair), F32)],
            )
        whole = tn(flat(normed), flat(dd))
        cols = [w_qkv[:, i * width + part * pair : i * width + (part + 1) * pair] for i in range(3)]
        gain_part = jnp.sum(whole * jnp.concatenate(cols, axis=1).astype(F32), axis=1) / gain_first[0]
        gain_part = jnp.pad(gain_part.reshape(n, 1, share), ((0, 0), (0, 7), (0, 3 * pair - share)))
        return jnp.concatenate([whole.reshape(n, share, 3 * pair), gain_part], axis=1).astype(BF16)

    qkv_a = qkv_part(0, d_a)
    if ring:
        up_both = fsdp_pairs(up_part[0], after(up_part[1], gate_both))
        gate_share = fsdp_rest(gate_both)
        qkv_a_both = fsdp_pairs(*qkv_a)
        out_both = fsdp_pairs(out_cores[0], after(out_cores[1], up_both))
        q = after(q, up_both, gate_share)
    d_b, *v_b = attention_back(1, me, after(q, d_a), k, v, b, lse, cosine, sine)

    def normed_back(half, d_b):
        return vmem_call(
            functools.partial(normed_back_kernel, half),
            "normed_back",
            [((rows, d), BF16)] * 2,
            me,
            [d_a, d_b, w_qkv],
            cost(2 * 2 * rows * d * 3 * width, 8e6),
        )

    nb2, nb3 = normed_back(1, d_b)
    nb_both = sum_pairs(nb2, nb3)
    qkv_b = qkv_part(1, after(d_b, nb_both))
    nb0, nb1 = normed_back(0, after(d_b, qkv_b))
    p = [nb0, seq_permute(nb1, 1), seq_permute(nb_both, 2)]
    (tokens_grad,) = vmem_call(
        final_kernel,
        "final",
        [((rows, d), F32)],
        me,
        [*p, t0, gain_first, mback],
        cost(0, 6e6),
    )
    output = (middle + o[0].astype(F32) + o[1].astype(F32) + o[2].astype(F32)).astype(BF16)[None]
    v_all = exchange_four(v_a) + exchange_four(v_b)
    (values_grad,) = vmem_call(
        functools.partial(place_kernel, 2), "place_values", [((rows, d), F32)], me, v_all, cost(0, 3e6)
    )
    if ring:
        qkv_share = [fsdp_rest(qkv_a_both), fsdp_rest(fsdp_pairs(*qkv_b))]
        up_share = fsdp_rest(up_both)
        out_share = fsdp_rest(out_both)
    else:
        qkv_share = [scatter_whole(v) for v in (qkv_a, qkv_b)]
        mixed_rows = jnp.zeros((rows, d), BF16)
        for r in range(4):
            mixed_rows = lax.dynamic_update_slice(mixed_rows, m[r], (0, (s ^ r) * width))
        out_part = tn(mixed_rows, mlow)
        halves = [columns(out_part, core ^ j, d // 2).reshape(n, share, d // 2) for j in range(2)]
        gain_part = ggrad_second[0].reshape(n, 1, share)
        gain_part = jnp.pad(gain_part, ((0, 0), (0, 7), (0, d // 2 - share)))
        keep = jnp.concatenate([halves[0], gain_part], axis=1)
        send = jnp.pad(halves[1], ((0, 0), (0, 8), (0, 0))).astype(BF16)
        out_share = scatter_whole((keep + seq_permute(send, 1).astype(F32)).astype(BF16))
    out_share = (out_share.astype(F32) + seq_permute(out_share, 2).astype(F32)).astype(BF16)
    out_other = seq_permute(out_share, 1)
    second_gain_grad = out_share[share, :share].astype(F32) + out_other[share, :share].astype(F32)
    out_grad = jnp.where(
        core == 0,
        jnp.concatenate([out_share[:share], out_other[:share]], axis=1),
        jnp.concatenate([out_other[:share], out_share[:share]], axis=1),
    ).astype(F32)

    def place_units(own):
        return vmem_call(
            place_units_kernel,
            "place_units",
            [((share, 4 * units), F32)],
            me,
            gather_four(own),
            cost(0, 3e6),
            [pltpu.VMEM((4, units, share), F32)],
        )[0]

    gate_grad, up_grad, down_grad = (place_units(v) for v in (gate_share, up_share, down_share))
    pieces = [one for v in qkv_share for one in gather_four(v)]
    query_grad, key_grad, value_grad, gain_grad = vmem_call(
        place_qkv_kernel,
        "place_qkv",
        [((share, d), F32)] * 3 + [((8, share), F32)],
        me,
        pieces,
        cost(0, 3e6),
    )
    return (
        output,
        tokens_grad[None],
        values_grad[None],
        gain_grad[0],
        query_grad,
        key_grad,
        value_grad,
        out_grad,
        second_gain_grad,
        gate_grad,
        up_grad,
        down_grad,
    )


def solution(mesh):
    rows = P("fsdp", "seq", None)
    weight = P("fsdp", None)
    gain = P("fsdp")
    in_specs = (rows,) * 3 + (gain,) + (weight,) * 4 + (gain,) + (weight,) * 3
    out_specs = (rows,) * 3 + (gain,) + (weight,) * 4 + (gain,) + (weight,) * 3
    return jax.shard_map(
        per_device, mesh=mesh, in_specs=in_specs, out_specs=out_specs, check_vma=False
    )
```

```python
import functools
import math

import jax
import jax.numpy as jnp
from jax import lax
from jax.experimental import pallas as pl
from jax.experimental.pallas import tpu as pltpu
from jax.sharding import PartitionSpec as P

HEADS = 16
HEAD_DIM = 64
GROUPS = 4
EPSILON = 1e-06
NEGATIVE = -1e30
F32 = jnp.float32
BF16 = jnp.bfloat16
PARAMS = pltpu.CompilerParams(vmem_limit_bytes=56 * 2**20)


def nn(a, b):
    return lax.dot_general(a, b, (((1,), (0,)), ((), ())), preferred_element_type=F32)


def nt(a, b):
    return lax.dot_general(a, b, (((1,), (1,)), ((), ())), preferred_element_type=F32)


def tn(a, b):
    return lax.dot_general(a, b, (((0,), (0,)), ((), ())), preferred_element_type=F32)


def cost(flops, nbytes, trans=0):
    flops, nbytes, trans = 1, 1, 0
    return pl.CostEstimate(flops=int(flops), bytes_accessed=int(nbytes), transcendentals=int(trans))


def turn(u, cosine, sine):
    lane = lax.broadcasted_iota(jnp.int32, (u.shape[0], 128), 1)
    first = lane % HEAD_DIM < HEAD_DIM // 2
    parts = []
    for j in range(u.shape[1] // 128):
        part = u[:, 128 * j : 128 * (j + 1)]
        other = jnp.where(first, pltpu.roll(part, 96, 1), pltpu.roll(part, 32, 1))
        parts.append(part * cosine + other * sine)
    return jnp.concatenate(parts, axis=1)


def inverse_rms(v):
    return lax.rsqrt(jnp.mean(v * v, axis=-1, keepdims=True) + EPSILON)


ANY = pl.BlockSpec(memory_space=pl.ANY)


def qkv_kernel(count, me, t0, f0, p1, p2, p3, *refs):
    pieces, rest = refs[:count], refs[count:]
    cosine, sine, q, k, v, n, w, tv, fv, sems = rest
    width = q.shape[-1]
    d = tv.shape[-1]
    share = d // count
    first = []
    for i, piece in enumerate(pieces):
        at = pl.ds(pl.multiple_of((me[0] ^ i) * share, share), share)
        first.append(pltpu.make_async_copy(piece, w.at[:, at], sems.at[8 + i]))
    loads = [(t0, f0)] + [(p.at[:, :d], p.at[:, d : d + width]) for p in (p1, p2, p3)]
    copies = []
    for i, (t, f) in enumerate(loads):
        copies.append(pltpu.make_async_copy(t, tv.at[i], sems.at[2 * i]))
        copies.append(pltpu.make_async_copy(f, fv.at[i], sems.at[2 * i + 1]))
    for copy in copies[:2] + first + copies[2:]:
        copy.start()
    for i in range(4):
        copies[2 * i].wait()
        if i == 0:
            for copy in first:
                copy.wait()
        gain = w[3 * width : 3 * width + 1].astype(F32)
        x = tv[i].astype(F32)
        normed = (x * inverse_rms(x) * gain).astype(BF16)
        n[i] = normed
        u = nt(normed, w[: 3 * width])
        c, s = cosine[i], sine[i]
        q[i] = (turn(u[:, :width], c, s).astype(BF16).astype(F32) * 0.125).astype(BF16)
        k[i] = turn(u[:, width : 2 * width], c, s).astype(BF16)
        copies[2 * i + 1].wait()
        v[i] = (0.5 * u[:, 2 * width :] + 0.5 * fv[i].astype(F32)).astype(BF16)


def qkv(where, t, f, packed, pieces, cosine, sine):
    rows, d = t.shape
    width = f.shape[1]
    full = lambda *shape: pl.BlockSpec(shape, lambda i, me: (0,) * len(shape))
    shapes = [(4, rows, width)] * 3 + [(4, rows, d), (pieces[0].shape[0], d)]
    return pl.pallas_call(
        functools.partial(qkv_kernel, len(pieces)),
        grid_spec=pltpu.PrefetchScalarGridSpec(
            num_scalar_prefetch=1,
            grid=(1,),
            in_specs=[ANY] * (5 + len(pieces)) + [full(4, rows, 128)] * 2,
            out_specs=[full(*s) for s in shapes],
            scratch_shapes=[
                pltpu.VMEM((4, rows, d), BF16),
                pltpu.VMEM((4, rows, width), BF16),
                pltpu.SemaphoreType.DMA((8 + len(pieces),)),
            ],
        ),
        out_shape=[jax.ShapeDtypeStruct(s, BF16) for s in shapes],
        compiler_params=PARAMS,
        cost_estimate=cost(2 * 4 * rows * d * 3 * width, 12e6),
        name="qkv",
    )(where.reshape(1), t, f, *packed, *pieces, cosine, sine)


def attn_kernel(me, q, k, v, *refs):
    before, (o0, o1, o2, o3, lse, o) = refs[:-6], refs[-6:]
    h = pl.program_id(0)
    rows, width = q.shape[1:]
    mine = lax.broadcasted_iota(jnp.int32, (1, width), 1) // HEAD_DIM == h
    row = lax.broadcasted_iota(jnp.int32, (rows, rows), 0)
    col = lax.broadcasted_iota(jnp.int32, (rows, rows), 1)
    s = me[0]
    for i in range(GROUPS):
        ri = i ^ s
        qi = jnp.where(mine, q[ri], jnp.zeros((), BF16))
        tiles = []
        for j in range(i + 1):
            tile = nt(qi, k[j ^ s])
            if j == i:
                tile = jnp.where(col <= row, tile, NEGATIVE)
            tiles.append(tile)
        largest = tiles[0].max(axis=1, keepdims=True)
        for tile in tiles[1:]:
            largest = jnp.maximum(largest, tile.max(axis=1, keepdims=True))
        tiles = [jnp.exp(tile - largest) for tile in tiles]
        total = tiles[0].sum(axis=1, keepdims=True)
        for tile in tiles[1:]:
            total = total + tile.sum(axis=1, keepdims=True)
        inverse = 1.0 / total
        acc = jnp.zeros((rows, width), F32)
        for j in range(i + 1):
            acc = acc + nn((tiles[j] * inverse).astype(BF16), v[j ^ s])
        o[ri] = jnp.where(mine, acc.astype(BF16), o[ri])
        stat = jnp.broadcast_to(largest + jnp.log(total), (rows, 128))
        lse[0, i] = jnp.transpose(stat)[:8]

    @pl.when(h == pl.num_programs(0) - 1)
    def _():
        for r, out in enumerate((o0, o1, o2, o3)):
            if before:
                out[:, :width] = before[r][...]
                out[:, width:] = o[r]
            else:
                out[...] = o[r]


def attention(part, me, q, k, v, *before):
    rows = q.shape[1]
    width = 2 * HEAD_DIM
    full = lambda *shape: pl.BlockSpec(shape, lambda h, me: (0,) * len(shape))
    pair = pl.BlockSpec((4, rows, width), lambda h, me: (0, 0, part))
    both = (rows, 2 * width if before else width)
    return pl.pallas_call(
        attn_kernel,
        grid_spec=pltpu.PrefetchScalarGridSpec(
            num_scalar_prefetch=1,
            grid=(2,),
            in_specs=[pair] * 3 + [full(*one.shape) for one in before],
            out_specs=[full(*both)] * 4
            + [pl.BlockSpec((1, 4, 8, rows), lambda h, me: (h, 0, 0, 0))],
            scratch_shapes=[pltpu.VMEM((4, rows, width), BF16)],
        ),
        out_shape=[jax.ShapeDtypeStruct(both, BF16)] * 4
        + [jax.ShapeDtypeStruct((2, 4, 8, rows), F32)],
        compiler_params=PARAMS,
        cost_estimate=cost(2 * 2 * 10 * rows * rows * width * 4, 4e6, 20 * rows * rows),
        name="attention",
    )(me, q, k, v, *before)


def attn_back_kernel(me, q, k, v, b0, b1, b2, b3, lse, cosine, sine, *rest):
    before, (out, vout, do, dq, dk, dv) = rest[:-6], rest[-6:]
    h = pl.program_id(0)
    rows, width = q.shape[1:]
    mine = lax.broadcasted_iota(jnp.int32, (1, width), 1) // HEAD_DIM == h
    key = lax.broadcasted_iota(jnp.int32, (rows, rows), 0)
    query = lax.broadcasted_iota(jnp.int32, (rows, rows), 1)
    s = me[0]
    zero = jnp.zeros((), BF16)

    @pl.when(h == 0)
    def _():
        for r, b in enumerate((b0, b1, b2, b3)):
            do[r] = b[...]
        dq[...] = jnp.zeros_like(dq)
        dk[...] = jnp.zeros_like(dk)
        dv[...] = jnp.zeros_like(dv)

    for i in range(GROUPS):
        qi = jnp.where(mine, q[i ^ s], zero)
        doi = jnp.where(mine, do[i ^ s], zero)
        stat = lse[0, i][:1]
        soft, back = [], []
        dot = jnp.zeros((1, rows), F32)
        for j in range(i + 1):
            tile = nt(k[j ^ s], qi)
            if j == i:
                tile = jnp.where(key <= query, tile, NEGATIVE)
            p = jnp.exp(tile - stat)
            dp = nt(v[j ^ s], doi)
            dot = dot + jnp.sum(p * dp, axis=0, keepdims=True)
            soft.append(p)
            back.append(dp)
        acc = jnp.zeros((rows, width), F32)
        for j in range(i + 1):
            ds = (soft[j] * (back[j] - dot)).astype(BF16)
            dk[j] += nn(ds, qi)
            dv[j] += nn(soft[j].astype(BF16), doi)
            acc = acc + tn(ds, jnp.where(mine, k[j ^ s], zero))
        dq[i] += acc

    @pl.when(h == pl.num_programs(0) - 1)
    def _():
        for i in range(GROUPS):
            ri = i ^ s
            c, n = cosine[ri], -sine[ri]
            out[ri, :, :width] = turn(dq[i] * 0.125, c, n).astype(BF16)
            out[ri, :, width : 2 * width] = turn(dk[i], c, n).astype(BF16)
            half = (0.5 * dv[i]).astype(BF16)
            out[ri, :, 2 * width :] = half
            vout[i, :, len(before) * width :] = half
            if before:
                vout[i, :, :width] = before[0][i]


def attention_back(part, me, q, k, v, b, lse, cosine, sine, *before):
    rows = q.shape[1]
    width = 2 * HEAD_DIM
    full = lambda *shape: pl.BlockSpec(shape, lambda h, me: (0,) * len(shape))
    pair = pl.BlockSpec((4, rows, width), lambda h, me: (0, 0, part))
    return pl.pallas_call(
        attn_back_kernel,
        grid_spec=pltpu.PrefetchScalarGridSpec(
            num_scalar_prefetch=1,
            grid=(2,),
            in_specs=[pair] * 3
            + [pl.BlockSpec((rows, width), lambda h, me: (0, part))] * 4
            + [pl.BlockSpec((1, 4, 8, rows), lambda h, me: (h, 0, 0, 0))]
            + [full(4, rows, 128)] * 2
            + [full(*one.shape) for one in before],
            out_specs=[full(4, rows, 3 * width), full(4, rows, (1 + len(before)) * width)],
            scratch_shapes=[pltpu.VMEM((4, rows, width), BF16)]
            + [pltpu.VMEM((4, rows, width), F32)] * 3,
        ),
        out_shape=[
            jax.ShapeDtypeStruct((4, rows, 3 * width), BF16),
            jax.ShapeDtypeStruct((4, rows, (1 + len(before)) * width), BF16),
        ],
        compiler_params=PARAMS,
        cost_estimate=cost(5 * 2 * 10 * rows * rows * width * 4, 4e6, 20 * rows * rows),
        name="attention_back",
    )(me, q, k, v, *b, lse, cosine, sine, *before)


def out_kernel(me, m0, m1, m2, m3, w0, w1, t, gains, middle, second):
    s = me[0]
    width = m0.shape[1]
    half = w1.shape[0]
    for j, w in enumerate((w0.at[w0.shape[0] - half :], w1)):
        cols = pl.ds(pl.multiple_of(((s % 2) ^ j) * half, half), half)
        part = None
        for r, m in enumerate((m0, m1, m2, m3)):
            one = nt(m[...], w[:, pl.ds(pl.multiple_of((s ^ r) * width, width), width)])
            part = one if part is None else part + one
        middle[:, cols] = t[:, cols].astype(F32) + part
    acc = middle[...]
    second[...] = (acc * inverse_rms(acc) * gains[1:2].astype(F32)).astype(BF16)


def vmem_call(kernel, name, shapes, me, args, estimate, scratch=()):
    full = lambda shape: pl.BlockSpec(shape, lambda i, me: (0,) * len(shape))
    outs = [jax.ShapeDtypeStruct(s, t) for s, t in shapes]
    return pl.pallas_call(
        kernel,
        grid_spec=pltpu.PrefetchScalarGridSpec(
            num_scalar_prefetch=1,
            grid=(1,),
            in_specs=[full(a.shape) for a in args],
            out_specs=[full(s) for s, _ in shapes],
            scratch_shapes=scratch,
        ),
        out_shape=outs,
        compiler_params=PARAMS,
        cost_estimate=estimate,
        name=name,
    )(me, *args)


def mlp_kernel(count, me, sa, sb, ga, gb, down, *refs):
    pieces, outs = refs[:count], refs[count : count + 5]
    sv, gv, wv, dv, hid, gback, uback, sback, sems = refs[count + 5 :]
    units, d = dv.shape
    share = d // count
    rows = sa.shape[0]
    copies = [pltpu.make_async_copy(sa, sv.at[0], sems.at[0])]
    parts = [[], []]
    for h in range(2):
        for i, piece in enumerate(pieces):
            at = pl.ds(pl.multiple_of((me[0] ^ i) * share, share), share)
            part = piece.at[h * units : (h + 1) * units]
            sem = sems.at[15 + h * count + i]
            parts[h].append(pltpu.make_async_copy(part, wv.at[h, :, at], sem))
    copies.append(pltpu.make_async_copy(ga, gv.at[0], sems.at[4]))
    copies.append(pltpu.make_async_copy(down.at[down.shape[0] - units :], dv, sems.at[1]))
    copies.append(pltpu.make_async_copy(sb, sv.at[1], sems.at[5]))
    copies.append(pltpu.make_async_copy(gb, gv.at[1], sems.at[6]))
    for copy in copies[:1] + parts[0] + parts[1] + copies[1:]:
        copy.start()
    writes = []

    def write(buf, out):
        copy = pltpu.make_async_copy(buf, out, sems.at[7 + len(writes)])
        copy.start()
        writes.append(copy)

    for i in range(2):
        copies[3 if i else 0].wait()
        if i == 0:
            for copy in parts[0]:
                copy.wait()
        gate = nt(sv[i], wv[0])
        if i == 0:
            for copy in parts[1]:
                copy.wait()
        up = nt(sv[i], wv[1])
        sg = jax.nn.sigmoid(gate)
        act = gate * sg
        hid[i] = (act * up).astype(BF16)
        at = slice(i * rows, (i + 1) * rows)
        write(hid.at[i], outs[0].at[at])
        copies[4 if i else 1].wait()
        if i == 0:
            copies[2].wait()
        hb = nt(gv[i], dv[...])
        gate_back = (hb * up * sg * (1.0 + gate * (1.0 - sg))).astype(BF16)
        up_back = (hb * act).astype(BF16)
        gback[i] = gate_back
        write(gback.at[i], outs[1].at[at])
        uback[i] = up_back
        write(uback.at[i], outs[2].at[at])
        sback[i] = (nn(gate_back, wv[0]) + nn(up_back, wv[1])).astype(BF16)
        write(sback.at[i], outs[3 + i])
    for copy in writes:
        copy.wait()


def any_call(kernel, name, shapes, me, args, estimate, scratch):
    return pl.pallas_call(
        kernel,
        grid_spec=pltpu.PrefetchScalarGridSpec(
            num_scalar_prefetch=1,
            grid=(1,),
            in_specs=[ANY] * len(args),
            out_specs=[ANY] * len(shapes),
            scratch_shapes=scratch,
        ),
        out_shape=[jax.ShapeDtypeStruct(s, t) for s, t in shapes],
        compiler_params=PARAMS,
        cost_estimate=estimate,
        name=name,
    )(me, *args)


def mlp(where, sa, sb, ga, gb, pieces, down):
    rows, d = sa.shape
    units = pieces[0].shape[0] // 2
    part = ((2 * rows, units), BF16)
    return any_call(
        functools.partial(mlp_kernel, len(pieces)),
        "mlp",
        [part] * 3 + [((rows, d), BF16)] * 2,
        where.reshape(1),
        [sa, sb, ga, gb, down, *pieces],
        cost(2 * 5 * 2 * rows * d * units, 12e6, 2 * rows * units),
        [pltpu.VMEM((2, rows, d), BF16)] * 2
        + [pltpu.VMEM((2, units, d), BF16), pltpu.VMEM((units, d), BF16)]
        + [pltpu.VMEM((2, rows, units), BF16)] * 3
        + [pltpu.VMEM((2, rows, d), BF16), pltpu.SemaphoreType.DMA((15 + 2 * len(pieces),))],
    )


def mlp_out_kernel(me, hn, hf, rest, o0, o1, o2, o3):
    rows = o0.shape[0]
    w = rest.at[rest.shape[0] - hn.shape[1] :]
    for h, outs in ((hn, (o0, o1)), (hf, (o2, o3))):
        for i, out in enumerate(outs):
            out[...] = nn(h[i * rows : (i + 1) * rows], w[...]).astype(BF16)


def unit_grad_kernel(count, me, *refs):
    ins, outs, acc = refs[: 2 * count + 4], refs[2 * count + 4 : -1], refs[-1]
    blocks = ins[2 * count :]
    y = me[0] % 2
    near = jnp.concatenate([blocks[0][...], blocks[1][...]], axis=0)
    far = jnp.concatenate([blocks[2][...], blocks[3][...]], axis=0)
    share = outs[0].shape[2]
    for i in range(count):
        acc[...] = tn(ins[2 * i][...], near) + tn(ins[2 * i + 1][...], far)
        for z in range(outs[0].shape[0]):
            for j in range(2):
                at = pl.multiple_of((2 * z + (y ^ j)) * share, share)
                outs[2 * i + j][z] = acc[:, pl.ds(at, share)].astype(BF16)


def unit_grads(pairs, blocks):
    n = lax.axis_size("fsdp")
    units, d = pairs[0][0].shape[1], blocks[0].shape[1]
    if n != 8:
        near, far = jnp.concatenate(blocks[:2]), jnp.concatenate(blocks[2:])
        outs = [(tn(a, near) + tn(b, far)).astype(BF16) for a, b in pairs]
        return [(jnp.transpose(o.reshape(units, n, d // n), (1, 0, 2)),) for o in outs]
    me = lax.axis_index("fsdp").astype(jnp.int32).reshape(1)
    outs = vmem_call(
        functools.partial(unit_grad_kernel, len(pairs)),
        "unit_grads",
        [((n // 2, units, d // n), BF16)] * (2 * len(pairs)),
        me,
        [a for pair in pairs for a in pair] + list(blocks),
        cost(2 * 4 * blocks[0].shape[0] * units * d * len(pairs), 6e6),
        [pltpu.VMEM((units, d), F32)],
    )
    return [outs[2 * i : 2 * i + 2] for i in range(len(pairs))]


def out_grad_kernel(me, m0, m1, m2, m3, beside, low, low_beside, gain, mine, other, acc):
    s, y = me[0], me[1] % 2
    width = m0.shape[1]
    half = acc.shape[0]
    low_here = low[:, pl.ds(pl.multiple_of((s % 2) * half, half), half)]
    for r, m in enumerate((m0, m1, m2, m3)):
        cols = pl.ds(pl.multiple_of((s ^ r) * width, width), width)
        theirs = beside[:, (r ^ 1) * width : ((r ^ 1) + 1) * width]
        acc[:, cols] = tn(low_here, m[...]) + tn(low_beside[...], theirs)
    share = mine.shape[2]
    for j, out in enumerate((mine, other)):
        for z in range(out.shape[0]):
            cols = pl.ds(pl.multiple_of((2 * z + (y ^ j)) * share, share), share)
            out[z, :half] = acc[:, cols].astype(BF16)
            out[z, half:] = gain[:, cols].astype(BF16)


def qkv_grad_kernel(me, normed, da, db, w, mine, other, acc):
    y = me[1] % 2
    share = mine.shape[2]
    pair = da.shape[1] // 3
    total = jnp.zeros((1, acc.shape[1]), F32)
    for part, dd in enumerate((da, db)):
        acc[3 * part * pair : 3 * (part + 1) * pair] = tn(dd[...], normed[...])
        for i in range(3):
            one = acc[(3 * part + i) * pair : (3 * part + i + 1) * pair]
            rows = w[(2 * i + part) * pair : (2 * i + part + 1) * pair].astype(F32)
            total = total + jnp.sum(one * rows, axis=0, keepdims=True)
    total = total / w[6 * pair : 6 * pair + 1].astype(F32)
    for j, out in enumerate((mine, other)):
        for z in range(mine.shape[0]):
            cols = pl.ds(pl.multiple_of((2 * z + (y ^ j)) * share, share), share)
            out[z, : 6 * pair] = acc[:, cols].astype(BF16)
    for f in range(acc.shape[1] // share):
        row = jnp.broadcast_to(total[:, f * share : (f + 1) * share], (8, share)).astype(BF16)
        for j, out in enumerate((mine, other)):

            @pl.when((f % 2) == (y ^ j))
            def _():
                out[f // 2, 6 * pair :] = row


def normed_back_kernel(half, me, da, db, w, n0, n1):
    pair = da.shape[2] // 3
    for i, out in enumerate((n0, n1)):
        r = 2 * half + i
        parts = [d[r, :, j * pair : (j + 1) * pair] for j in range(3) for d in (da, db)]
        out[...] = nn(jnp.concatenate(parts, axis=1), w[: 6 * pair]).astype(BF16)


def place_values_kernel(me, v, out):
    width = v.shape[2]
    for j in range(GROUPS):
        out[:, j * width : (j + 1) * width] = v[j].astype(F32)


def place_qkv_kernel(me, p0, p1, p2, p3, oq, ok, ov, gain):
    s = me[0]
    size = (p0.shape[0] - 8) // 6
    share = p0.shape[1]
    total = jnp.zeros((8, share), F32)
    for r, piece in enumerate((p0, p1, p2, p3)):
        for p in range(2):
            start = p * 3 * size
            at = pl.multiple_of((s ^ r) * 2 * size + p * size, size)
            for i, out in enumerate((oq, ok, ov)):
                block = piece[start + i * size : start + (i + 1) * size]
                out[:, pl.ds(at, size)] = jnp.transpose(block.astype(F32))
        total = total + piece[6 * size :].astype(F32)
    gain[...] = total[:1]


def place_units_kernel(me, p0, p1, p2, p3, *refs):
    outs, buf = refs[:-1], refs[-1]
    s = me[0]
    units = p0.shape[0] // len(outs)
    for r, p in enumerate((p0, p1, p2, p3)):
        buf[s ^ r] = p[...].astype(F32)
    for i, out in enumerate(outs):
        for j in range(GROUPS):
            out[:, j * units : (j + 1) * units] = jnp.transpose(buf[j, i * units : (i + 1) * units])


def place_out_kernel(me, own, other, out, gain):
    core = me[0] % 2
    half = own.shape[0] - 8
    for j, piece in enumerate((own, other)):
        at = pl.multiple_of((core ^ j) * half, half)
        out[:, pl.ds(at, half)] = jnp.transpose(piece[:half].astype(F32))
    gain[...] = own[half : half + 1].astype(F32) + other[half : half + 1].astype(F32)


def middle_kernel(me, p0, p1, p2, middle, g, gains, w0, w1, mback, mlow, mhalf, b0, b1, b2, b3, ggrad):
    s = me[0]
    width = b0.shape[1]
    dn = p0[...].astype(F32) + p1[...].astype(F32) + p2[...].astype(F32)
    v = middle[...]
    r = inverse_rms(v)
    x = v * r
    ggrad[...] = jnp.broadcast_to(jnp.sum(dn * x, axis=0, keepdims=True), ggrad.shape)
    dx = dn * gains[1:2].astype(F32)
    total = g[...].astype(F32) + r * (dx - x * jnp.mean(dx * x, axis=-1, keepdims=True))
    mback[...] = total
    mlow[...] = total.astype(BF16)
    half = w1.shape[0]
    lows = [mlow[:, pl.ds(pl.multiple_of(((s % 2) ^ j) * half, half), half)] for j in range(2)]
    mhalf[...] = lows[1]
    for i, b in enumerate((b0, b1, b2, b3)):
        cols = pl.ds(pl.multiple_of((s ^ i) * width, width), width)
        b[...] = (nn(lows[0], w0[w0.shape[0] - half :, cols]) + nn(lows[1], w1[:, cols])).astype(BF16)


def final_kernel(me, p0, p1, p2, t, gains, mback, out):
    dn = p0[...].astype(F32) + p1[...].astype(F32) + p2[...].astype(F32)
    v = t[...].astype(F32)
    r = inverse_rms(v)
    x = v * r
    dx = dn * gains[:1].astype(F32)
    out[...] = mback[...] + r * (dx - x * jnp.mean(dx * x, axis=-1, keepdims=True))


def after(value, *others):
    return lax.optimization_barrier((value,) + others)[0]


def all_after(values, *others):
    return list(lax.optimization_barrier(tuple(values) + others)[: len(values)])


def add(*terms):
    return sum((term.astype(F32) for term in terms[1:]), terms[0].astype(F32)).astype(BF16)


def seq_permute(value, flip):
    return lax.ppermute(value, "seq", [(i, i ^ flip) for i in range(GROUPS)])


def gather_four(own):
    near = seq_permute(own, 1)
    far = seq_permute(own, 2)
    return own, near, far, seq_permute(far, 1)


def exchange_four(pieces):
    return [pieces[0]] + [seq_permute(pieces[r], r) for r in (1, 2, 3)]


def fsdp_permute(value, flip):
    n = lax.axis_size("fsdp")
    return lax.ppermute(value, "fsdp", [(i, i ^ flip) for i in range(n)])


def fsdp_send(both):
    z = lax.axis_index("fsdp") // 2
    parts = [lax.dynamic_index_in_dim(both, z ^ k, 0, keepdims=False) for k in range(both.shape[0])]
    return [parts[0]] + [fsdp_permute(parts[k], 2 * k) for k in range(1, len(parts))]


def scatter_whole(parts):
    return lax.psum_scatter(parts, "fsdp", scatter_dimension=0, tiled=False)


def per_device(
    tokens,
    first_values,
    cotangent,
    first_gain,
    query_weight,
    key_weight,
    value_weight,
    out_weight,
    second_gain,
    gate_weight,
    up_weight,
    down_weight,
):
    n = lax.axis_size("fsdp")
    s = lax.axis_index("seq").astype(jnp.int32)
    me = s.reshape(1)
    place3 = [jnp.stack([s, lax.axis_index("fsdp").astype(jnp.int32), jnp.int32(p)]) for p in (0, 1)]
    t0, g0, f0 = tokens[0], cotangent[0], first_values[0]
    rows, d = t0.shape
    width = d // GROUPS
    pair = width // 2
    units = gate_weight.shape[1] // GROUPS
    share = d // n
    core = s % 2
    ring = n == 8

    def columns(v, which, size):
        return lax.dynamic_slice_in_dim(v, which * size, size, 1)

    here = lax.axis_index("fsdp").astype(jnp.int32)
    gains = jnp.concatenate([first_gain[None], second_gain[None], jnp.zeros((6, share), BF16)])
    qkv_weights = (query_weight, key_weight, value_weight)
    own_qkv = [columns(w, s, width).T for w in qkv_weights]
    own_qkv += [gains, columns(out_weight, core, d // 2).T]
    own_qkv = jnp.concatenate(own_qkv, axis=0)
    own_units = [columns(w, s, units).T for w in (gate_weight, up_weight, down_weight)]
    own_units, own_down = jnp.concatenate(own_units[:2], axis=0), own_units[2]
    places = (jnp.arange(4, dtype=jnp.int32) ^ s)[:, None] * rows + jnp.arange(rows, dtype=jnp.int32)
    half_dim = HEAD_DIM // 2
    freqs = jnp.exp(jnp.arange(half_dim, dtype=F32) * (-2.0 * math.log(10000.0) / HEAD_DIM))
    angles = places.astype(F32)[:, :, None] * jnp.tile(freqs, 4)
    sign = jnp.tile(jnp.repeat(jnp.array([-1.0, 1.0], F32), half_dim), 2)
    cosine, sine = jnp.cos(angles), jnp.sin(angles) * sign
    f = [columns(f0, s ^ r, width) for r in range(4)]
    if ring:
        first = [fsdp_permute(own_qkv, flip) for flip in (6, 4, 2)][::-1]
        first_y = fsdp_permute(own_qkv, 1)
    packed2 = seq_permute(jnp.concatenate([t0, f[2], f[3]], axis=1), 2)
    if ring:
        pieces = [own_qkv, first_y]
        for i in range(3):
            one = after(first[i], cosine, sine) if i == 0 else first[i]
            pieces += [one, fsdp_permute(one, 1)]
    else:
        pieces = [lax.all_gather(own_qkv, "fsdp", axis=1, tiled=True)]
        unit_pieces = [lax.all_gather(own_units, "fsdp", axis=1, tiled=True)]
    w_down = lax.all_gather(own_down, "fsdp", axis=1, tiled=True)
    where = here if ring else jnp.int32(0)
    packed1 = seq_permute(jnp.concatenate([t0, f[1]], axis=1), 1)
    crossing = jnp.concatenate([packed2[:, :d], packed2[:, d + width :]], axis=1)
    if ring:
        crossing = after(crossing, pieces[1], pieces[3], pieces[5], first[2])
    packed3 = seq_permute(crossing, 1)

    if ring:
        sent = after(own_units, pieces[3])
        second = [fsdp_permute(sent, flip) for flip in (2, 4, 6)]
        second_y = fsdp_permute(after(own_units, pieces[5]), 1)
    g2 = seq_permute(after(g0, packed2, *pieces[1::2]), 2)

    q, k, v, normed, w_qkv = qkv(where, t0, f[0], (packed1, packed2, packed3), pieces, cosine, sine)
    gains = w_qkv[3 * width : 3 * width + 8]
    w_out_sent = w_qkv[3 * width + 8 :]
    *m, lse_a = attention(0, me, q, k, v)
    if ring:
        second_y, *second = all_after([second_y] + second, m[0])
        q = after(q, second_y, *second)
    *m, lse_b = attention(1, me, q, k, v, *m)
    g2 = after(g2, m[0])
    w_out_other = after(seq_permute(w_out_sent, 1), m[0])
    m = all_after(m, g2, w_out_other)
    m = exchange_four(m)
    if ring:
        unit_pieces = [own_units, second_y]
        for one in second:
            unit_pieces += [one, after(fsdp_permute(one, 1), m[1])]
        m = all_after(m, *unit_pieces[3::2])
    middle, second = vmem_call(
        out_kernel,
        "out",
        [((rows, d), F32), ((rows, d), BF16)],
        me,
        [*m, w_qkv, w_out_other, t0, gains],
        cost(2 * rows * d * d, 8e6),
    )
    s0, s1, s2 = second, seq_permute(second, 1), seq_permute(second, 2)
    g1 = seq_permute(after(g0, second), 1)
    g3 = seq_permute(g2, 1)
    hid_near, gate_near, up_near, sb0, sb1 = mlp(where, s0, s1, g0, g1, unit_pieces, w_down)
    s2 = after(s2, sb0)
    s3 = seq_permute(s2, 1)
    hid_far, gate_far, up_far, sb2, sb3 = mlp(where, s2, s3, g2, g3, unit_pieces, w_down)
    sb_both = add(sb2, seq_permute(sb3, 1))
    p = [sb0, seq_permute(after(sb1, sb_both), 1), seq_permute(sb_both, 2)]

    (down_part,) = unit_grads([(hid_near, after(hid_far, p[1]))], (g0, g1, g2, g3))
    if ring:
        down_crossed = fsdp_permute(down_part[1], 1)
    o = vmem_call(
        mlp_out_kernel,
        "mlp_out",
        [((rows, d), BF16)] * 4,
        me,
        [hid_near, after(hid_far, down_part[0]), w_down],
        cost(2 * 4 * rows * d * units, 8e6),
    )
    gate_part, up_part = unit_grads(
        [(gate_near, after(gate_far, o[0])), (up_near, up_far)], (s0, s1, s2, s3)
    )
    o1, o3 = all_after([seq_permute(o[1], 1), seq_permute(o[3], 1)], gate_part[0])
    o_both = add(o[2], o3)
    p[2] = after(p[2], gate_part[0])
    p[0] = after(p[0], o_both, o1)
    if ring:
        down_both = add(down_part[0], after(down_crossed, p[2]))
        p[2] = after(p[2], down_both)
        gate_crossed = fsdp_permute(after(gate_part[1], down_both), 1)
        mixed_beside = seq_permute(jnp.concatenate(m, axis=1), 1)
        p[0] = after(p[0], mixed_beside)
    mback, mlow, mhalf, b0, b1, b2, b3, ggrad_second = vmem_call(
        middle_kernel,
        "middle",
        [((rows, d), F32), ((rows, d), BF16), ((rows, d // 2), BF16)]
        + [((rows, width), BF16)] * 4
        + [((8, d), F32)],
        me,
        [*p, middle, g0, gains, w_qkv, w_out_other],
        cost(2 * rows * d * d, 12e6),
    )
    b = exchange_four([b0, b1, b2, b3])
    flat = lambda x: x.reshape(4 * rows, -1)
    qb = q
    if ring:
        low_beside = seq_permute(mhalf, 1)
        out_part = vmem_call(
            out_grad_kernel,
            "out_grad",
            [((n // 2, d // 2 + 8, share), BF16)] * 2,
            place3[0],
            [*m, mixed_beside, mlow, low_beside, ggrad_second],
            cost(2 * rows * d * d, 6e6),
            [pltpu.VMEM((d // 2, d), F32)],
        )
        b[1:] = all_after(b[1:], out_part[0])
        down_sent = fsdp_send(after(down_both, b[2], b[3]))

    def qkv_grads(d_a, d_b):
        if ring:
            return vmem_call(
                qkv_grad_kernel,
                "qkv_grad",
                [((n // 2, 6 * pair + 8, share), BF16)] * 2,
                place3[0],
                [flat(normed), flat(d_a), flat(d_b), w_qkv],
                cost(2 * 4 * rows * d * 6 * pair, 6e6),
                [pltpu.VMEM((6 * pair, d), F32)],
            )
        whole = tn(jnp.concatenate([flat(d_a), flat(d_b)], axis=1), flat(normed))
        starts = [i * width + part * pair for part in range(2) for i in range(3)]
        w = jnp.concatenate([w_qkv[i : i + pair] for i in starts]).astype(F32)
        gain_part = jnp.sum(whole * w, axis=0, keepdims=True) / gains[:1].astype(F32)
        whole = jnp.concatenate([whole, gain_part, jnp.zeros((7, d), F32)]).astype(BF16)
        return (jnp.transpose(whole.reshape(6 * pair + 8, n, share), (1, 0, 2)),)

    d_a, v_a = attention_back(0, me, qb, k, v, b, lse_a, cosine, sine)
    o2 = seq_permute(after(o_both, d_a), 2)
    qb = after(qb, d_a)
    if ring:
        gate_both = add(gate_part[0], after(gate_crossed, d_a))
        down_share = add(*all_after(down_sent, d_a))
        gate_sent = fsdp_send(after(gate_both, down_share))
        up_crossed = fsdp_permute(after(up_part[1], gate_both), 1)
        qb = after(qb, gate_both, down_share)
    d_b, v_b = attention_back(1, me, qb, k, v, b, lse_b, cosine, sine, v_a)
    o2 = after(o2, d_b)
    d_b = after(d_b, o2)
    if ring:
        up_crossed, *gate_sent = all_after([up_crossed] + gate_sent, d_b)
        up_both = add(up_part[0], up_crossed)
        gate_share = add(*gate_sent)
        up_sent = fsdp_send(after(up_both, gate_share))
        out_crossed = fsdp_permute(after(out_part[1], up_both), 1)
        d_b = after(d_b, up_both, gate_share)

    def normed_back(half, d_b):
        return vmem_call(
            functools.partial(normed_back_kernel, half),
            "normed_back",
            [((rows, d), BF16)] * 2,
            me,
            [d_a, d_b, w_qkv],
            cost(2 * 2 * rows * d * 3 * width, 8e6),
        )

    nb2, nb3 = normed_back(1, d_b)
    nb_both = add(nb2, seq_permute(nb3, 1))
    crossed_far = seq_permute(nb_both, 2)
    qkv_sums = qkv_grads(d_a, after(d_b, nb_both))
    if ring:
        out_both = add(out_part[0], after(out_crossed, qkv_sums[0]))
        qkv_crossed = fsdp_permute(after(qkv_sums[1], out_both), 1)
    nb0, nb1 = normed_back(0, after(d_b, qkv_sums[0]))
    p = [nb0, seq_permute(nb1, 1), after(crossed_far, nb0)]
    if ring:
        up_share = add(*all_after(up_sent, nb0))
        out_sent = fsdp_send(after(out_both, up_share))
        p[1] = after(p[1], up_share)
    (tokens_grad,) = vmem_call(
        final_kernel,
        "final",
        [((rows, d), F32)],
        me,
        [*p, t0, gains, mback],
        cost(0, 6e6),
    )
    if ring:
        qkv_both = add(qkv_sums[0], after(qkv_crossed, tokens_grad))
        out_share = add(*all_after(out_sent, tokens_grad))
        qkv_sent = fsdp_send(after(qkv_both, out_share))
        units_sent = jnp.concatenate([gate_share, up_share, down_share], axis=0)
    else:
        gate_share, up_share, down_share, qkv_share = (
            scatter_whole(v[0]) for v in (gate_part, up_part, down_part, qkv_sums)
        )
        mixed_rows = jnp.zeros((rows, d), BF16)
        for r in range(4):
            mixed_rows = lax.dynamic_update_slice(mixed_rows, m[r], (0, (s ^ r) * width))
        out_part = tn(mlow, mixed_rows)
        halves = [lax.dynamic_slice_in_dim(out_part, (core ^ j) * (d // 2), d // 2) for j in range(2)]
        keep = jnp.concatenate([halves[0], ggrad_second]).reshape(d // 2 + 8, n, share)
        send = jnp.pad(halves[1], ((0, 8), (0, 0))).astype(BF16).reshape(d // 2 + 8, n, share)
        whole = (keep + seq_permute(send, 1).astype(F32)).astype(BF16)
        out_share = scatter_whole(jnp.transpose(whole, (1, 0, 2)))
        units_sent = jnp.concatenate([gate_share, up_share, down_share], axis=0)
    out_share = add(out_share, seq_permute(out_share, 2))
    v_all = lax.all_to_all(after(v_b, tokens_grad), "seq", split_axis=0, concat_axis=0)
    output = add(middle, o[0], o1, o2)[None]
    out_grad, second_gain_grad = vmem_call(
        place_out_kernel,
        "place_out",
        [((share, d), F32), ((1, share), F32)],
        me,
        [out_share, seq_permute(out_share, 1)],
        cost(0, 1e6),
    )
    (values_grad,) = vmem_call(
        place_values_kernel, "place_values", [((rows, d), F32)], me, [v_all], cost(0, 3e6)
    )
    units_far = seq_permute(units_sent, 2)
    if ring:
        qkv_share = add(*all_after(qkv_sent, out_grad, values_grad, output))
        units_far = after(units_far, qkv_share)
    qkv_far = seq_permute(qkv_share, 2)
    gate_grad, up_grad, down_grad = vmem_call(
        place_units_kernel,
        "place_units",
        [((share, 4 * units), F32)] * 3,
        me,
        [units_sent, seq_permute(units_sent, 1), units_far, seq_permute(units_far, 1)],
        cost(0, 3e6),
        [pltpu.VMEM((4, 3 * units, share), F32)],
    )
    qkv_far = after(qkv_far, gate_grad)
    qkv_all = [qkv_share, seq_permute(qkv_share, 1), qkv_far, seq_permute(qkv_far, 1)]
    query_grad, key_grad, value_grad, gain_grad = vmem_call(
        place_qkv_kernel,
        "place_qkv",
        [((share, d), F32)] * 3 + [((1, share), F32)],
        me,
        qkv_all,
        cost(0, 3e6),
    )
    return (
        output,
        tokens_grad[None],
        values_grad[None],
        gain_grad.reshape(share),
        query_grad,
        key_grad,
        value_grad,
        out_grad,
        second_gain_grad.reshape(share),
        gate_grad,
        up_grad,
        down_grad,
    )


def solution(mesh):
    rows = P("fsdp", "seq", None)
    weight = P("fsdp", None)
    gain = P("fsdp")
    in_specs = (rows,) * 3 + (gain,) + (weight,) * 4 + (gain,) + (weight,) * 3
    out_specs = (rows,) * 3 + (gain,) + (weight,) * 4 + (gain,) + (weight,) * 3
    return jax.shard_map(
        per_device, mesh=mesh, in_specs=in_specs, out_specs=out_specs, check_vma=False
    )
```

```python
import functools
import math

import jax
import jax.numpy as jnp
from jax import lax
from jax.experimental import pallas as pl
from jax.experimental.pallas import tpu as pltpu
from jax.sharding import PartitionSpec as P

HEADS = 16
HEAD_DIM = 64
GROUPS = 4
EPSILON = 1e-06
NEGATIVE = -1e30
F32 = jnp.float32
BF16 = jnp.bfloat16
PARAMS = pltpu.CompilerParams(vmem_limit_bytes=56 * 2**20)


def nn(a, b):
    return lax.dot_general(a, b, (((1,), (0,)), ((), ())), preferred_element_type=F32)


def nt(a, b):
    return lax.dot_general(a, b, (((1,), (1,)), ((), ())), preferred_element_type=F32)


def tn(a, b):
    return lax.dot_general(a, b, (((0,), (0,)), ((), ())), preferred_element_type=F32)


def cost(flops, nbytes, trans=0):
    flops, nbytes, trans = 1, 1, 0
    return pl.CostEstimate(flops=int(flops), bytes_accessed=int(nbytes), transcendentals=int(trans))


def turn(u, cosine, sine):
    lane = lax.broadcasted_iota(jnp.int32, (u.shape[0], 128), 1)
    first = lane % HEAD_DIM < HEAD_DIM // 2
    parts = []
    for j in range(u.shape[1] // 128):
        part = u[:, 128 * j : 128 * (j + 1)]
        other = jnp.where(first, pltpu.roll(part, 96, 1), pltpu.roll(part, 32, 1))
        parts.append(part * cosine + other * sine)
    return jnp.concatenate(parts, axis=1)


def inverse_rms(v):
    return lax.rsqrt(jnp.mean(v * v, axis=-1, keepdims=True) + EPSILON)


ANY = pl.BlockSpec(memory_space=pl.ANY)


def qkv_kernel(count, me, t0, f0, p1, p2, p3, *refs):
    pieces, rest = refs[:count], refs[count:]
    cosine, sine, q, k, v, n, w, tv, fv, sems = rest
    width = q.shape[-1]
    d = tv.shape[-1]
    share = d // count
    first = []
    for i, piece in enumerate(pieces):
        at = pl.ds(pl.multiple_of((me[0] ^ i) * share, share), share)
        first.append(pltpu.make_async_copy(piece, w.at[:, at], sems.at[8 + i]))
    loads = [(t0, f0)] + [(p.at[:, :d], p.at[:, d : d + width]) for p in (p1, p2, p3)]
    copies = []
    for i, (t, f) in enumerate(loads):
        copies.append(pltpu.make_async_copy(t, tv.at[i], sems.at[2 * i]))
        copies.append(pltpu.make_async_copy(f, fv.at[i], sems.at[2 * i + 1]))
    for copy in copies[:2] + first + copies[2:]:
        copy.start()
    for i in range(4):
        copies[2 * i].wait()
        if i == 0:
            for copy in first:
                copy.wait()
        gain = w[3 * width : 3 * width + 1].astype(F32)
        x = tv[i].astype(F32)
        normed = (x * inverse_rms(x) * gain).astype(BF16)
        n[i] = normed
        u = nt(normed, w[: 3 * width])
        c, s = cosine[i], sine[i]
        q[i] = (turn(u[:, :width], c, s).astype(BF16).astype(F32) * 0.125).astype(BF16)
        k[i] = turn(u[:, width : 2 * width], c, s).astype(BF16)
        copies[2 * i + 1].wait()
        v[i] = (0.5 * u[:, 2 * width :] + 0.5 * fv[i].astype(F32)).astype(BF16)


def qkv(where, t, f, packed, pieces, cosine, sine):
    rows, d = t.shape
    width = f.shape[1]
    full = lambda *shape: pl.BlockSpec(shape, lambda i, me: (0,) * len(shape))
    shapes = [(4, rows, width)] * 3 + [(4, rows, d), (pieces[0].shape[0], d)]
    return pl.pallas_call(
        functools.partial(qkv_kernel, len(pieces)),
        grid_spec=pltpu.PrefetchScalarGridSpec(
            num_scalar_prefetch=1,
            grid=(1,),
            in_specs=[ANY] * (5 + len(pieces)) + [full(4, rows, 128)] * 2,
            out_specs=[full(*s) for s in shapes],
            scratch_shapes=[
                pltpu.VMEM((4, rows, d), BF16),
                pltpu.VMEM((4, rows, width), BF16),
                pltpu.SemaphoreType.DMA((8 + len(pieces),)),
            ],
        ),
        out_shape=[jax.ShapeDtypeStruct(s, BF16) for s in shapes],
        compiler_params=PARAMS,
        cost_estimate=cost(2 * 4 * rows * d * 3 * width, 12e6),
        name="qkv",
    )(where.reshape(1), t, f, *packed, *pieces, cosine, sine)


def attn_kernel(me, q, k, v, *refs):
    before, (o0, o1, o2, o3, lse, o) = refs[:-6], refs[-6:]
    h = pl.program_id(0)
    rows, width = q.shape[1:]
    mine = lax.broadcasted_iota(jnp.int32, (1, width), 1) // HEAD_DIM == h
    row = lax.broadcasted_iota(jnp.int32, (rows, rows), 0)
    col = lax.broadcasted_iota(jnp.int32, (rows, rows), 1)
    s = me[0]
    for i in range(GROUPS):
        ri = i ^ s
        qi = jnp.where(mine, q[ri], jnp.zeros((), BF16))
        tiles = []
        for j in range(i + 1):
            tile = nt(qi, k[j ^ s])
            if j == i:
                tile = jnp.where(col <= row, tile, NEGATIVE)
            tiles.append(tile)
        largest = tiles[0].max(axis=1, keepdims=True)
        for tile in tiles[1:]:
            largest = jnp.maximum(largest, tile.max(axis=1, keepdims=True))
        tiles = [jnp.exp(tile - largest) for tile in tiles]
        total = tiles[0].sum(axis=1, keepdims=True)
        for tile in tiles[1:]:
            total = total + tile.sum(axis=1, keepdims=True)
        inverse = 1.0 / total
        acc = jnp.zeros((rows, width), F32)
        for j in range(i + 1):
            acc = acc + nn((tiles[j] * inverse).astype(BF16), v[j ^ s])
        o[ri] = jnp.where(mine, acc.astype(BF16), o[ri])
        stat = jnp.broadcast_to(largest + jnp.log(total), (rows, 128))
        lse[0, i] = jnp.transpose(stat)[:8]

    @pl.when(h == pl.num_programs(0) - 1)
    def _():
        for r, out in enumerate((o0, o1, o2, o3)):
            if before:
                out[:, :width] = before[r][...]
                out[:, width:] = o[r]
            else:
                out[...] = o[r]


def attention(part, me, q, k, v, *before):
    rows = q.shape[1]
    width = 2 * HEAD_DIM
    full = lambda *shape: pl.BlockSpec(shape, lambda h, me: (0,) * len(shape))
    pair = pl.BlockSpec((4, rows, width), lambda h, me: (0, 0, part))
    both = (rows, 2 * width if before else width)
    return pl.pallas_call(
        attn_kernel,
        grid_spec=pltpu.PrefetchScalarGridSpec(
            num_scalar_prefetch=1,
            grid=(2,),
            in_specs=[pair] * 3 + [full(*one.shape) for one in before],
            out_specs=[full(*both)] * 4
            + [pl.BlockSpec((1, 4, 8, rows), lambda h, me: (h, 0, 0, 0))],
            scratch_shapes=[pltpu.VMEM((4, rows, width), BF16)],
        ),
        out_shape=[jax.ShapeDtypeStruct(both, BF16)] * 4
        + [jax.ShapeDtypeStruct((2, 4, 8, rows), F32)],
        compiler_params=PARAMS,
        cost_estimate=cost(2 * 2 * 10 * rows * rows * width * 4, 4e6, 20 * rows * rows),
        name="attention",
    )(me, q, k, v, *before)


def attn_back_kernel(me, q, k, v, b0, b1, b2, b3, lse, cosine, sine, *rest):
    before, (out, vout, do, dq, dk, dv) = rest[:-6], rest[-6:]
    h = pl.program_id(0)
    rows, width = q.shape[1:]
    mine = lax.broadcasted_iota(jnp.int32, (1, width), 1) // HEAD_DIM == h
    key = lax.broadcasted_iota(jnp.int32, (rows, rows), 0)
    query = lax.broadcasted_iota(jnp.int32, (rows, rows), 1)
    s = me[0]
    zero = jnp.zeros((), BF16)

    @pl.when(h == 0)
    def _():
        for r, b in enumerate((b0, b1, b2, b3)):
            do[r] = b[...]
        dq[...] = jnp.zeros_like(dq)
        dk[...] = jnp.zeros_like(dk)
        dv[...] = jnp.zeros_like(dv)

    for i in range(GROUPS):
        qi = jnp.where(mine, q[i ^ s], zero)
        doi = jnp.where(mine, do[i ^ s], zero)
        stat = lse[0, i][:1]
        soft, back = [], []
        dot = jnp.zeros((1, rows), F32)
        for j in range(i + 1):
            tile = nt(k[j ^ s], qi)
            if j == i:
                tile = jnp.where(key <= query, tile, NEGATIVE)
            p = jnp.exp(tile - stat)
            dp = nt(v[j ^ s], doi)
            dot = dot + jnp.sum(p * dp, axis=0, keepdims=True)
            soft.append(p)
            back.append(dp)
        acc = jnp.zeros((rows, width), F32)
        for j in range(i + 1):
            ds = (soft[j] * (back[j] - dot)).astype(BF16)
            dk[j] += nn(ds, qi)
            dv[j] += nn(soft[j].astype(BF16), doi)
            acc = acc + tn(ds, jnp.where(mine, k[j ^ s], zero))
        dq[i] += acc

    @pl.when(h == pl.num_programs(0) - 1)
    def _():
        for i in range(GROUPS):
            ri = i ^ s
            c, n = cosine[ri], -sine[ri]
            out[ri, :, :width] = turn(dq[i] * 0.125, c, n).astype(BF16)
            out[ri, :, width : 2 * width] = turn(dk[i], c, n).astype(BF16)
            half = (0.5 * dv[i]).astype(BF16)
            out[ri, :, 2 * width :] = half
            vout[i, :, len(before) * width :] = half
            if before:
                vout[i, :, :width] = before[0][i]


def attention_back(part, me, q, k, v, b, lse, cosine, sine, *before):
    rows = q.shape[1]
    width = 2 * HEAD_DIM
    full = lambda *shape: pl.BlockSpec(shape, lambda h, me: (0,) * len(shape))
    pair = pl.BlockSpec((4, rows, width), lambda h, me: (0, 0, part))
    return pl.pallas_call(
        attn_back_kernel,
        grid_spec=pltpu.PrefetchScalarGridSpec(
            num_scalar_prefetch=1,
            grid=(2,),
            in_specs=[pair] * 3
            + [pl.BlockSpec((rows, width), lambda h, me: (0, part))] * 4
            + [pl.BlockSpec((1, 4, 8, rows), lambda h, me: (h, 0, 0, 0))]
            + [full(4, rows, 128)] * 2
            + [full(*one.shape) for one in before],
            out_specs=[full(4, rows, 3 * width), full(4, rows, (1 + len(before)) * width)],
            scratch_shapes=[pltpu.VMEM((4, rows, width), BF16)]
            + [pltpu.VMEM((4, rows, width), F32)] * 3,
        ),
        out_shape=[
            jax.ShapeDtypeStruct((4, rows, 3 * width), BF16),
            jax.ShapeDtypeStruct((4, rows, (1 + len(before)) * width), BF16),
        ],
        compiler_params=PARAMS,
        cost_estimate=cost(5 * 2 * 10 * rows * rows * width * 4, 4e6, 20 * rows * rows),
        name="attention_back",
    )(me, q, k, v, *b, lse, cosine, sine, *before)


def out_kernel(me, m0, m1, m2, m3, w0, x0, x1, x2, x3, t, gains, middle, second):
    s = me[0]
    width = m0.shape[1]
    quarter = x0.shape[0]
    first = w0.shape[0] - 4 * quarter
    ws = [[w0.at[first + i * quarter : first + (i + 1) * quarter] for i in range(4)], [x0, x1, x2, x3]]
    for j in range(2):
        for i, w in enumerate(ws[j]):
            start = ((s % 2) ^ j) * 4 * quarter + i * quarter
            cols = pl.ds(pl.multiple_of(start, quarter), quarter)
            part = None
            for r, m in enumerate((m0, m1, m2, m3)):
                one = nt(m[...], w[:, pl.ds(pl.multiple_of((s ^ r) * width, width), width)])
                part = one if part is None else part + one
            middle[:, cols] = t[:, cols].astype(F32) + part
    acc = middle[...]
    second[...] = (acc * inverse_rms(acc) * gains[1:2].astype(F32)).astype(BF16)


def vmem_call(kernel, name, shapes, me, args, estimate, scratch=()):
    full = lambda shape: pl.BlockSpec(shape, lambda i, me: (0,) * len(shape))
    outs = [jax.ShapeDtypeStruct(s, t) for s, t in shapes]
    return pl.pallas_call(
        kernel,
        grid_spec=pltpu.PrefetchScalarGridSpec(
            num_scalar_prefetch=1,
            grid=(1,),
            in_specs=[full(a.shape) for a in args],
            out_specs=[full(s) for s, _ in shapes],
            scratch_shapes=scratch,
        ),
        out_shape=outs,
        compiler_params=PARAMS,
        cost_estimate=estimate,
        name=name,
    )(me, *args)


def mlp_kernel(count, me, sa, sb, ga, gb, down, *refs):
    pieces, outs = refs[:count], refs[count : count + 5]
    sv, gv, wv, dv, hid, gback, uback, sback, sems = refs[count + 5 :]
    units, d = dv.shape
    share = d // count
    rows = sa.shape[0]
    copies = [pltpu.make_async_copy(sa, sv.at[0], sems.at[0])]
    parts = [[], []]
    for h in range(2):
        for i, piece in enumerate(pieces):
            at = pl.ds(pl.multiple_of((me[0] ^ i) * share, share), share)
            part = piece.at[h * units : (h + 1) * units]
            sem = sems.at[15 + h * count + i]
            parts[h].append(pltpu.make_async_copy(part, wv.at[h, :, at], sem))
    copies.append(pltpu.make_async_copy(ga, gv.at[0], sems.at[4]))
    copies.append(pltpu.make_async_copy(down.at[down.shape[0] - units :], dv, sems.at[1]))
    copies.append(pltpu.make_async_copy(sb, sv.at[1], sems.at[5]))
    copies.append(pltpu.make_async_copy(gb, gv.at[1], sems.at[6]))
    for copy in copies[:1] + parts[0] + parts[1] + copies[1:]:
        copy.start()
    writes = []

    def write(buf, out):
        copy = pltpu.make_async_copy(buf, out, sems.at[7 + len(writes)])
        copy.start()
        writes.append(copy)

    for i in range(2):
        copies[3 if i else 0].wait()
        if i == 0:
            for copy in parts[0]:
                copy.wait()
        gate = nt(sv[i], wv[0])
        if i == 0:
            for copy in parts[1]:
                copy.wait()
        up = nt(sv[i], wv[1])
        sg = jax.nn.sigmoid(gate)
        act = gate * sg
        hid[i] = (act * up).astype(BF16)
        at = slice(i * rows, (i + 1) * rows)
        write(hid.at[i], outs[0].at[at])
        copies[4 if i else 1].wait()
        if i == 0:
            copies[2].wait()
        hb = nt(gv[i], dv[...])
        gate_back = (hb * up * sg * (1.0 + gate * (1.0 - sg))).astype(BF16)
        up_back = (hb * act).astype(BF16)
        gback[i] = gate_back
        write(gback.at[i], outs[1].at[at])
        uback[i] = up_back
        write(uback.at[i], outs[2].at[at])
        sback[i] = (nn(gate_back, wv[0]) + nn(up_back, wv[1])).astype(BF16)
        write(sback.at[i], outs[3 + i])
    for copy in writes:
        copy.wait()


def any_call(kernel, name, shapes, me, args, estimate, scratch):
    return pl.pallas_call(
        kernel,
        grid_spec=pltpu.PrefetchScalarGridSpec(
            num_scalar_prefetch=1,
            grid=(1,),
            in_specs=[ANY] * len(args),
            out_specs=[ANY] * len(shapes),
            scratch_shapes=scratch,
        ),
        out_shape=[jax.ShapeDtypeStruct(s, t) for s, t in shapes],
        compiler_params=PARAMS,
        cost_estimate=estimate,
        name=name,
    )(me, *args)


def mlp(where, sa, sb, ga, gb, pieces, down):
    rows, d = sa.shape
    units = pieces[0].shape[0] // 2
    part = ((2 * rows, units), BF16)
    return any_call(
        functools.partial(mlp_kernel, len(pieces)),
        "mlp",
        [part] * 3 + [((rows, d), BF16)] * 2,
        where.reshape(1),
        [sa, sb, ga, gb, down, *pieces],
        cost(2 * 5 * 2 * rows * d * units, 12e6, 2 * rows * units),
        [pltpu.VMEM((2, rows, d), BF16)] * 2
        + [pltpu.VMEM((2, units, d), BF16), pltpu.VMEM((units, d), BF16)]
        + [pltpu.VMEM((2, rows, units), BF16)] * 3
        + [pltpu.VMEM((2, rows, d), BF16), pltpu.SemaphoreType.DMA((15 + 2 * len(pieces),))],
    )


def mlp_out_kernel(me, hn, hf, rest, o0, o1, o2, o3):
    rows = o0.shape[0]
    w = rest.at[rest.shape[0] - hn.shape[1] :]
    for h, outs in ((hn, (o0, o1)), (hf, (o2, o3))):
        for i, out in enumerate(outs):
            out[...] = nn(h[i * rows : (i + 1) * rows], w[...]).astype(BF16)


def unit_grad_kernel(count, me, *refs):
    ins, outs, acc = refs[: 2 * count + 4], refs[2 * count + 4 : -1], refs[-1]
    blocks = ins[2 * count :]
    y = me[0] % 2
    near = jnp.concatenate([blocks[0][...], blocks[1][...]], axis=0)
    far = jnp.concatenate([blocks[2][...], blocks[3][...]], axis=0)
    share = outs[0].shape[2]
    for i in range(count):
        acc[...] = tn(ins[2 * i][...], near) + tn(ins[2 * i + 1][...], far)
        for z in range(outs[0].shape[0]):
            for j in range(2):
                at = pl.multiple_of((2 * z + (y ^ j)) * share, share)
                outs[2 * i + j][z] = acc[:, pl.ds(at, share)].astype(BF16)


def unit_grads(pairs, blocks):
    n = lax.axis_size("fsdp")
    units, d = pairs[0][0].shape[1], blocks[0].shape[1]
    if n != 8:
        near, far = jnp.concatenate(blocks[:2]), jnp.concatenate(blocks[2:])
        outs = [(tn(a, near) + tn(b, far)).astype(BF16) for a, b in pairs]
        return [(jnp.transpose(o.reshape(units, n, d // n), (1, 0, 2)),) for o in outs]
    me = lax.axis_index("fsdp").astype(jnp.int32).reshape(1)
    outs = vmem_call(
        functools.partial(unit_grad_kernel, len(pairs)),
        "unit_grads",
        [((n // 2, units, d // n), BF16)] * (2 * len(pairs)),
        me,
        [a for pair in pairs for a in pair] + list(blocks),
        cost(2 * 4 * blocks[0].shape[0] * units * d * len(pairs), 6e6),
        [pltpu.VMEM((units, d), F32)],
    )
    return [outs[2 * i : 2 * i + 2] for i in range(len(pairs))]


def out_grad_kernel(me, m0, m1, m2, m3, beside, low, low_beside, gain, mine, other, acc):
    s, y = me[0], me[1] % 2
    width = m0.shape[1]
    half = acc.shape[0]
    low_here = low[:, pl.ds(pl.multiple_of((s % 2) * half, half), half)]
    for r, m in enumerate((m0, m1, m2, m3)):
        cols = pl.ds(pl.multiple_of((s ^ r) * width, width), width)
        theirs = beside[:, (r ^ 1) * width : ((r ^ 1) + 1) * width]
        acc[:, cols] = tn(low_here, m[...]) + tn(low_beside[...], theirs)
    share = mine.shape[2]
    for j, out in enumerate((mine, other)):
        for z in range(out.shape[0]):
            cols = pl.ds(pl.multiple_of((2 * z + (y ^ j)) * share, share), share)
            out[z, :half] = acc[:, cols].astype(BF16)
            out[z, half:] = gain[:, cols].astype(BF16)


def qkv_grad_kernel(me, normed, da, db, w, mine, other, acc):
    y = me[1] % 2
    share = mine.shape[2]
    pair = da.shape[1] // 3
    total = jnp.zeros((1, acc.shape[1]), F32)
    for part, dd in enumerate((da, db)):
        acc[3 * part * pair : 3 * (part + 1) * pair] = tn(dd[...], normed[...])
        for i in range(3):
            one = acc[(3 * part + i) * pair : (3 * part + i + 1) * pair]
            rows = w[(2 * i + part) * pair : (2 * i + part + 1) * pair].astype(F32)
            total = total + jnp.sum(one * rows, axis=0, keepdims=True)
    total = total / w[6 * pair : 6 * pair + 1].astype(F32)
    for j, out in enumerate((mine, other)):
        for z in range(mine.shape[0]):
            cols = pl.ds(pl.multiple_of((2 * z + (y ^ j)) * share, share), share)
            out[z, : 6 * pair] = acc[:, cols].astype(BF16)
    for f in range(acc.shape[1] // share):
        row = jnp.broadcast_to(total[:, f * share : (f + 1) * share], (8, share)).astype(BF16)
        for j, out in enumerate((mine, other)):

            @pl.when((f % 2) == (y ^ j))
            def _():
                out[f // 2, 6 * pair :] = row


def joined(r, da, db):
    pair = da.shape[2] // 3
    parts = [d[r, :, j * pair : (j + 1) * pair] for j in range(3) for d in (da, db)]
    return jnp.concatenate(parts, axis=1)


def normed_back_kernel(me, da, db, w, n3, n2, n1):
    for r, out in ((3, n3), (2, n2), (1, n1)):
        out[...] = nn(joined(r, da, db), w[: 2 * da.shape[2]]).astype(BF16)


def place_values_kernel(me, v, out):
    width = v.shape[2]
    for j in range(GROUPS):
        out[:, j * width : (j + 1) * width] = v[j].astype(F32)


def place_qkv_kernel(me, p0, p1, p2, p3, oq, ok, ov, gain):
    s = me[0]
    size = (p0.shape[0] - 8) // 6
    share = p0.shape[1]
    total = jnp.zeros((8, share), F32)
    for r, piece in enumerate((p0, p1, p2, p3)):
        for p in range(2):
            start = p * 3 * size
            at = pl.multiple_of((s ^ r) * 2 * size + p * size, size)
            for i, out in enumerate((oq, ok, ov)):
                block = piece[start + i * size : start + (i + 1) * size]
                out[:, pl.ds(at, size)] = jnp.transpose(block.astype(F32))
        total = total + piece[6 * size :].astype(F32)
    gain[...] = total[:1]


def place_units_kernel(me, p0, p1, p2, p3, *refs):
    outs, buf = refs[:-1], refs[-1]
    s = me[0]
    units = p0.shape[0] // len(outs)
    for r, p in enumerate((p0, p1, p2, p3)):
        buf[s ^ r] = p[...].astype(F32)
    for i, out in enumerate(outs):
        for j in range(GROUPS):
            out[:, j * units : (j + 1) * units] = jnp.transpose(buf[j, i * units : (i + 1) * units])


def place_out_kernel(me, own, other, out, gain):
    core = me[0] % 2
    half = own.shape[0] - 8
    for j, piece in enumerate((own, other)):
        at = pl.multiple_of((core ^ j) * half, half)
        out[:, pl.ds(at, half)] = jnp.transpose(piece[:half].astype(F32))
    gain[...] = own[half : half + 1].astype(F32) + other[half : half + 1].astype(F32)


def middle_kernel(me, p0, p1, p2, middle, g, gains, w0, x0, x1, x2, x3, mback, mlow, mhalf, b0, b1, b2, b3, ggrad):
    s = me[0]
    width = b0.shape[1]
    dn = p0[...].astype(F32) + p1[...].astype(F32) + p2[...].astype(F32)
    v = middle[...]
    r = inverse_rms(v)
    x = v * r
    ggrad[...] = jnp.broadcast_to(jnp.sum(dn * x, axis=0, keepdims=True), ggrad.shape)
    dx = dn * gains[1:2].astype(F32)
    total = g[...].astype(F32) + r * (dx - x * jnp.mean(dx * x, axis=-1, keepdims=True))
    mback[...] = total
    mlow[...] = total.astype(BF16)
    half = 4 * x0.shape[0]
    lows = [mlow[:, pl.ds(pl.multiple_of(((s % 2) ^ j) * half, half), half)] for j in range(2)]
    mhalf[...] = lows[1]
    for i, b in enumerate((b0, b1, b2, b3)):
        cols = pl.ds(pl.multiple_of((s ^ i) * width, width), width)
        w1 = jnp.concatenate([x[:, cols] for x in (x0, x1, x2, x3)], axis=0)
        b[...] = (nn(lows[0], w0[w0.shape[0] - half :, cols]) + nn(lows[1], w1)).astype(BF16)


def final_kernel(me, p1, p2, da, db, w, t, gains, mback, out):
    dn = nn(joined(0, da, db), w[: 2 * da.shape[2]])
    dn = dn + p1[...].astype(F32) + p2[...].astype(F32)
    v = t[...].astype(F32)
    r = inverse_rms(v)
    x = v * r
    dx = dn * gains[:1].astype(F32)
    out[...] = mback[...] + r * (dx - x * jnp.mean(dx * x, axis=-1, keepdims=True))


def after(value, *others):
    return lax.optimization_barrier((value,) + others)[0]


def all_after(values, *others):
    return list(lax.optimization_barrier(tuple(values) + others)[: len(values)])


def add(*terms):
    return sum((term.astype(F32) for term in terms[1:]), terms[0].astype(F32)).astype(BF16)


def seq_permute(value, flip):
    return lax.ppermute(value, "seq", [(i, i ^ flip) for i in range(GROUPS)])


def gather_four(own):
    near = seq_permute(own, 1)
    far = seq_permute(own, 2)
    return own, near, far, seq_permute(far, 1)


def exchange_four(pieces):
    return [pieces[0]] + [seq_permute(pieces[r], r) for r in (1, 2, 3)]


def fsdp_permute(value, flip):
    n = lax.axis_size("fsdp")
    return lax.ppermute(value, "fsdp", [(i, i ^ flip) for i in range(n)])


def fsdp_send(both):
    z = lax.axis_index("fsdp") // 2
    parts = [lax.dynamic_index_in_dim(both, z ^ k, 0, keepdims=False) for k in range(both.shape[0])]
    return [parts[0]] + [fsdp_permute(parts[k], 2 * k) for k in range(1, len(parts))]


def scatter_whole(parts):
    return lax.psum_scatter(parts, "fsdp", scatter_dimension=0, tiled=False)


def per_device(
    tokens,
    first_values,
    cotangent,
    first_gain,
    query_weight,
    key_weight,
    value_weight,
    out_weight,
    second_gain,
    gate_weight,
    up_weight,
    down_weight,
):
    n = lax.axis_size("fsdp")
    s = lax.axis_index("seq").astype(jnp.int32)
    me = s.reshape(1)
    place3 = [jnp.stack([s, lax.axis_index("fsdp").astype(jnp.int32), jnp.int32(p)]) for p in (0, 1)]
    t0, g0, f0 = tokens[0], cotangent[0], first_values[0]
    rows, d = t0.shape
    width = d // GROUPS
    pair = width // 2
    units = gate_weight.shape[1] // GROUPS
    share = d // n
    core = s % 2
    ring = n == 8

    def columns(v, which, size):
        return lax.dynamic_slice_in_dim(v, which * size, size, 1)

    here = lax.axis_index("fsdp").astype(jnp.int32)
    gains = jnp.concatenate([first_gain[None], second_gain[None], jnp.zeros((6, share), BF16)])
    qkv_weights = (query_weight, key_weight, value_weight)
    own_qkv = [columns(w, s, width).T for w in qkv_weights]
    own_qkv += [gains, columns(out_weight, core, d // 2).T]
    own_qkv = jnp.concatenate(own_qkv, axis=0)
    own_units = [columns(w, s, units).T for w in (gate_weight, up_weight, down_weight)]
    own_units, own_down = jnp.concatenate(own_units[:2], axis=0), own_units[2]
    places = (jnp.arange(4, dtype=jnp.int32) ^ s)[:, None] * rows + jnp.arange(rows, dtype=jnp.int32)
    half_dim = HEAD_DIM // 2
    freqs = jnp.exp(jnp.arange(half_dim, dtype=F32) * (-2.0 * math.log(10000.0) / HEAD_DIM))
    angles = places.astype(F32)[:, :, None] * jnp.tile(freqs, 4)
    sign = jnp.tile(jnp.repeat(jnp.array([-1.0, 1.0], F32), half_dim), 2)
    cosine, sine = jnp.cos(angles), jnp.sin(angles) * sign
    f = [columns(f0, s ^ r, width) for r in range(4)]
    if ring:
        first = [fsdp_permute(own_qkv, flip) for flip in (6, 4, 2)][::-1]
        first_y = fsdp_permute(own_qkv, 1)
    packed2 = seq_permute(jnp.concatenate([t0, f[2], f[3]], axis=1), 2)
    if ring:
        pieces = [own_qkv, first_y]
        for i in range(3):
            one = after(first[i], cosine, sine) if i == 0 else first[i]
            pieces += [one, fsdp_permute(one, 1)]
    else:
        pieces = [lax.all_gather(own_qkv, "fsdp", axis=1, tiled=True)]
        unit_pieces = [lax.all_gather(own_units, "fsdp", axis=1, tiled=True)]
    w_down = lax.all_gather(own_down, "fsdp", axis=1, tiled=True)
    where = here if ring else jnp.int32(0)
    packed1 = seq_permute(jnp.concatenate([t0, f[1]], axis=1), 1)
    crossing = jnp.concatenate([packed2[:, :d], packed2[:, d + width :]], axis=1)
    if ring:
        crossing = after(crossing, *pieces[1::2])
    packed3 = seq_permute(crossing, 1)

    if ring:
        sent = after(own_units, pieces[3])
        second = [fsdp_permute(sent, flip) for flip in (2, 4, 6)]
        second_y = fsdp_permute(after(own_units, pieces[5]), 1)
    g2 = seq_permute(after(g0, packed2, *pieces[1::2]), 2)

    q, k, v, normed, w_qkv = qkv(where, t0, f[0], (packed1, packed2, packed3), pieces, cosine, sine)
    gains = w_qkv[3 * width : 3 * width + 8]
    w_out_sent = w_qkv[3 * width + 8 :]
    *m, lse_a = attention(0, me, q, k, v)
    *m, lse_b = attention(1, me, q, k, v, *m)
    g2 = after(g2, m[0])
    if ring:
        second_y, *second = all_after([second_y] + second, m[0])
        m = all_after(m, second_y, *second)
    m = all_after(m, g2)
    m = exchange_four(m)
    w_out_sent = after(w_out_sent, m[2], m[3])
    w_out_other = [
        seq_permute(lax.slice_in_dim(w_out_sent, i * (d // 8), (i + 1) * (d // 8)), 1) for i in range(4)
    ]
    if ring:
        unit_pieces = [own_units, second_y]
        for one in second:
            unit_pieces += [one, after(fsdp_permute(one, 1), m[1])]
        m = all_after(m, *unit_pieces[3::2])
    m = all_after(m, *w_out_other, w_down)
    middle, second = vmem_call(
        out_kernel,
        "out",
        [((rows, d), F32), ((rows, d), BF16)],
        me,
        [*m, w_qkv, *w_out_other, t0, gains],
        cost(2 * rows * d * d, 8e6),
    )
    s0, s1, s2 = second, seq_permute(second, 1), seq_permute(second, 2)
    g1 = seq_permute(after(g0, second), 1)
    g3 = seq_permute(g2, 1)
    hid_near, gate_near, up_near, sb0, sb1 = mlp(where, s0, s1, g0, g1, unit_pieces, w_down)
    s2 = after(s2, sb0)
    s3 = seq_permute(s2, 1)
    hid_far, gate_far, up_far, sb2, sb3 = mlp(where, s2, s3, g2, g3, unit_pieces, w_down)
    sb_both = add(sb2, seq_permute(sb3, 1))
    p = [sb0, seq_permute(after(sb1, sb_both), 1), seq_permute(sb_both, 2)]

    (down_part,) = unit_grads([(hid_near, after(hid_far, p[1]))], (g0, g1, g2, g3))
    if ring:
        down_crossed = fsdp_permute(down_part[1], 1)
    o = vmem_call(
        mlp_out_kernel,
        "mlp_out",
        [((rows, d), BF16)] * 4,
        me,
        [hid_near, after(hid_far, down_part[0]), w_down],
        cost(2 * 4 * rows * d * units, 8e6),
    )
    (gate_part,) = unit_grads([(gate_near, after(gate_far, o[0]))], (s0, s1, s2, s3))
    o1, o3 = all_after([seq_permute(o[1], 1), seq_permute(o[3], 1)], gate_part[0])
    p[2] = after(p[2], gate_part[0])
    p[0] = after(p[0], o3, o1)
    if ring:
        down_both = add(down_part[0], after(down_crossed, p[2]))
        p[2] = after(p[2], down_both)
        gate_crossed = fsdp_permute(after(gate_part[1], down_both), 1)
        mixed_beside = seq_permute(jnp.concatenate(m, axis=1), 1)
        p[0] = after(p[0], mixed_beside)
    mback, mlow, mhalf, b0, b1, b2, b3, ggrad_second = vmem_call(
        middle_kernel,
        "middle",
        [((rows, d), F32), ((rows, d), BF16), ((rows, d // 2), BF16)]
        + [((rows, width), BF16)] * 4
        + [((8, d), F32)],
        me,
        [*p, middle, g0, gains, w_qkv, *w_out_other],
        cost(2 * rows * d * d, 12e6),
    )
    b = exchange_four([b0, b1, b2, b3])
    o_both = add(o[2], after(o3, mlow))
    flat = lambda x: x.reshape(4 * rows, -1)
    qb = q
    if ring:
        low_beside = seq_permute(mhalf, 1)
        out_part = vmem_call(
            out_grad_kernel,
            "out_grad",
            [((n // 2, d // 2 + 8, share), BF16)] * 2,
            place3[0],
            [*m, mixed_beside, mlow, low_beside, ggrad_second],
            cost(2 * rows * d * d, 6e6),
            [pltpu.VMEM((d // 2, d), F32)],
        )
        (up_part,) = unit_grads([(up_near, after(up_far, out_part[0]))], (s0, s1, s2, s3))
        b[1:] = all_after(b[1:], up_part[0], o_both)
        down_sent = fsdp_send(after(down_both, b[2], b[3]))
    else:
        (up_part,) = unit_grads([(up_near, up_far)], (s0, s1, s2, s3))

    def qkv_grads(d_a, d_b):
        if ring:
            return vmem_call(
                qkv_grad_kernel,
                "qkv_grad",
                [((n // 2, 6 * pair + 8, share), BF16)] * 2,
                place3[0],
                [flat(normed), flat(d_a), flat(d_b), w_qkv],
                cost(2 * 4 * rows * d * 6 * pair, 6e6),
                [pltpu.VMEM((6 * pair, d), F32)],
            )
        whole = tn(jnp.concatenate([flat(d_a), flat(d_b)], axis=1), flat(normed))
        starts = [i * width + part * pair for part in range(2) for i in range(3)]
        w = jnp.concatenate([w_qkv[i : i + pair] for i in starts]).astype(F32)
        gain_part = jnp.sum(whole * w, axis=0, keepdims=True) / gains[:1].astype(F32)
        whole = jnp.concatenate([whole, gain_part, jnp.zeros((7, d), F32)]).astype(BF16)
        return (jnp.transpose(whole.reshape(6 * pair + 8, n, share), (1, 0, 2)),)

    d_a, v_a = attention_back(0, me, qb, k, v, b, lse_a, cosine, sine)
    o2 = seq_permute(after(o_both, d_a), 2)
    qb = after(qb, d_a)
    if ring:
        gate_both = add(gate_part[0], after(gate_crossed, d_a))
        down_share = add(*all_after(down_sent, d_a))
        gate_sent = fsdp_send(after(gate_both, down_share))
        up_crossed = fsdp_permute(after(up_part[1], gate_both), 1)
        qb = after(qb, gate_both, down_share)
    d_b, v_b = attention_back(1, me, qb, k, v, b, lse_b, cosine, sine, v_a)
    o2 = after(o2, d_b)
    d_b = after(d_b, o2)
    if ring:
        up_crossed, *gate_sent = all_after([up_crossed] + gate_sent, d_b)
        up_both = add(up_part[0], up_crossed)
        gate_share = add(*gate_sent)
        up_sent = fsdp_send(after(up_both, gate_share))
        out_crossed = fsdp_permute(after(out_part[1], up_both), 1)
        d_b = after(d_b, up_both, gate_share)

    nb3, nb2, nb1 = vmem_call(
        normed_back_kernel,
        "normed_back",
        [((rows, d), BF16)] * 3,
        me,
        [d_a, d_b, w_qkv],
        cost(2 * 3 * rows * d * 3 * width, 8e6),
    )
    nb_both = add(nb2, seq_permute(nb3, 1))
    beside = seq_permute(nb1, 1)
    crossed_far = seq_permute(nb_both, 2)
    qkv_sums = qkv_grads(d_a, after(d_b, nb_both, beside))
    crossed_far = after(crossed_far, qkv_sums[0])
    if ring:
        out_both = add(out_part[0], after(out_crossed, qkv_sums[0]))
        qkv_crossed = fsdp_permute(after(qkv_sums[1], out_both), 1)
        up_share = add(*all_after(up_sent, qkv_sums[0]))
        out_sent = fsdp_send(after(out_both, up_share))
        beside = after(beside, up_share)
    (tokens_grad,) = vmem_call(
        final_kernel,
        "final",
        [((rows, d), F32)],
        me,
        [beside, crossed_far, d_a, d_b, w_qkv, t0, gains, mback],
        cost(0, 6e6),
    )
    if ring:
        qkv_both = add(qkv_sums[0], after(qkv_crossed, tokens_grad))
        out_share = add(*all_after(out_sent, tokens_grad))
        qkv_sent = fsdp_send(after(qkv_both, out_share))
        units_sent = after(jnp.concatenate([gate_share, up_share, down_share], axis=0), tokens_grad)
    else:
        gate_share, up_share, down_share, qkv_share = (
            scatter_whole(v[0]) for v in (gate_part, up_part, down_part, qkv_sums)
        )
        mixed_rows = jnp.zeros((rows, d), BF16)
        for r in range(4):
            mixed_rows = lax.dynamic_update_slice(mixed_rows, m[r], (0, (s ^ r) * width))
        out_part = tn(mlow, mixed_rows)
        halves = [lax.dynamic_slice_in_dim(out_part, (core ^ j) * (d // 2), d // 2) for j in range(2)]
        keep = jnp.concatenate([halves[0], ggrad_second]).reshape(d // 2 + 8, n, share)
        send = jnp.pad(halves[1], ((0, 8), (0, 0))).astype(BF16).reshape(d // 2 + 8, n, share)
        whole = (keep + seq_permute(send, 1).astype(F32)).astype(BF16)
        out_share = scatter_whole(jnp.transpose(whole, (1, 0, 2)))
        units_sent = jnp.concatenate([gate_share, up_share, down_share], axis=0)
    out_share = add(out_share, seq_permute(out_share, 2))
    v_all = lax.all_to_all(after(v_b, tokens_grad), "seq", split_axis=0, concat_axis=0)
    output = add(middle, o[0], o1, o2)[None]
    out_grad, second_gain_grad = vmem_call(
        place_out_kernel,
        "place_out",
        [((share, d), F32), ((1, share), F32)],
        me,
        [out_share, seq_permute(out_share, 1)],
        cost(0, 1e6),
    )
    (values_grad,) = vmem_call(
        place_values_kernel, "place_values", [((rows, d), F32)], me, [v_all], cost(0, 3e6)
    )
    units_far = seq_permute(units_sent, 2)
    if ring:
        qkv_share = add(*all_after(qkv_sent, out_grad, values_grad, output))
        units_far = after(units_far, qkv_share)
    qkv_far = seq_permute(qkv_share, 2)
    gate_grad, up_grad, down_grad = vmem_call(
        place_units_kernel,
        "place_units",
        [((share, 4 * units), F32)] * 3,
        me,
        [units_sent, seq_permute(units_sent, 1), units_far, seq_permute(units_far, 1)],
        cost(0, 3e6),
        [pltpu.VMEM((4, 3 * units, share), F32)],
    )
    qkv_far = after(qkv_far, gate_grad)
    qkv_all = [qkv_share, seq_permute(qkv_share, 1), qkv_far, seq_permute(qkv_far, 1)]
    query_grad, key_grad, value_grad, gain_grad = vmem_call(
        place_qkv_kernel,
        "place_qkv",
        [((share, d), F32)] * 3 + [((1, share), F32)],
        me,
        qkv_all,
        cost(0, 3e6),
    )
    return (
        output,
        tokens_grad[None],
        values_grad[None],
        gain_grad.reshape(share),
        query_grad,
        key_grad,
        value_grad,
        out_grad,
        second_gain_grad.reshape(share),
        gate_grad,
        up_grad,
        down_grad,
    )


def solution(mesh):
    rows = P("fsdp", "seq", None)
    weight = P("fsdp", None)
    gain = P("fsdp")
    in_specs = (rows,) * 3 + (gain,) + (weight,) * 4 + (gain,) + (weight,) * 3
    out_specs = (rows,) * 3 + (gain,) + (weight,) * 4 + (gain,) + (weight,) * 3
    return jax.shard_map(
        per_device, mesh=mesh, in_specs=in_specs, out_specs=out_specs, check_vma=False
    )
```

```python
import functools
import math

import jax
import jax.numpy as jnp
from jax import lax
from jax.experimental import pallas as pl
from jax.experimental.pallas import tpu as pltpu
from jax.sharding import PartitionSpec as P

HEADS = 16
HEAD_DIM = 64
GROUPS = 4
EPSILON = 1e-06
NEGATIVE = -1e30
F32 = jnp.float32
BF16 = jnp.bfloat16
PARAMS = pltpu.CompilerParams(vmem_limit_bytes=56 * 2**20)


def nn(a, b):
    return lax.dot_general(a, b, (((1,), (0,)), ((), ())), preferred_element_type=F32)


def nt(a, b):
    return lax.dot_general(a, b, (((1,), (1,)), ((), ())), preferred_element_type=F32)


def tn(a, b):
    return lax.dot_general(a, b, (((0,), (0,)), ((), ())), preferred_element_type=F32)


def cost(flops, nbytes, trans=0):
    flops, nbytes, trans = 1, 1, 0
    return pl.CostEstimate(flops=int(flops), bytes_accessed=int(nbytes), transcendentals=int(trans))


def turn(u, cosine, sine):
    lane = lax.broadcasted_iota(jnp.int32, (u.shape[0], 128), 1)
    first = lane % HEAD_DIM < HEAD_DIM // 2
    parts = []
    for j in range(u.shape[1] // 128):
        part = u[:, 128 * j : 128 * (j + 1)]
        other = jnp.where(first, pltpu.roll(part, 96, 1), pltpu.roll(part, 32, 1))
        parts.append(part * cosine + other * sine)
    return jnp.concatenate(parts, axis=1)


def inverse_rms(v):
    return lax.rsqrt(jnp.mean(v * v, axis=-1, keepdims=True) + EPSILON)


ANY = pl.BlockSpec(memory_space=pl.ANY)


def qkv_kernel(count, me, t0, f0, p1, p2, p3, *refs):
    pieces, rest = refs[:count], refs[count:]
    cosine, sine, q, k, v, n, w, tv, fv, sems = rest
    width = q.shape[-1]
    d = tv.shape[-1]
    share = d // count
    first = []
    for i, piece in enumerate(pieces):
        at = pl.ds(pl.multiple_of((me[0] ^ i) * share, share), share)
        first.append(pltpu.make_async_copy(piece, w.at[:, at], sems.at[8 + i]))
    loads = [(t0, f0)] + [(p.at[:, :d], p.at[:, d : d + width]) for p in (p1, p2, p3)]
    copies = []
    for i, (t, f) in enumerate(loads):
        copies.append(pltpu.make_async_copy(t, tv.at[i], sems.at[2 * i]))
        copies.append(pltpu.make_async_copy(f, fv.at[i], sems.at[2 * i + 1]))
    for copy in copies[:2] + first + copies[2:]:
        copy.start()
    for i in range(4):
        copies[2 * i].wait()
        if i == 0:
            for copy in first:
                copy.wait()
        gain = w[3 * width : 3 * width + 1].astype(F32)
        x = tv[i].astype(F32)
        normed = (x * inverse_rms(x) * gain).astype(BF16)
        n[i] = normed
        u = nt(normed, w[: 3 * width])
        c, s = cosine[i], sine[i]
        q[i] = (turn(u[:, :width], c, s).astype(BF16).astype(F32) * 0.125).astype(BF16)
        k[i] = turn(u[:, width : 2 * width], c, s).astype(BF16)
        copies[2 * i + 1].wait()
        v[i] = (0.5 * u[:, 2 * width :] + 0.5 * fv[i].astype(F32)).astype(BF16)


def qkv(where, t, f, packed, pieces, cosine, sine):
    rows, d = t.shape
    width = f.shape[1]
    full = lambda *shape: pl.BlockSpec(shape, lambda i, me: (0,) * len(shape))
    shapes = [(4, rows, width)] * 3 + [(4, rows, d), (pieces[0].shape[0], d)]
    return pl.pallas_call(
        functools.partial(qkv_kernel, len(pieces)),
        grid_spec=pltpu.PrefetchScalarGridSpec(
            num_scalar_prefetch=1,
            grid=(1,),
            in_specs=[ANY] * (5 + len(pieces)) + [full(4, rows, 128)] * 2,
            out_specs=[full(*s) for s in shapes],
            scratch_shapes=[
                pltpu.VMEM((4, rows, d), BF16),
                pltpu.VMEM((4, rows, width), BF16),
                pltpu.SemaphoreType.DMA((8 + len(pieces),)),
            ],
        ),
        out_shape=[jax.ShapeDtypeStruct(s, BF16) for s in shapes],
        compiler_params=PARAMS,
        cost_estimate=cost(2 * 4 * rows * d * 3 * width, 12e6),
        name="qkv",
    )(where.reshape(1), t, f, *packed, *pieces, cosine, sine)


def attn_kernel(me, q, k, v, *refs):
    before, (o0, o1, o2, o3, lse, o) = refs[:-6], refs[-6:]
    h = pl.program_id(0)
    rows, width = q.shape[1:]
    mine = lax.broadcasted_iota(jnp.int32, (1, width), 1) // HEAD_DIM == h
    row = lax.broadcasted_iota(jnp.int32, (rows, rows), 0)
    col = lax.broadcasted_iota(jnp.int32, (rows, rows), 1)
    s = me[0]
    for i in range(GROUPS):
        ri = i ^ s
        qi = jnp.where(mine, q[ri], jnp.zeros((), BF16))
        tiles = []
        for j in range(i + 1):
            tile = nt(qi, k[j ^ s])
            if j == i:
                tile = jnp.where(col <= row, tile, NEGATIVE)
            tiles.append(tile)
        largest = tiles[0].max(axis=1, keepdims=True)
        for tile in tiles[1:]:
            largest = jnp.maximum(largest, tile.max(axis=1, keepdims=True))
        tiles = [jnp.exp(tile - largest) for tile in tiles]
        total = tiles[0].sum(axis=1, keepdims=True)
        for tile in tiles[1:]:
            total = total + tile.sum(axis=1, keepdims=True)
        inverse = 1.0 / total
        acc = jnp.zeros((rows, width), F32)
        for j in range(i + 1):
            acc = acc + nn((tiles[j] * inverse).astype(BF16), v[j ^ s])
        o[ri] = jnp.where(mine, acc.astype(BF16), o[ri])
        stat = jnp.broadcast_to(largest + jnp.log(total), (rows, 128))
        lse[0, i] = jnp.transpose(stat)[:8]

    @pl.when(h == pl.num_programs(0) - 1)
    def _():
        for r, out in enumerate((o0, o1, o2, o3)):
            if before:
                out[:, :width] = before[r][...]
                out[:, width:] = o[r]
            else:
                out[...] = o[r]


def attention(part, me, q, k, v, *before):
    rows = q.shape[1]
    width = 2 * HEAD_DIM
    full = lambda *shape: pl.BlockSpec(shape, lambda h, me: (0,) * len(shape))
    pair = pl.BlockSpec((4, rows, width), lambda h, me: (0, 0, part))
    both = (rows, 2 * width if before else width)
    return pl.pallas_call(
        attn_kernel,
        grid_spec=pltpu.PrefetchScalarGridSpec(
            num_scalar_prefetch=1,
            grid=(2,),
            in_specs=[pair] * 3 + [full(*one.shape) for one in before],
            out_specs=[full(*both)] * 4
            + [pl.BlockSpec((1, 4, 8, rows), lambda h, me: (h, 0, 0, 0))],
            scratch_shapes=[pltpu.VMEM((4, rows, width), BF16)],
        ),
        out_shape=[jax.ShapeDtypeStruct(both, BF16)] * 4
        + [jax.ShapeDtypeStruct((2, 4, 8, rows), F32)],
        compiler_params=PARAMS,
        cost_estimate=cost(2 * 2 * 10 * rows * rows * width * 4, 4e6, 20 * rows * rows),
        name="attention",
    )(me, q, k, v, *before)


def attn_back_kernel(me, q, k, v, b0, b1, b2, b3, lse, cosine, sine, *rest):
    before, (out, vout, do, dq, dk, dv) = rest[:-6], rest[-6:]
    h = pl.program_id(0)
    rows, width = q.shape[1:]
    mine = lax.broadcasted_iota(jnp.int32, (1, width), 1) // HEAD_DIM == h
    key = lax.broadcasted_iota(jnp.int32, (rows, rows), 0)
    query = lax.broadcasted_iota(jnp.int32, (rows, rows), 1)
    s = me[0]
    zero = jnp.zeros((), BF16)

    @pl.when(h == 0)
    def _():
        for r, b in enumerate((b0, b1, b2, b3)):
            do[r] = b[...]
        dq[...] = jnp.zeros_like(dq)
        dk[...] = jnp.zeros_like(dk)
        dv[...] = jnp.zeros_like(dv)

    for i in range(GROUPS):
        qi = jnp.where(mine, q[i ^ s], zero)
        doi = jnp.where(mine, do[i ^ s], zero)
        stat = lse[0, i][:1]
        soft, back = [], []
        dot = jnp.zeros((1, rows), F32)
        for j in range(i + 1):
            tile = nt(k[j ^ s], qi)
            if j == i:
                tile = jnp.where(key <= query, tile, NEGATIVE)
            p = jnp.exp(tile - stat)
            dp = nt(v[j ^ s], doi)
            dot = dot + jnp.sum(p * dp, axis=0, keepdims=True)
            soft.append(p)
            back.append(dp)
        acc = jnp.zeros((rows, width), F32)
        for j in range(i + 1):
            ds = (soft[j] * (back[j] - dot)).astype(BF16)
            dk[j] += nn(ds, qi)
            dv[j] += nn(soft[j].astype(BF16), doi)
            acc = acc + tn(ds, jnp.where(mine, k[j ^ s], zero))
        dq[i] += acc

    @pl.when(h == pl.num_programs(0) - 1)
    def _():
        for i in range(GROUPS):
            ri = i ^ s
            c, n = cosine[ri], -sine[ri]
            out[ri, :, :width] = turn(dq[i] * 0.125, c, n).astype(BF16)
            out[ri, :, width : 2 * width] = turn(dk[i], c, n).astype(BF16)
            half = (0.5 * dv[i]).astype(BF16)
            out[ri, :, 2 * width :] = half
            vout[i, :, len(before) * width :] = half
            if before:
                vout[i, :, :width] = before[0][i]


def attention_back(part, me, q, k, v, b, lse, cosine, sine, *before):
    rows = q.shape[1]
    width = 2 * HEAD_DIM
    full = lambda *shape: pl.BlockSpec(shape, lambda h, me: (0,) * len(shape))
    pair = pl.BlockSpec((4, rows, width), lambda h, me: (0, 0, part))
    return pl.pallas_call(
        attn_back_kernel,
        grid_spec=pltpu.PrefetchScalarGridSpec(
            num_scalar_prefetch=1,
            grid=(2,),
            in_specs=[pair] * 3
            + [pl.BlockSpec((rows, width), lambda h, me: (0, part))] * 4
            + [pl.BlockSpec((1, 4, 8, rows), lambda h, me: (h, 0, 0, 0))]
            + [full(4, rows, 128)] * 2
            + [full(*one.shape) for one in before],
            out_specs=[full(4, rows, 3 * width), full(4, rows, (1 + len(before)) * width)],
            scratch_shapes=[pltpu.VMEM((4, rows, width), BF16)]
            + [pltpu.VMEM((4, rows, width), F32)] * 3,
        ),
        out_shape=[
            jax.ShapeDtypeStruct((4, rows, 3 * width), BF16),
            jax.ShapeDtypeStruct((4, rows, (1 + len(before)) * width), BF16),
        ],
        compiler_params=PARAMS,
        cost_estimate=cost(5 * 2 * 10 * rows * rows * width * 4, 4e6, 20 * rows * rows),
        name="attention_back",
    )(me, q, k, v, *b, lse, cosine, sine, *before)


def out_kernel(me, m0, m1, m2, m3, w0, x0, x1, x2, x3, t, gains, middle, lo, hi):
    s = me[0]
    width = m0.shape[1]
    quarter = x0.shape[0]
    first = w0.shape[0] - 4 * quarter
    ws = [[w0.at[first + i * quarter : first + (i + 1) * quarter] for i in range(4)], [x0, x1, x2, x3]]
    for j in range(2):
        for i, w in enumerate(ws[j]):
            start = ((s % 2) ^ j) * 4 * quarter + i * quarter
            cols = pl.ds(pl.multiple_of(start, quarter), quarter)
            part = None
            for r, m in enumerate((m0, m1, m2, m3)):
                one = nt(m[...], w[:, pl.ds(pl.multiple_of((s ^ r) * width, width), width)])
                part = one if part is None else part + one
            middle[:, cols] = t[:, cols].astype(F32) + part
    acc = middle[...]
    second = (acc * inverse_rms(acc) * gains[1:2].astype(F32)).astype(BF16)
    lo[...] = second[: lo.shape[0]]
    hi[...] = second[lo.shape[0] :]


def vmem_call(kernel, name, shapes, me, args, estimate, scratch=()):
    full = lambda shape: pl.BlockSpec(shape, lambda i, me: (0,) * len(shape))
    outs = [jax.ShapeDtypeStruct(s, t) for s, t in shapes]
    return pl.pallas_call(
        kernel,
        grid_spec=pltpu.PrefetchScalarGridSpec(
            num_scalar_prefetch=1,
            grid=(1,),
            in_specs=[full(a.shape) for a in args],
            out_specs=[full(s) for s, _ in shapes],
            scratch_shapes=scratch,
        ),
        out_shape=outs,
        compiler_params=PARAMS,
        cost_estimate=estimate,
        name=name,
    )(me, *args)


def mlp_kernel(count, me, sa0, sa1, sb0, sb1, ga, gb, *refs):
    pieces, outs = refs[: 3 * count], refs[3 * count : 3 * count + 5]
    sv, gv, wv, hid, gback, uback, sback, sems = refs[3 * count + 5 :]
    _, units, d = wv.shape
    rows = ga.shape[0]
    copies = [pltpu.make_async_copy(sa0, sv.at[0, : rows // 2], sems.at[0])]
    copies.append(pltpu.make_async_copy(sa1, sv.at[0, rows // 2 :], sems.at[1]))
    parts = []
    for h in range(3):
        loads = []
        if count == 1:
            loads.append((pieces[h], wv.at[h]))
        else:
            share = d // 8
            for k in range(4):
                mine, other = pieces[h * count + k], pieces[h * count + 4].at[k * units : (k + 1) * units]
                for piece, flip in ((mine, 2 * k), (other, 2 * k + 1)):
                    at = pl.ds(pl.multiple_of((me[0] ^ flip) * share, share), share)
                    loads.append((piece, wv.at[h, :, at]))
        sem = lambda i, h=h: sems.at[15 + 8 * h + i]
        parts.append([pltpu.make_async_copy(a, b, sem(i)) for i, (a, b) in enumerate(loads)])
    copies.append(pltpu.make_async_copy(ga, gv.at[0], sems.at[4]))
    copies.append(pltpu.make_async_copy(sb0, sv.at[1, : rows // 2], sems.at[2]))
    copies.append(pltpu.make_async_copy(sb1, sv.at[1, rows // 2 :], sems.at[5]))
    copies.append(pltpu.make_async_copy(gb, gv.at[1], sems.at[6]))
    for copy in copies[:2] + parts[0] + parts[1] + copies[2:3] + parts[2] + copies[3:]:
        copy.start()
    writes = []

    def write(buf, out):
        copy = pltpu.make_async_copy(buf, out, sems.at[7 + len(writes)])
        copy.start()
        writes.append(copy)

    for i in range(2):
        copies[3 if i else 0].wait()
        copies[4 if i else 1].wait()
        if i == 0:
            for copy in parts[0]:
                copy.wait()
        gate = nt(sv[i], wv[0])
        if i == 0:
            for copy in parts[1]:
                copy.wait()
        up = nt(sv[i], wv[1])
        sg = jax.nn.sigmoid(gate)
        act = gate * sg
        hid[i] = (act * up).astype(BF16)
        at = slice(i * rows, (i + 1) * rows)
        write(hid.at[i], outs[0].at[at])
        copies[5 if i else 2].wait()
        if i == 0:
            for copy in parts[2]:
                copy.wait()
        hb = nt(gv[i], wv[2])
        gate_back = (hb * up * sg * (1.0 + gate * (1.0 - sg))).astype(BF16)
        up_back = (hb * act).astype(BF16)
        gback[i] = gate_back
        write(gback.at[i], outs[1].at[at])
        uback[i] = up_back
        write(uback.at[i], outs[2].at[at])
        sback[i] = (nn(gate_back, wv[0]) + nn(up_back, wv[1])).astype(BF16)
        write(sback.at[i], outs[3 + i])
    for copy in writes:
        copy.wait()


def any_call(kernel, name, shapes, me, args, estimate, scratch):
    return pl.pallas_call(
        kernel,
        grid_spec=pltpu.PrefetchScalarGridSpec(
            num_scalar_prefetch=1,
            grid=(1,),
            in_specs=[ANY] * len(args),
            out_specs=[ANY] * len(shapes),
            scratch_shapes=scratch,
        ),
        out_shape=[jax.ShapeDtypeStruct(s, t) for s, t in shapes],
        compiler_params=PARAMS,
        cost_estimate=estimate,
        name=name,
    )(me, *args)


def mlp(where, sa, sb, ga, gb, pieces):
    rows, d = ga.shape
    units = pieces[0][0].shape[0]
    part = ((2 * rows, units), BF16)
    return any_call(
        functools.partial(mlp_kernel, len(pieces[0])),
        "mlp",
        [part] * 3 + [((rows, d), BF16)] * 2,
        where.reshape(1),
        [*sa, *sb, ga, gb] + [one for some in pieces for one in some],
        cost(2 * 5 * 2 * rows * d * units, 12e6, 2 * rows * units),
        [pltpu.VMEM((2, rows, d), BF16)] * 2
        + [pltpu.VMEM((3, units, d), BF16)]
        + [pltpu.VMEM((2, rows, units), BF16)] * 3
        + [pltpu.VMEM((2, rows, d), BF16), pltpu.SemaphoreType.DMA((39,))],
    )


def mlp_out_kernel(count, me, hn, hf, *refs):
    pieces, outs, w = refs[:count], refs[count : count + 4], refs[-1]
    units, d = w.shape
    rows = outs[0].shape[0]
    if count == 1:
        w[...] = pieces[0][...]
    else:
        share = d // 8
        for k in range(4):
            for piece, flip in ((pieces[k], 2 * k), (pieces[4].at[k * units : (k + 1) * units], 2 * k + 1)):
                w[:, pl.ds(pl.multiple_of((me[0] ^ flip) * share, share), share)] = piece[...]
    for h, pair in ((hn, outs[:2]), (hf, outs[2:])):
        for i, out in enumerate(pair):
            out[...] = nn(h[i * rows : (i + 1) * rows], w[...]).astype(BF16)


def unit_grad_kernel(count, me, *refs):
    ins, outs, acc = refs[: -1 - 2 * count], refs[-1 - 2 * count : -1], refs[-1]
    blocks = [block[...] for block in ins[2 * count :]]
    y = me[0] % 2
    near = jnp.concatenate(blocks[: len(blocks) // 2], axis=0)
    far = jnp.concatenate(blocks[len(blocks) // 2 :], axis=0)
    share = outs[0].shape[2]
    for i in range(count):
        acc[...] = tn(ins[2 * i][...], near) + tn(ins[2 * i + 1][...], far)
        for z in range(outs[0].shape[0]):
            for j in range(2):
                at = pl.multiple_of((2 * z + (y ^ j)) * share, share)
                outs[2 * i + j][z] = acc[:, pl.ds(at, share)].astype(BF16)


def unit_grads(pairs, blocks):
    n = lax.axis_size("fsdp")
    units, d = pairs[0][0].shape[1], blocks[0].shape[1]
    if n != 8:
        half = len(blocks) // 2
        near, far = jnp.concatenate(blocks[:half]), jnp.concatenate(blocks[half:])
        outs = [(tn(a, near) + tn(b, far)).astype(BF16) for a, b in pairs]
        return [(jnp.transpose(o.reshape(units, n, d // n), (1, 0, 2)),) for o in outs]
    me = lax.axis_index("fsdp").astype(jnp.int32).reshape(1)
    outs = vmem_call(
        functools.partial(unit_grad_kernel, len(pairs)),
        "unit_grads",
        [((n // 2, units, d // n), BF16)] * (2 * len(pairs)),
        me,
        [a for pair in pairs for a in pair] + list(blocks),
        cost(1, 1),
        [pltpu.VMEM((units, d), F32)],
    )
    return [outs[2 * i : 2 * i + 2] for i in range(len(pairs))]


def out_grad_kernel(me, m0, m1, m2, m3, beside, low, low_beside, gain, mine, other, acc):
    s, y = me[0], me[1] % 2
    width = m0.shape[1]
    half = acc.shape[0]
    low_here = low[:, pl.ds(pl.multiple_of((s % 2) * half, half), half)]
    for r, m in enumerate((m0, m1, m2, m3)):
        cols = pl.ds(pl.multiple_of((s ^ r) * width, width), width)
        theirs = beside[:, (r ^ 1) * width : ((r ^ 1) + 1) * width]
        acc[:, cols] = tn(low_here, m[...]) + tn(low_beside[...], theirs)
    share = mine.shape[2]
    for j, out in enumerate((mine, other)):
        for z in range(out.shape[0]):
            cols = pl.ds(pl.multiple_of((2 * z + (y ^ j)) * share, share), share)
            out[z, :half] = acc[:, cols].astype(BF16)
            out[z, half:] = gain[:, cols].astype(BF16)


def qkv_grad_kernel(me, normed, da, db, w, mine, other, acc):
    y = me[1] % 2
    share = mine.shape[2]
    pair = da.shape[1] // 3
    total = jnp.zeros((1, acc.shape[1]), F32)
    for part, dd in enumerate((da, db)):
        acc[3 * part * pair : 3 * (part + 1) * pair] = tn(dd[...], normed[...])
        for i in range(3):
            one = acc[(3 * part + i) * pair : (3 * part + i + 1) * pair]
            rows = w[(2 * i + part) * pair : (2 * i + part + 1) * pair].astype(F32)
            total = total + jnp.sum(one * rows, axis=0, keepdims=True)
    total = total / w[6 * pair : 6 * pair + 1].astype(F32)
    for j, out in enumerate((mine, other)):
        for z in range(mine.shape[0]):
            cols = pl.ds(pl.multiple_of((2 * z + (y ^ j)) * share, share), share)
            out[z, : 6 * pair] = acc[:, cols].astype(BF16)
    for f in range(acc.shape[1] // share):
        row = jnp.broadcast_to(total[:, f * share : (f + 1) * share], (8, share)).astype(BF16)
        for j, out in enumerate((mine, other)):

            @pl.when((f % 2) == (y ^ j))
            def _():
                out[f // 2, 6 * pair :] = row


def joined(r, da, db):
    pair = da.shape[2] // 3
    parts = [d[r, :, j * pair : (j + 1) * pair] for j in range(3) for d in (da, db)]
    return jnp.concatenate(parts, axis=1)


def normed_back_kernel(me, da, db, w, n3, n2, n1):
    for r, out in ((3, n3), (2, n2), (1, n1)):
        out[...] = nn(joined(r, da, db), w[: 2 * da.shape[2]]).astype(BF16)


def place_values_kernel(me, v, out):
    width = v.shape[2]
    for j in range(GROUPS):
        out[:, j * width : (j + 1) * width] = v[j].astype(F32)


def place_qkv_kernel(me, p0, p1, p2, p3, oq, ok, ov, gain):
    s = me[0]
    size = (p0.shape[0] - 8) // 6
    share = p0.shape[1]
    total = jnp.zeros((8, share), F32)
    for r, piece in enumerate((p0, p1, p2, p3)):
        for p in range(2):
            start = p * 3 * size
            at = pl.multiple_of((s ^ r) * 2 * size + p * size, size)
            for i, out in enumerate((oq, ok, ov)):
                block = piece[start + i * size : start + (i + 1) * size]
                out[:, pl.ds(at, size)] = jnp.transpose(block.astype(F32))
        total = total + piece[6 * size :].astype(F32)
    gain[...] = total[:1]


def place_units_kernel(me, p0, p1, p2, p3, *refs):
    outs, buf = refs[:-1], refs[-1]
    s = me[0]
    units = p0.shape[0] // len(outs)
    for r, p in enumerate((p0, p1, p2, p3)):
        buf[s ^ r] = p[...].astype(F32)
    for i, out in enumerate(outs):
        for j in range(GROUPS):
            out[:, j * units : (j + 1) * units] = jnp.transpose(buf[j, i * units : (i + 1) * units])


def place_out_kernel(me, own, other, out, gain):
    core = me[0] % 2
    half = own.shape[0] - 8
    for j, piece in enumerate((own, other)):
        at = pl.multiple_of((core ^ j) * half, half)
        out[:, pl.ds(at, half)] = jnp.transpose(piece[:half].astype(F32))
    gain[...] = own[half : half + 1].astype(F32) + other[half : half + 1].astype(F32)


def middle_kernel(me, p0, p1, p2, middle, g, gains, w0, x0, x1, x2, x3, mback, mlow, mhalf, b0, b1, b2, b3, ggrad):
    s = me[0]
    width = b0.shape[1]
    dn = p0[...].astype(F32) + p1[...].astype(F32) + p2[...].astype(F32)
    v = middle[...]
    r = inverse_rms(v)
    x = v * r
    ggrad[...] = jnp.broadcast_to(jnp.sum(dn * x, axis=0, keepdims=True), ggrad.shape)
    dx = dn * gains[1:2].astype(F32)
    total = g[...].astype(F32) + r * (dx - x * jnp.mean(dx * x, axis=-1, keepdims=True))
    mback[...] = total
    mlow[...] = total.astype(BF16)
    half = 4 * x0.shape[0]
    lows = [mlow[:, pl.ds(pl.multiple_of(((s % 2) ^ j) * half, half), half)] for j in range(2)]
    mhalf[...] = lows[1]
    for i, b in enumerate((b0, b1, b2, b3)):
        cols = pl.ds(pl.multiple_of((s ^ i) * width, width), width)
        w1 = jnp.concatenate([x[:, cols] for x in (x0, x1, x2, x3)], axis=0)
        b[...] = (nn(lows[0], w0[w0.shape[0] - half :, cols]) + nn(lows[1], w1)).astype(BF16)


def final_kernel(me, p1, p2, da, db, w, t, gains, mback, out):
    dn = nn(joined(0, da, db), w[: 2 * da.shape[2]])
    dn = dn + p1[...].astype(F32) + p2[...].astype(F32)
    v = t[...].astype(F32)
    r = inverse_rms(v)
    x = v * r
    dx = dn * gains[:1].astype(F32)
    out[...] = mback[...] + r * (dx - x * jnp.mean(dx * x, axis=-1, keepdims=True))


def after(value, *others):
    return lax.optimization_barrier((value,) + others)[0]


def all_after(values, *others):
    return list(lax.optimization_barrier(tuple(values) + others)[: len(values)])


def add(*terms):
    return sum((term.astype(F32) for term in terms[1:]), terms[0].astype(F32)).astype(BF16)


def seq_permute(value, flip):
    return lax.ppermute(value, "seq", [(i, i ^ flip) for i in range(GROUPS)])


def gather_four(own):
    near = seq_permute(own, 1)
    far = seq_permute(own, 2)
    return own, near, far, seq_permute(far, 1)


def exchange_four(pieces):
    return [pieces[0]] + [seq_permute(pieces[r], r) for r in (1, 2, 3)]


def fsdp_permute(value, flip):
    n = lax.axis_size("fsdp")
    return lax.ppermute(value, "fsdp", [(i, i ^ flip) for i in range(n)])


def fsdp_send(both):
    z = lax.axis_index("fsdp") // 2
    parts = [lax.dynamic_index_in_dim(both, z ^ k, 0, keepdims=False) for k in range(both.shape[0])]
    return [parts[0]] + [fsdp_permute(parts[k], 2 * k) for k in range(1, len(parts))]


def scatter_whole(parts):
    return lax.psum_scatter(parts, "fsdp", scatter_dimension=0, tiled=False)


def per_device(
    tokens,
    first_values,
    cotangent,
    first_gain,
    query_weight,
    key_weight,
    value_weight,
    out_weight,
    second_gain,
    gate_weight,
    up_weight,
    down_weight,
):
    n = lax.axis_size("fsdp")
    s = lax.axis_index("seq").astype(jnp.int32)
    me = s.reshape(1)
    place3 = [jnp.stack([s, lax.axis_index("fsdp").astype(jnp.int32), jnp.int32(p)]) for p in (0, 1)]
    t0, g0, f0 = tokens[0], cotangent[0], first_values[0]
    rows, d = t0.shape
    width = d // GROUPS
    pair = width // 2
    units = gate_weight.shape[1] // GROUPS
    share = d // n
    core = s % 2
    ring = n == 8

    def columns(v, which, size):
        return lax.dynamic_slice_in_dim(v, which * size, size, 1)

    here = lax.axis_index("fsdp").astype(jnp.int32)
    gains = jnp.concatenate([first_gain[None], second_gain[None], jnp.zeros((6, share), BF16)])
    qkv_weights = (query_weight, key_weight, value_weight)
    own_qkv = [columns(w, s, width).T for w in qkv_weights]
    own_qkv += [gains, columns(out_weight, core, d // 2).T]
    own_qkv = jnp.concatenate(own_qkv, axis=0)
    own_units = [columns(w, s, units).T for w in (gate_weight, up_weight, down_weight)]
    places = (jnp.arange(4, dtype=jnp.int32) ^ s)[:, None] * rows + jnp.arange(rows, dtype=jnp.int32)
    half_dim = HEAD_DIM // 2
    freqs = jnp.exp(jnp.arange(half_dim, dtype=F32) * (-2.0 * math.log(10000.0) / HEAD_DIM))
    angles = places.astype(F32)[:, :, None] * jnp.tile(freqs, 4)
    sign = jnp.tile(jnp.repeat(jnp.array([-1.0, 1.0], F32), half_dim), 2)
    cosine, sine = jnp.cos(angles), jnp.sin(angles) * sign
    f = [columns(f0, s ^ r, width) for r in range(4)]
    if ring:
        first = [fsdp_permute(own_qkv, flip) for flip in (6, 4, 2)][::-1]
        first_y = fsdp_permute(own_qkv, 1)
    packed2 = seq_permute(jnp.concatenate([t0, f[2], f[3]], axis=1), 2)
    if ring:
        pieces = [own_qkv, first_y]
        for i in range(3):
            one = after(first[i], cosine, sine) if i == 0 else first[i]
            pieces += [one, fsdp_permute(one, 1)]
    else:
        pieces = [lax.all_gather(own_qkv, "fsdp", axis=1, tiled=True)]
        unit_pieces = [[lax.all_gather(w, "fsdp", axis=1, tiled=True)] for w in own_units]
    where = here if ring else jnp.int32(0)
    packed1 = seq_permute(jnp.concatenate([t0, f[1]], axis=1), 1)
    crossing = jnp.concatenate([packed2[:, :d], packed2[:, d + width :]], axis=1)
    if ring:
        def pair_send(own, *waits):
            own = after(own, *waits)
            return [own] + [fsdp_permute(own, flip) for flip in (2, 4, 6)]

        gate_w = pair_send(own_units[0], *first, pieces[1], pieces[3])
        crossing = after(crossing, *pieces[1::2], *gate_w)
    packed3 = seq_permute(crossing, 1)

    if ring:
        gate_w.append(fsdp_permute(jnp.concatenate(gate_w, axis=0), 1))
        up_w = pair_send(own_units[1], gate_w[1])
    g2 = seq_permute(after(g0, packed2, *pieces[1::2]), 2)

    q, k, v, normed, w_qkv = qkv(where, t0, f[0], (packed1, packed2, packed3), pieces, cosine, sine)
    gains = w_qkv[3 * width : 3 * width + 8]
    w_out_sent = w_qkv[3 * width + 8 :]
    *m, lse_a = attention(0, me, q, k, v)
    g2 = after(g2, m[0])
    q = after(q, g2)
    g1, g3 = seq_permute(after(g0, g2), 1), seq_permute(g2, 1)
    if ring:
        up_w[1:] = all_after(up_w[1:], m[0])
        gate_w[4] = after(gate_w[4], m[0])
        up_w.append(fsdp_permute(jnp.concatenate(up_w, axis=0), 1))
        down_w = pair_send(own_units[2], *up_w[:4])
        q = after(q, gate_w[4])
    *m, lse_b = attention(1, me, q, k, v, *m)
    if ring:
        up_w[4] = after(up_w[4], m[0])
        down_w[1:] = all_after(down_w[1:], m[0])
        down_w.append(fsdp_permute(jnp.concatenate(down_w, axis=0), 1))
        m = all_after(m, up_w[4])
    m = exchange_four(m)
    if ring:
        m = all_after(m, *down_w[:4])
    w_out_sent = after(w_out_sent, m[2], m[3])
    w_out_other = [
        seq_permute(lax.slice_in_dim(w_out_sent, i * (d // 8), (i + 1) * (d // 8)), 1) for i in range(4)
    ]
    if ring:
        unit_pieces = [gate_w, up_w, down_w]
    m = all_after(m, *w_out_other)
    middle, *s0 = vmem_call(
        out_kernel,
        "out",
        [((rows, d), F32)] + [((rows // 2, d), BF16)] * 2,
        me,
        [*m, w_qkv, *w_out_other, t0, gains],
        cost(2 * rows * d * d, 8e6),
    )
    s1 = [seq_permute(one, 1) for one in s0]
    s2 = [seq_permute(one, 2) for one in s0]
    hid_near, gate_near, up_near, sb0, sb1 = mlp(where, s0, s1, g0, g1, unit_pieces)
    s2 = all_after(s2, sb0)
    s3 = [seq_permute(one, 1) for one in s2]
    hid_far, gate_far, up_far, sb2, sb3 = mlp(where, s2, s3, g2, g3, unit_pieces)
    sb_both = add(sb2, seq_permute(sb3, 1))
    p = [sb0, seq_permute(after(sb1, sb_both), 1), seq_permute(sb_both, 2)]

    (down_part,) = unit_grads([(hid_near, after(hid_far, p[1]))], (g0, g1, g2, g3))
    if ring:
        down_crossed = fsdp_permute(down_part[1], 1)
    o = vmem_call(
        functools.partial(mlp_out_kernel, len(unit_pieces[2])),
        "mlp_out",
        [((rows, d), BF16)] * 4,
        where.reshape(1),
        [hid_near, after(hid_far, down_part[0]), *unit_pieces[2]],
        cost(2 * 4 * rows * d * units, 8e6),
        [pltpu.VMEM((units, d), BF16)],
    )
    (gate_part,) = unit_grads([(gate_near, after(gate_far, o[0]))], (*s0, *s1, *s2, *s3))
    o1, o3 = all_after([seq_permute(o[1], 1), seq_permute(o[3], 1)], gate_part[0])
    p[2] = after(p[2], gate_part[0])
    p[0] = after(p[0], o3, o1)
    if ring:
        down_both = add(down_part[0], after(down_crossed, p[2]))
        p[2] = after(p[2], down_both)
        gate_crossed = fsdp_permute(after(gate_part[1], down_both), 1)
        mixed_beside = seq_permute(jnp.concatenate(m, axis=1), 1)
        p[0] = after(p[0], mixed_beside)
    mback, mlow, mhalf, b0, b1, b2, b3, ggrad_second = vmem_call(
        middle_kernel,
        "middle",
        [((rows, d), F32), ((rows, d), BF16), ((rows, d // 2), BF16)]
        + [((rows, width), BF16)] * 4
        + [((8, d), F32)],
        me,
        [*p, middle, g0, gains, w_qkv, *w_out_other],
        cost(2 * rows * d * d, 12e6),
    )
    b = exchange_four([b0, b1, b2, b3])
    o_both = add(o[2], after(o3, mlow))
    flat = lambda x: x.reshape(4 * rows, -1)
    qb = q
    if ring:
        low_beside = seq_permute(mhalf, 1)
        out_part = vmem_call(
            out_grad_kernel,
            "out_grad",
            [((n // 2, d // 2 + 8, share), BF16)] * 2,
            place3[0],
            [*m, mixed_beside, mlow, low_beside, ggrad_second],
            cost(2 * rows * d * d, 6e6),
            [pltpu.VMEM((d // 2, d), F32)],
        )
        (up_part,) = unit_grads([(up_near, after(up_far, out_part[0]))], (*s0, *s1, *s2, *s3))
        b[1:] = all_after(b[1:], up_part[0], o_both)
        down_sent = fsdp_send(after(down_both, b[2], b[3]))
    else:
        (up_part,) = unit_grads([(up_near, up_far)], (*s0, *s1, *s2, *s3))

    def qkv_grads(d_a, d_b):
        if ring:
            return vmem_call(
                qkv_grad_kernel,
                "qkv_grad",
                [((n // 2, 6 * pair + 8, share), BF16)] * 2,
                place3[0],
                [flat(normed), flat(d_a), flat(d_b), w_qkv],
                cost(2 * 4 * rows * d * 6 * pair, 6e6),
                [pltpu.VMEM((6 * pair, d), F32)],
            )
        whole = tn(jnp.concatenate([flat(d_a), flat(d_b)], axis=1), flat(normed))
        starts = [i * width + part * pair for part in range(2) for i in range(3)]
        w = jnp.concatenate([w_qkv[i : i + pair] for i in starts]).astype(F32)
        gain_part = jnp.sum(whole * w, axis=0, keepdims=True) / gains[:1].astype(F32)
        whole = jnp.concatenate([whole, gain_part, jnp.zeros((7, d), F32)]).astype(BF16)
        return (jnp.transpose(whole.reshape(6 * pair + 8, n, share), (1, 0, 2)),)

    d_a, v_a = attention_back(0, me, qb, k, v, b, lse_a, cosine, sine)
    o2 = seq_permute(after(o_both, d_a), 2)
    qb = after(qb, d_a)
    if ring:
        gate_both = add(gate_part[0], after(gate_crossed, d_a))
        down_share = add(*all_after(down_sent, d_a))
        gate_sent = fsdp_send(after(gate_both, down_share))
        up_crossed = fsdp_permute(after(up_part[1], gate_both), 1)
        qb = after(qb, gate_both, down_share)
    d_b, v_b = attention_back(1, me, qb, k, v, b, lse_b, cosine, sine, v_a)
    o2 = after(o2, d_b)
    d_b = after(d_b, o2)
    if ring:
        up_crossed, *gate_sent = all_after([up_crossed] + gate_sent, d_b)
        up_both = add(up_part[0], up_crossed)
        gate_share = add(*gate_sent)
        up_sent = fsdp_send(after(up_both, gate_share))
        out_crossed = fsdp_permute(after(out_part[1], up_both), 1)
        d_b = after(d_b, up_both, gate_share)

    nb3, nb2, nb1 = vmem_call(
        normed_back_kernel,
        "normed_back",
        [((rows, d), BF16)] * 3,
        me,
        [d_a, d_b, w_qkv],
        cost(2 * 3 * rows * d * 3 * width, 8e6),
    )
    nb_both = add(nb2, seq_permute(nb3, 1))
    beside = seq_permute(nb1, 1)
    crossed_far = seq_permute(nb_both, 2)
    qkv_sums = qkv_grads(d_a, after(d_b, nb_both, beside))
    crossed_far = after(crossed_far, qkv_sums[0])
    if ring:
        out_both = add(out_part[0], after(out_crossed, qkv_sums[0]))
        qkv_crossed = fsdp_permute(after(qkv_sums[1], out_both), 1)
        up_share = add(*all_after(up_sent, qkv_sums[0]))
        out_sent = fsdp_send(after(out_both, up_share))
        beside = after(beside, up_share)
        units_sent = jnp.concatenate([gate_share, up_share, down_share], axis=0)
        units_far = seq_permute(units_sent, 2)
    (tokens_grad,) = vmem_call(
        final_kernel,
        "final",
        [((rows, d), F32)],
        me,
        [beside, crossed_far, d_a, d_b, w_qkv, t0, gains, mback],
        cost(0, 6e6),
    )
    if ring:
        units_far = after(units_far, tokens_grad)
        qkv_both = add(qkv_sums[0], after(qkv_crossed, tokens_grad))
        out_share = add(*all_after(out_sent, tokens_grad))
        qkv_sent = fsdp_send(after(qkv_both, out_share))
    else:
        gate_share, up_share, down_share, qkv_share = (
            scatter_whole(v[0]) for v in (gate_part, up_part, down_part, qkv_sums)
        )
        mixed_rows = jnp.zeros((rows, d), BF16)
        for r in range(4):
            mixed_rows = lax.dynamic_update_slice(mixed_rows, m[r], (0, (s ^ r) * width))
        out_part = tn(mlow, mixed_rows)
        halves = [lax.dynamic_slice_in_dim(out_part, (core ^ j) * (d // 2), d // 2) for j in range(2)]
        keep = jnp.concatenate([halves[0], ggrad_second]).reshape(d // 2 + 8, n, share)
        send = jnp.pad(halves[1], ((0, 8), (0, 0))).astype(BF16).reshape(d // 2 + 8, n, share)
        whole = (keep + seq_permute(send, 1).astype(F32)).astype(BF16)
        out_share = scatter_whole(jnp.transpose(whole, (1, 0, 2)))
        units_sent = jnp.concatenate([gate_share, up_share, down_share], axis=0)
    v_all = lax.all_to_all(after(v_b, tokens_grad), "seq", split_axis=0, concat_axis=0)
    output = add(middle, o[0], o1, o2)[None]
    (values_grad,) = vmem_call(
        place_values_kernel, "place_values", [((rows, d), F32)], me, [v_all], cost(0, 3e6)
    )
    if not ring:
        units_far = seq_permute(units_sent, 2)
    gate_grad, up_grad, down_grad = vmem_call(
        place_units_kernel,
        "place_units",
        [((share, 4 * units), F32)] * 3,
        me,
        [units_sent, seq_permute(units_sent, 1), units_far, seq_permute(units_far, 1)],
        cost(0, 3e6),
        [pltpu.VMEM((4, 3 * units, share), F32)],
    )
    if ring:
        out_far = after(seq_permute(after(out_share, qkv_both), 2), gate_grad)
    else:
        out_far = seq_permute(out_share, 2)
    out_share = add(out_share, out_far)
    out_grad, second_gain_grad = vmem_call(
        place_out_kernel,
        "place_out",
        [((share, d), F32), ((1, share), F32)],
        me,
        [out_share, seq_permute(out_share, 1)],
        cost(0, 1e6),
    )
    if ring:
        qkv_share = add(*all_after(qkv_sent, out_grad, values_grad, output, gate_grad))
    qkv_far = seq_permute(qkv_share, 2)
    qkv_all = [qkv_share, seq_permute(qkv_share, 1), qkv_far, seq_permute(qkv_far, 1)]
    query_grad, key_grad, value_grad, gain_grad = vmem_call(
        place_qkv_kernel,
        "place_qkv",
        [((share, d), F32)] * 3 + [((1, share), F32)],
        me,
        qkv_all,
        cost(0, 3e6),
    )
    return (
        output,
        tokens_grad[None],
        values_grad[None],
        gain_grad.reshape(share),
        query_grad,
        key_grad,
        value_grad,
        out_grad,
        second_gain_grad.reshape(share),
        gate_grad,
        up_grad,
        down_grad,
    )


def solution(mesh):
    rows = P("fsdp", "seq", None)
    weight = P("fsdp", None)
    gain = P("fsdp")
    in_specs = (rows,) * 3 + (gain,) + (weight,) * 4 + (gain,) + (weight,) * 3
    out_specs = (rows,) * 3 + (gain,) + (weight,) * 4 + (gain,) + (weight,) * 3
    return jax.shard_map(
        per_device, mesh=mesh, in_specs=in_specs, out_specs=out_specs, check_vma=False
    )
```

```python
import functools
import math

import jax
import jax.numpy as jnp
from jax import lax
from jax.experimental import pallas as pl
from jax.experimental.pallas import tpu as pltpu
from jax.sharding import PartitionSpec as P

HEADS = 16
HEAD_DIM = 64
GROUPS = 4
EPSILON = 1e-06
NEGATIVE = -1e30
F32 = jnp.float32
BF16 = jnp.bfloat16
PARAMS = pltpu.CompilerParams(vmem_limit_bytes=56 * 2**20)


def nn(a, b):
    return lax.dot_general(a, b, (((1,), (0,)), ((), ())), preferred_element_type=F32)


def nt(a, b):
    return lax.dot_general(a, b, (((1,), (1,)), ((), ())), preferred_element_type=F32)


def tn(a, b):
    return lax.dot_general(a, b, (((0,), (0,)), ((), ())), preferred_element_type=F32)


def cost(flops, nbytes, trans=0):
    flops, nbytes, trans = 1, 1, 0
    return pl.CostEstimate(flops=int(flops), bytes_accessed=int(nbytes), transcendentals=int(trans))


def turn(u, cosine, sine):
    lane = lax.broadcasted_iota(jnp.int32, (u.shape[0], 128), 1)
    first = lane % HEAD_DIM < HEAD_DIM // 2
    parts = []
    for j in range(u.shape[1] // 128):
        part = u[:, 128 * j : 128 * (j + 1)]
        other = jnp.where(first, pltpu.roll(part, 96, 1), pltpu.roll(part, 32, 1))
        parts.append(part * cosine + other * sine)
    return jnp.concatenate(parts, axis=1)


def inverse_rms(v):
    return lax.rsqrt(jnp.mean(v * v, axis=-1, keepdims=True) + EPSILON)


ANY = pl.BlockSpec(memory_space=pl.ANY)


def qkv_kernel(count, me, t0, f0, p1, p2, p3, *refs):
    pieces, rest = refs[:count], refs[count:]
    cosine, sine, q, k, v, n, w, wo, tv, fv, sems = rest
    width = q.shape[-1]
    d = tv.shape[-1]
    share = d // count
    first, last = [], []
    for i, piece in enumerate(pieces):
        at = pl.ds(pl.multiple_of((me[0] ^ i) * share, share), share)
        first.append(pltpu.make_async_copy(piece.at[: w.shape[0]], w.at[:, at], sems.at[8 + i]))
        last.append(pltpu.make_async_copy(piece.at[w.shape[0] :], wo.at[:, at], sems.at[16 + i]))
    loads = [(t0, f0)] + [(p.at[:, :d], p.at[:, d : d + width]) for p in (p1, p2, p3)]
    copies = []
    for i, (t, f) in enumerate(loads):
        copies.append(pltpu.make_async_copy(t, tv.at[i], sems.at[2 * i]))
        copies.append(pltpu.make_async_copy(f, fv.at[i], sems.at[2 * i + 1]))
    for copy in copies[:2] + first + copies[2:] + last:
        copy.start()
    for i in range(4):
        copies[2 * i].wait()
        if i == 0:
            for copy in first:
                copy.wait()
        gain = w[3 * width : 3 * width + 1].astype(F32)
        x = tv[i].astype(F32)
        normed = (x * inverse_rms(x) * gain).astype(BF16)
        n[i] = normed
        u = nt(normed, w[: 3 * width])
        c, s = cosine[i], sine[i]
        q[i] = (turn(u[:, :width], c, s).astype(BF16).astype(F32) * 0.125).astype(BF16)
        k[i] = turn(u[:, width : 2 * width], c, s).astype(BF16)
        copies[2 * i + 1].wait()
        v[i] = (0.5 * u[:, 2 * width :] + 0.5 * fv[i].astype(F32)).astype(BF16)
    for copy in last:
        copy.wait()


def qkv(where, t, f, packed, pieces, cosine, sine):
    rows, d = t.shape
    width = f.shape[1]
    full = lambda *shape: pl.BlockSpec(shape, lambda i, me: (0,) * len(shape))
    main = 3 * width + 8
    shapes = [(4, rows, width)] * 3 + [(4, rows, d), (main, d), (pieces[0].shape[0] - main, d)]
    return pl.pallas_call(
        functools.partial(qkv_kernel, len(pieces)),
        grid_spec=pltpu.PrefetchScalarGridSpec(
            num_scalar_prefetch=1,
            grid=(1,),
            in_specs=[ANY] * (5 + len(pieces)) + [full(4, rows, 128)] * 2,
            out_specs=[full(*s) for s in shapes],
            scratch_shapes=[
                pltpu.VMEM((4, rows, d), BF16),
                pltpu.VMEM((4, rows, width), BF16),
                pltpu.SemaphoreType.DMA((24,)),
            ],
        ),
        out_shape=[jax.ShapeDtypeStruct(s, BF16) for s in shapes],
        compiler_params=PARAMS,
        cost_estimate=cost(2 * 4 * rows * d * 3 * width, 12e6),
        name="qkv",
    )(where.reshape(1), t, f, *packed, *pieces, cosine, sine)


def attn_kernel(me, q, k, v, *refs):
    before, (o0, o1, o2, o3, lse, o) = refs[:-6], refs[-6:]
    h = pl.program_id(0)
    rows, width = q.shape[1:]
    mine = lax.broadcasted_iota(jnp.int32, (1, width), 1) // HEAD_DIM == h
    row = lax.broadcasted_iota(jnp.int32, (rows, rows), 0)
    col = lax.broadcasted_iota(jnp.int32, (rows, rows), 1)
    s = me[0]
    for i in range(GROUPS):
        ri = i ^ s
        qi = jnp.where(mine, q[ri], jnp.zeros((), BF16))
        tiles = []
        for j in range(i + 1):
            tile = nt(qi, k[j ^ s])
            if j == i:
                tile = jnp.where(col <= row, tile, NEGATIVE)
            tiles.append(tile)
        largest = tiles[0].max(axis=1, keepdims=True)
        for tile in tiles[1:]:
            largest = jnp.maximum(largest, tile.max(axis=1, keepdims=True))
        tiles = [jnp.exp(tile - largest) for tile in tiles]
        total = tiles[0].sum(axis=1, keepdims=True)
        for tile in tiles[1:]:
            total = total + tile.sum(axis=1, keepdims=True)
        inverse = 1.0 / total
        acc = jnp.zeros((rows, width), F32)
        for j in range(i + 1):
            acc = acc + nn((tiles[j] * inverse).astype(BF16), v[j ^ s])
        o[ri] = jnp.where(mine, acc.astype(BF16), o[ri])
        stat = jnp.broadcast_to(largest + jnp.log(total), (rows, 128))
        lse[0, i] = jnp.transpose(stat)[:8]

    @pl.when(h == pl.num_programs(0) - 1)
    def _():
        for r, out in enumerate((o0, o1, o2, o3)):
            if before:
                out[:, :width] = before[r][...]
                out[:, width:] = o[r]
            else:
                out[...] = o[r]


def attention(part, me, q, k, v, *before):
    rows = q.shape[1]
    width = 2 * HEAD_DIM
    full = lambda *shape: pl.BlockSpec(shape, lambda h, me: (0,) * len(shape))
    pair = pl.BlockSpec((4, rows, width), lambda h, me: (0, 0, part))
    both = (rows, 2 * width if before else width)
    return pl.pallas_call(
        attn_kernel,
        grid_spec=pltpu.PrefetchScalarGridSpec(
            num_scalar_prefetch=1,
            grid=(2,),
            in_specs=[pair] * 3 + [full(*one.shape) for one in before],
            out_specs=[full(*both)] * 4
            + [pl.BlockSpec((1, 4, 8, rows), lambda h, me: (h, 0, 0, 0))],
            scratch_shapes=[pltpu.VMEM((4, rows, width), BF16)],
        ),
        out_shape=[jax.ShapeDtypeStruct(both, BF16)] * 4
        + [jax.ShapeDtypeStruct((2, 4, 8, rows), F32)],
        compiler_params=PARAMS,
        cost_estimate=cost(2 * 2 * 10 * rows * rows * width * 4, 4e6, 20 * rows * rows),
        name="attention",
    )(me, q, k, v, *before)


def attn_back_kernel(me, q, k, v, b0, b1, b2, b3, lse, cosine, sine, *rest):
    before, (out, vout, do, dq, dk, dv) = rest[:-6], rest[-6:]
    h = pl.program_id(0)
    rows, width = q.shape[1:]
    mine = lax.broadcasted_iota(jnp.int32, (1, width), 1) // HEAD_DIM == h
    key = lax.broadcasted_iota(jnp.int32, (rows, rows), 0)
    query = lax.broadcasted_iota(jnp.int32, (rows, rows), 1)
    s = me[0]
    zero = jnp.zeros((), BF16)

    @pl.when(h == 0)
    def _():
        for r, b in enumerate((b0, b1, b2, b3)):
            do[r] = b[...]
        dq[...] = jnp.zeros_like(dq)
        dk[...] = jnp.zeros_like(dk)
        dv[...] = jnp.zeros_like(dv)

    for i in range(GROUPS):
        qi = jnp.where(mine, q[i ^ s], zero)
        doi = jnp.where(mine, do[i ^ s], zero)
        stat = lse[0, i][:1]
        soft, back = [], []
        dot = jnp.zeros((1, rows), F32)
        for j in range(i + 1):
            tile = nt(k[j ^ s], qi)
            if j == i:
                tile = jnp.where(key <= query, tile, NEGATIVE)
            p = jnp.exp(tile - stat)
            dp = nt(v[j ^ s], doi)
            dot = dot + jnp.sum(p * dp, axis=0, keepdims=True)
            soft.append(p)
            back.append(dp)
        acc = jnp.zeros((rows, width), F32)
        for j in range(i + 1):
            ds = (soft[j] * (back[j] - dot)).astype(BF16)
            dk[j] += nn(ds, qi)
            dv[j] += nn(soft[j].astype(BF16), doi)
            acc = acc + tn(ds, jnp.where(mine, k[j ^ s], zero))
        dq[i] += acc

    @pl.when(h == pl.num_programs(0) - 1)
    def _():
        for i in range(GROUPS):
            ri = i ^ s
            c, n = cosine[ri], -sine[ri]
            out[ri, :, :width] = turn(dq[i] * 0.125, c, n).astype(BF16)
            out[ri, :, width : 2 * width] = turn(dk[i], c, n).astype(BF16)
            half = (0.5 * dv[i]).astype(BF16)
            out[ri, :, 2 * width :] = half
            vout[i, :, len(before) * width :] = half
            if before:
                vout[i, :, :width] = before[0][i]


def attention_back(part, me, q, k, v, b, lse, cosine, sine, *before):
    rows = q.shape[1]
    width = 2 * HEAD_DIM
    full = lambda *shape: pl.BlockSpec(shape, lambda h, me: (0,) * len(shape))
    pair = pl.BlockSpec((4, rows, width), lambda h, me: (0, 0, part))
    return pl.pallas_call(
        attn_back_kernel,
        grid_spec=pltpu.PrefetchScalarGridSpec(
            num_scalar_prefetch=1,
            grid=(2,),
            in_specs=[pair] * 3
            + [pl.BlockSpec((rows, width), lambda h, me: (0, part))] * 4
            + [pl.BlockSpec((1, 4, 8, rows), lambda h, me: (h, 0, 0, 0))]
            + [full(4, rows, 128)] * 2
            + [full(*one.shape) for one in before],
            out_specs=[full(4, rows, 3 * width), full(4, rows, (1 + len(before)) * width)],
            scratch_shapes=[pltpu.VMEM((4, rows, width), BF16)]
            + [pltpu.VMEM((4, rows, width), F32)] * 3,
        ),
        out_shape=[
            jax.ShapeDtypeStruct((4, rows, 3 * width), BF16),
            jax.ShapeDtypeStruct((4, rows, (1 + len(before)) * width), BF16),
        ],
        compiler_params=PARAMS,
        cost_estimate=cost(5 * 2 * 10 * rows * rows * width * 4, 4e6, 20 * rows * rows),
        name="attention_back",
    )(me, q, k, v, *b, lse, cosine, sine, *before)


def out_kernel(me, m0, m1, m2, m3, w0, x0, x1, x2, x3, t, gains, middle, lo, hi):
    s = me[0]
    width = m0.shape[1]
    quarter = x0.shape[0]
    first = w0.shape[0] - 4 * quarter
    ws = [[w0.at[first + i * quarter : first + (i + 1) * quarter] for i in range(4)], [x0, x1, x2, x3]]
    for j in range(2):
        for i, w in enumerate(ws[j]):
            start = ((s % 2) ^ j) * 4 * quarter + i * quarter
            cols = pl.ds(pl.multiple_of(start, quarter), quarter)
            part = None
            for r, m in enumerate((m0, m1, m2, m3)):
                one = nt(m[...], w[:, pl.ds(pl.multiple_of((s ^ r) * width, width), width)])
                part = one if part is None else part + one
            middle[:, cols] = t[:, cols].astype(F32) + part
    acc = middle[...]
    second = (acc * inverse_rms(acc) * gains[1:2].astype(F32)).astype(BF16)
    lo[...] = second[: lo.shape[0]]
    hi[...] = second[lo.shape[0] :]


def vmem_call(kernel, name, shapes, me, args, estimate, scratch=()):
    full = lambda shape: pl.BlockSpec(shape, lambda i, me: (0,) * len(shape))
    outs = [jax.ShapeDtypeStruct(s, t) for s, t in shapes]
    return pl.pallas_call(
        kernel,
        grid_spec=pltpu.PrefetchScalarGridSpec(
            num_scalar_prefetch=1,
            grid=(1,),
            in_specs=[full(a.shape) for a in args],
            out_specs=[full(s) for s, _ in shapes],
            scratch_shapes=scratch,
        ),
        out_shape=outs,
        compiler_params=PARAMS,
        cost_estimate=estimate,
        name=name,
    )(me, *args)


def mlp_kernel(count, me, sa0, sa1, sb0, sb1, ga, gb, *refs):
    pieces, outs = refs[: 3 * count], refs[3 * count : 3 * count + 5]
    sv, gv, wv, hid, gback, uback, sback, sems = refs[3 * count + 5 :]
    _, units, d = wv.shape
    rows = ga.shape[0]
    copies = [pltpu.make_async_copy(sa0, sv.at[0, : rows // 2], sems.at[0])]
    copies.append(pltpu.make_async_copy(sa1, sv.at[0, rows // 2 :], sems.at[1]))
    parts = []
    for h in range(3):
        loads = []
        if count == 1:
            loads.append((pieces[h], wv.at[h]))
        else:
            share = d // 8
            for k in range(4):
                mine, other = pieces[h * count + k], pieces[h * count + 4].at[k * units : (k + 1) * units]
                for piece, flip in ((mine, 2 * k), (other, 2 * k + 1)):
                    at = pl.ds(pl.multiple_of((me[0] ^ flip) * share, share), share)
                    loads.append((piece, wv.at[h, :, at]))
        sem = lambda i, h=h: sems.at[15 + 8 * h + i]
        parts.append([pltpu.make_async_copy(a, b, sem(i)) for i, (a, b) in enumerate(loads)])
    copies.append(pltpu.make_async_copy(ga, gv.at[0], sems.at[4]))
    copies.append(pltpu.make_async_copy(sb0, sv.at[1, : rows // 2], sems.at[2]))
    copies.append(pltpu.make_async_copy(sb1, sv.at[1, rows // 2 :], sems.at[5]))
    copies.append(pltpu.make_async_copy(gb, gv.at[1], sems.at[6]))
    for copy in copies[:2] + parts[0] + parts[1] + copies[2:3] + parts[2] + copies[3:]:
        copy.start()
    writes = []

    def write(buf, out):
        copy = pltpu.make_async_copy(buf, out, sems.at[7 + len(writes)])
        copy.start()
        writes.append(copy)

    for i in range(2):
        copies[3 if i else 0].wait()
        copies[4 if i else 1].wait()
        if i == 0:
            for copy in parts[0]:
                copy.wait()
        gate = nt(sv[i], wv[0])
        if i == 0:
            for copy in parts[1]:
                copy.wait()
        up = nt(sv[i], wv[1])
        sg = jax.nn.sigmoid(gate)
        act = gate * sg
        hid[i] = (act * up).astype(BF16)
        at = slice(i * rows, (i + 1) * rows)
        write(hid.at[i], outs[0].at[at])
        copies[5 if i else 2].wait()
        if i == 0:
            for copy in parts[2]:
                copy.wait()
        hb = nt(gv[i], wv[2])
        gate_back = (hb * up * sg * (1.0 + gate * (1.0 - sg))).astype(BF16)
        up_back = (hb * act).astype(BF16)
        gback[i] = gate_back
        write(gback.at[i], outs[1].at[at])
        uback[i] = up_back
        write(uback.at[i], outs[2].at[at])
        sback[i] = (nn(gate_back, wv[0]) + nn(up_back, wv[1])).astype(BF16)
        write(sback.at[i], outs[3 + i])
    for copy in writes:
        copy.wait()


def any_call(kernel, name, shapes, me, args, estimate, scratch):
    return pl.pallas_call(
        kernel,
        grid_spec=pltpu.PrefetchScalarGridSpec(
            num_scalar_prefetch=1,
            grid=(1,),
            in_specs=[ANY] * len(args),
            out_specs=[ANY] * len(shapes),
            scratch_shapes=scratch,
        ),
        out_shape=[jax.ShapeDtypeStruct(s, t) for s, t in shapes],
        compiler_params=PARAMS,
        cost_estimate=estimate,
        name=name,
    )(me, *args)


def mlp(where, sa, sb, ga, gb, pieces):
    rows, d = ga.shape
    units = pieces[0][0].shape[0]
    part = ((2 * rows, units), BF16)
    return any_call(
        functools.partial(mlp_kernel, len(pieces[0])),
        "mlp",
        [part] * 3 + [((rows, d), BF16)] * 2,
        where.reshape(1),
        [*sa, *sb, ga, gb] + [one for some in pieces for one in some],
        cost(2 * 5 * 2 * rows * d * units, 12e6, 2 * rows * units),
        [pltpu.VMEM((2, rows, d), BF16)] * 2
        + [pltpu.VMEM((3, units, d), BF16)]
        + [pltpu.VMEM((2, rows, units), BF16)] * 3
        + [pltpu.VMEM((2, rows, d), BF16), pltpu.SemaphoreType.DMA((39,))],
    )


def mlp_out_kernel(count, me, hn, hf, *refs):
    pieces, outs, w = refs[:count], refs[count : count + 4], refs[-1]
    units, d = w.shape
    rows = outs[0].shape[0]
    if count == 1:
        w[...] = pieces[0][...]
    else:
        share = d // 8
        for k in range(4):
            for piece, flip in ((pieces[k], 2 * k), (pieces[4].at[k * units : (k + 1) * units], 2 * k + 1)):
                w[:, pl.ds(pl.multiple_of((me[0] ^ flip) * share, share), share)] = piece[...]
    for h, pair in ((hn, outs[:2]), (hf, outs[2:])):
        for i, out in enumerate(pair):
            out[...] = nn(h[i * rows : (i + 1) * rows], w[...]).astype(BF16)


def unit_grad_kernel(count, me, *refs):
    ins, outs, acc = refs[: -1 - 2 * count], refs[-1 - 2 * count : -1], refs[-1]
    blocks = [block[...] for block in ins[2 * count :]]
    y = me[0] % 2
    near = jnp.concatenate(blocks[: len(blocks) // 2], axis=0)
    far = jnp.concatenate(blocks[len(blocks) // 2 :], axis=0)
    share = outs[0].shape[2]
    for i in range(count):
        acc[...] = tn(ins[2 * i][...], near) + tn(ins[2 * i + 1][...], far)
        for z in range(outs[0].shape[0]):
            for j in range(2):
                at = pl.multiple_of((2 * z + (y ^ j)) * share, share)
                outs[2 * i + j][z] = acc[:, pl.ds(at, share)].astype(BF16)


def unit_grads(pairs, blocks):
    n = lax.axis_size("fsdp")
    units, d = pairs[0][0].shape[1], blocks[0].shape[1]
    if n != 8:
        half = len(blocks) // 2
        near, far = jnp.concatenate(blocks[:half]), jnp.concatenate(blocks[half:])
        outs = [(tn(a, near) + tn(b, far)).astype(BF16) for a, b in pairs]
        return [(jnp.transpose(o.reshape(units, n, d // n), (1, 0, 2)),) for o in outs]
    me = lax.axis_index("fsdp").astype(jnp.int32).reshape(1)
    outs = vmem_call(
        functools.partial(unit_grad_kernel, len(pairs)),
        "unit_grads",
        [((n // 2, units, d // n), BF16)] * (2 * len(pairs)),
        me,
        [a for pair in pairs for a in pair] + list(blocks),
        cost(1, 1),
        [pltpu.VMEM((units, d), F32)],
    )
    return [outs[2 * i : 2 * i + 2] for i in range(len(pairs))]


def out_grad_kernel(me, m0, m1, m2, m3, beside, low, low_beside, gain, mine, other, acc):
    s, y = me[0], me[1] % 2
    width = m0.shape[1]
    half = acc.shape[0]
    low_here = low[:, pl.ds(pl.multiple_of((s % 2) * half, half), half)]
    for r, m in enumerate((m0, m1, m2, m3)):
        cols = pl.ds(pl.multiple_of((s ^ r) * width, width), width)
        theirs = beside[:, (r ^ 1) * width : ((r ^ 1) + 1) * width]
        acc[:, cols] = tn(low_here, m[...]) + tn(low_beside[...], theirs)
    share = mine.shape[2]
    for j, out in enumerate((mine, other)):
        for z in range(out.shape[0]):
            cols = pl.ds(pl.multiple_of((2 * z + (y ^ j)) * share, share), share)
            out[z, :half] = acc[:, cols].astype(BF16)
            out[z, half:] = gain[:, cols].astype(BF16)


def qkv_grad_kernel(me, normed, da, db, w, mine, other, acc):
    y = me[1] % 2
    share = mine.shape[2]
    pair = da.shape[1] // 3
    total = jnp.zeros((1, acc.shape[1]), F32)
    for part, dd in enumerate((da, db)):
        acc[3 * part * pair : 3 * (part + 1) * pair] = tn(dd[...], normed[...])
        for i in range(3):
            one = acc[(3 * part + i) * pair : (3 * part + i + 1) * pair]
            rows = w[(2 * i + part) * pair : (2 * i + part + 1) * pair].astype(F32)
            total = total + jnp.sum(one * rows, axis=0, keepdims=True)
    total = total / w[6 * pair : 6 * pair + 1].astype(F32)
    for j, out in enumerate((mine, other)):
        for z in range(mine.shape[0]):
            cols = pl.ds(pl.multiple_of((2 * z + (y ^ j)) * share, share), share)
            out[z, : 6 * pair] = acc[:, cols].astype(BF16)
    for f in range(acc.shape[1] // share):
        row = jnp.broadcast_to(total[:, f * share : (f + 1) * share], (8, share)).astype(BF16)
        for j, out in enumerate((mine, other)):

            @pl.when((f % 2) == (y ^ j))
            def _():
                out[f // 2, 6 * pair :] = row


def joined(r, da, db):
    pair = da.shape[2] // 3
    parts = [d[r, :, j * pair : (j + 1) * pair] for j in range(3) for d in (da, db)]
    return jnp.concatenate(parts, axis=1)


def normed_back_kernel(me, da, db, w, n3, n2, n1):
    for r, out in ((3, n3), (2, n2), (1, n1)):
        out[...] = nn(joined(r, da, db), w[: 2 * da.shape[2]]).astype(BF16)


def place_values_kernel(me, v, out):
    width = v.shape[2]
    for j in range(GROUPS):
        out[:, j * width : (j + 1) * width] = v[j].astype(F32)


def place_qkv_kernel(me, p0, p1, p2, p3, oq, ok, ov, gain):
    s = me[0]
    size = (p0.shape[0] - 8) // 6
    share = p0.shape[1]
    total = jnp.zeros((8, share), F32)
    for r, piece in enumerate((p0, p1, p2, p3)):
        for p in range(2):
            start = p * 3 * size
            at = pl.multiple_of((s ^ r) * 2 * size + p * size, size)
            for i, out in enumerate((oq, ok, ov)):
                block = piece[start + i * size : start + (i + 1) * size]
                out[:, pl.ds(at, size)] = jnp.transpose(block.astype(F32))
        total = total + piece[6 * size :].astype(F32)
    gain[...] = total[:1]


def place_units_kernel(me, p0, p1, p2, p3, *refs):
    outs, buf = refs[:-1], refs[-1]
    s = me[0]
    units = p0.shape[0] // len(outs)
    for r, p in enumerate((p0, p1, p2, p3)):
        buf[s ^ r] = p[...].astype(F32)
    for i, out in enumerate(outs):
        for j in range(GROUPS):
            out[:, j * units : (j + 1) * units] = jnp.transpose(buf[j, i * units : (i + 1) * units])


def place_out_kernel(me, own, other, out, gain):
    core = me[0] % 2
    half = own.shape[0] - 8
    for j, piece in enumerate((own, other)):
        at = pl.multiple_of((core ^ j) * half, half)
        out[:, pl.ds(at, half)] = jnp.transpose(piece[:half].astype(F32))
    gain[...] = own[half : half + 1].astype(F32) + other[half : half + 1].astype(F32)


def middle_kernel(me, p0, p1, p2, middle, g, gains, w0, x0, x1, x2, x3, mback, mlow, mhalf, b0, b1, b2, b3, ggrad):
    s = me[0]
    width = b0.shape[1]
    dn = p0[...].astype(F32) + p1[...].astype(F32) + p2[...].astype(F32)
    v = middle[...]
    r = inverse_rms(v)
    x = v * r
    ggrad[...] = jnp.broadcast_to(jnp.sum(dn * x, axis=0, keepdims=True), ggrad.shape)
    dx = dn * gains[1:2].astype(F32)
    total = g[...].astype(F32) + r * (dx - x * jnp.mean(dx * x, axis=-1, keepdims=True))
    mback[...] = total
    mlow[...] = total.astype(BF16)
    half = 4 * x0.shape[0]
    lows = [mlow[:, pl.ds(pl.multiple_of(((s % 2) ^ j) * half, half), half)] for j in range(2)]
    mhalf[...] = lows[1]
    for i, b in enumerate((b0, b1, b2, b3)):
        cols = pl.ds(pl.multiple_of((s ^ i) * width, width), width)
        w1 = jnp.concatenate([x[:, cols] for x in (x0, x1, x2, x3)], axis=0)
        b[...] = (nn(lows[0], w0[w0.shape[0] - half :, cols]) + nn(lows[1], w1)).astype(BF16)


def final_kernel(me, p1, p2, da, db, w, t, gains, mback, out):
    dn = nn(joined(0, da, db), w[: 2 * da.shape[2]])
    dn = dn + p1[...].astype(F32) + p2[...].astype(F32)
    v = t[...].astype(F32)
    r = inverse_rms(v)
    x = v * r
    dx = dn * gains[:1].astype(F32)
    out[...] = mback[...] + r * (dx - x * jnp.mean(dx * x, axis=-1, keepdims=True))


def after(value, *others):
    return lax.optimization_barrier((value,) + others)[0]


def all_after(values, *others):
    return list(lax.optimization_barrier(tuple(values) + others)[: len(values)])


def add(*terms):
    return sum((term.astype(F32) for term in terms[1:]), terms[0].astype(F32)).astype(BF16)


def seq_permute(value, flip):
    return lax.ppermute(value, "seq", [(i, i ^ flip) for i in range(GROUPS)])


def gather_four(own):
    near = seq_permute(own, 1)
    far = seq_permute(own, 2)
    return own, near, far, seq_permute(far, 1)


def exchange_four(pieces):
    return [pieces[0]] + [seq_permute(pieces[r], r) for r in (1, 2, 3)]


def fsdp_permute(value, flip):
    n = lax.axis_size("fsdp")
    return lax.ppermute(value, "fsdp", [(i, i ^ flip) for i in range(n)])


def fsdp_send(both):
    z = lax.axis_index("fsdp") // 2
    parts = [lax.dynamic_index_in_dim(both, z ^ k, 0, keepdims=False) for k in range(both.shape[0])]
    return [parts[0]] + [fsdp_permute(parts[k], 2 * k) for k in range(1, len(parts))]


def scatter_whole(parts):
    return lax.psum_scatter(parts, "fsdp", scatter_dimension=0, tiled=False)


def per_device(
    tokens,
    first_values,
    cotangent,
    first_gain,
    query_weight,
    key_weight,
    value_weight,
    out_weight,
    second_gain,
    gate_weight,
    up_weight,
    down_weight,
):
    n = lax.axis_size("fsdp")
    s = lax.axis_index("seq").astype(jnp.int32)
    me = s.reshape(1)
    place3 = [jnp.stack([s, lax.axis_index("fsdp").astype(jnp.int32), jnp.int32(p)]) for p in (0, 1)]
    t0, g0, f0 = tokens[0], cotangent[0], first_values[0]
    rows, d = t0.shape
    width = d // GROUPS
    pair = width // 2
    units = gate_weight.shape[1] // GROUPS
    share = d // n
    core = s % 2
    ring = n == 8

    def columns(v, which, size):
        return lax.dynamic_slice_in_dim(v, which * size, size, 1)

    here = lax.axis_index("fsdp").astype(jnp.int32)
    gains = jnp.concatenate([first_gain[None], second_gain[None], jnp.zeros((6, share), BF16)])
    qkv_weights = (query_weight, key_weight, value_weight)
    own_qkv = [columns(w, s, width).T for w in qkv_weights]
    own_qkv += [gains, columns(out_weight, core, d // 2).T]
    own_qkv = jnp.concatenate(own_qkv, axis=0)
    own_units = [columns(w, s, units).T for w in (gate_weight, up_weight, down_weight)]
    places = (jnp.arange(4, dtype=jnp.int32) ^ s)[:, None] * rows + jnp.arange(rows, dtype=jnp.int32)
    half_dim = HEAD_DIM // 2
    freqs = jnp.exp(jnp.arange(half_dim, dtype=F32) * (-2.0 * math.log(10000.0) / HEAD_DIM))
    angles = places.astype(F32)[:, :, None] * jnp.tile(freqs, 4)
    sign = jnp.tile(jnp.repeat(jnp.array([-1.0, 1.0], F32), half_dim), 2)
    cosine, sine = jnp.cos(angles), jnp.sin(angles) * sign
    f = [columns(f0, s ^ r, width) for r in range(4)]
    if ring:
        first = [fsdp_permute(own_qkv, flip) for flip in (6, 4, 2)][::-1]
        first_y = fsdp_permute(own_qkv, 1)
    packed2 = seq_permute(jnp.concatenate([t0, f[2], f[3]], axis=1), 2)
    if ring:
        pieces = [own_qkv, first_y]
        for i in range(3):
            one = after(first[i], cosine, sine, *own_units) if i == 0 else first[i]
            pieces += [one, fsdp_permute(one, 1)]
    else:
        pieces = [lax.all_gather(own_qkv, "fsdp", axis=1, tiled=True)]
        unit_pieces = [[lax.all_gather(w, "fsdp", axis=1, tiled=True)] for w in own_units]
    where = here if ring else jnp.int32(0)
    packed1 = seq_permute(jnp.concatenate([t0, f[1]], axis=1), 1)
    crossing = jnp.concatenate([packed2[:, :d], packed2[:, d + width :]], axis=1)
    if ring:
        def pair_send(own, *waits):
            own = after(own, *waits)
            return [own] + [fsdp_permute(own, flip) for flip in (2, 4, 6)]

        gate_w = pair_send(own_units[0], *first, pieces[1], pieces[3])
        crossing = after(crossing, *pieces[1::2], *gate_w)
    packed3 = seq_permute(crossing, 1)

    if ring:
        gate_w.append(fsdp_permute(jnp.concatenate(gate_w, axis=0), 1))
        up_w = pair_send(own_units[1], gate_w[1])
    g2 = seq_permute(after(g0, packed2, *pieces[1::2]), 2)

    q, k, v, normed, w_qkv, w_out = qkv(where, t0, f[0], (packed1, packed2, packed3), pieces, cosine, sine)
    gains = w_qkv[3 * width : 3 * width + 8]
    w_out_sent = w_out
    *m, lse_a = attention(0, me, q, k, v)
    g2 = after(g2, m[0])
    q = after(q, g2)
    g1, g3 = seq_permute(after(g0, g2), 1), seq_permute(g2, 1)
    if ring:
        up_w[1:] = all_after(up_w[1:], m[0])
        gate_w[4] = after(gate_w[4], m[0])
        up_w.append(fsdp_permute(jnp.concatenate(up_w, axis=0), 1))
        down_w = pair_send(own_units[2], *up_w[:4])
        q = after(q, gate_w[4])
    *m, lse_b = attention(1, me, q, k, v, *m)
    if ring:
        up_w[4] = after(up_w[4], m[0])
        down_w[1:] = all_after(down_w[1:], m[0])
        down_w.append(fsdp_permute(jnp.concatenate(down_w, axis=0), 1))
        m = all_after(m, up_w[4])
    m = exchange_four(m)
    if ring:
        m = all_after(m, *down_w[:4])
    w_out_sent = after(w_out_sent, m[2], m[3])
    w_out_other = [
        seq_permute(lax.slice_in_dim(w_out_sent, i * (d // 8), (i + 1) * (d // 8)), 1) for i in range(4)
    ]
    if ring:
        unit_pieces = [gate_w, up_w, down_w]
    m = all_after(m, *w_out_other)
    middle, *s0 = vmem_call(
        out_kernel,
        "out",
        [((rows, d), F32)] + [((rows // 2, d), BF16)] * 2,
        me,
        [*m, w_out, *w_out_other, t0, gains],
        cost(2 * rows * d * d, 8e6),
    )
    s1 = [seq_permute(one, 1) for one in s0]
    s2 = [seq_permute(one, 2) for one in s0]
    hid_near, gate_near, up_near, sb0, sb1 = mlp(where, s0, s1, g0, g1, unit_pieces)
    s2 = all_after(s2, sb0)
    s3 = [seq_permute(one, 1) for one in s2]
    hid_far, gate_far, up_far, sb2, sb3 = mlp(where, s2, s3, g2, g3, unit_pieces)
    sb_both = add(sb2, seq_permute(sb3, 1))
    p = [sb0, seq_permute(after(sb1, sb_both), 1), seq_permute(sb_both, 2)]

    (down_part,) = unit_grads([(hid_near, after(hid_far, p[1]))], (g0, g1, g2, g3))
    if ring:
        down_crossed = fsdp_permute(down_part[1], 1)
    o = vmem_call(
        functools.partial(mlp_out_kernel, len(unit_pieces[2])),
        "mlp_out",
        [((rows, d), BF16)] * 4,
        where.reshape(1),
        [hid_near, after(hid_far, down_part[0]), *unit_pieces[2]],
        cost(2 * 4 * rows * d * units, 8e6),
        [pltpu.VMEM((units, d), BF16)],
    )
    (gate_part,) = unit_grads([(gate_near, after(gate_far, o[0]))], (*s0, *s1, *s2, *s3))
    o1, o3 = all_after([seq_permute(o[1], 1), seq_permute(o[3], 1)], gate_part[0])
    p[2] = after(p[2], gate_part[0])
    p[0] = after(p[0], o3, o1)
    if ring:
        down_both = add(down_part[0], after(down_crossed, p[2]))
        p[2] = after(p[2], down_both)
        gate_crossed = fsdp_permute(after(gate_part[1], down_both), 1)
        mixed_beside = seq_permute(jnp.concatenate(m, axis=1), 1)
        p[0] = after(p[0], mixed_beside)
    mback, mlow, mhalf, b0, b1, b2, b3, ggrad_second = vmem_call(
        middle_kernel,
        "middle",
        [((rows, d), F32), ((rows, d), BF16), ((rows, d // 2), BF16)]
        + [((rows, width), BF16)] * 4
        + [((8, d), F32)],
        me,
        [*p, middle, g0, gains, w_out, *w_out_other],
        cost(2 * rows * d * d, 12e6),
    )
    b = exchange_four([b0, b1, b2, b3])
    o_both = add(o[2], after(o3, mlow))
    flat = lambda x: x.reshape(4 * rows, -1)
    qb = q
    if ring:
        low_beside = seq_permute(mhalf, 1)
        out_part = vmem_call(
            out_grad_kernel,
            "out_grad",
            [((n // 2, d // 2 + 8, share), BF16)] * 2,
            place3[0],
            [*m, mixed_beside, mlow, low_beside, ggrad_second],
            cost(2 * rows * d * d, 6e6),
            [pltpu.VMEM((d // 2, d), F32)],
        )
        (up_part,) = unit_grads([(up_near, after(up_far, out_part[0]))], (*s0, *s1, *s2, *s3))
        b[1:] = all_after(b[1:], up_part[0], o_both)
        down_sent = fsdp_send(after(down_both, b[2], b[3]))
    else:
        (up_part,) = unit_grads([(up_near, up_far)], (*s0, *s1, *s2, *s3))

    def qkv_grads(d_a, d_b):
        if ring:
            return vmem_call(
                qkv_grad_kernel,
                "qkv_grad",
                [((n // 2, 6 * pair + 8, share), BF16)] * 2,
                place3[0],
                [flat(normed), flat(d_a), flat(d_b), w_qkv],
                cost(2 * 4 * rows * d * 6 * pair, 6e6),
                [pltpu.VMEM((6 * pair, d), F32)],
            )
        whole = tn(jnp.concatenate([flat(d_a), flat(d_b)], axis=1), flat(normed))
        starts = [i * width + part * pair for part in range(2) for i in range(3)]
        w = jnp.concatenate([w_qkv[i : i + pair] for i in starts]).astype(F32)
        gain_part = jnp.sum(whole * w, axis=0, keepdims=True) / gains[:1].astype(F32)
        whole = jnp.concatenate([whole, gain_part, jnp.zeros((7, d), F32)]).astype(BF16)
        return (jnp.transpose(whole.reshape(6 * pair + 8, n, share), (1, 0, 2)),)

    d_a, v_a = attention_back(0, me, qb, k, v, b, lse_a, cosine, sine)
    o2 = seq_permute(after(o_both, d_a), 2)
    qb = after(qb, d_a)
    if ring:
        gate_both = add(gate_part[0], after(gate_crossed, d_a))
        down_share = add(*all_after(down_sent, d_a))
        gate_sent = fsdp_send(after(gate_both, down_share))
        up_crossed = fsdp_permute(after(up_part[1], gate_both), 1)
        qb = after(qb, gate_both, down_share)
    d_b, v_b = attention_back(1, me, qb, k, v, b, lse_b, cosine, sine, v_a)
    o2 = after(o2, d_b)
    d_b = after(d_b, o2)
    if ring:
        up_crossed, *gate_sent = all_after([up_crossed] + gate_sent, d_b)
        up_both = add(up_part[0], up_crossed)
        gate_share = add(*gate_sent)
        up_sent = fsdp_send(after(up_both, gate_share))
        out_crossed = fsdp_permute(after(out_part[1], up_both), 1)
        d_b = after(d_b, up_both, gate_share)

    nb3, nb2, nb1 = vmem_call(
        normed_back_kernel,
        "normed_back",
        [((rows, d), BF16)] * 3,
        me,
        [d_a, d_b, w_qkv],
        cost(2 * 3 * rows * d * 3 * width, 8e6),
    )
    nb_both = add(nb2, seq_permute(nb3, 1))
    beside = seq_permute(nb1, 1)
    crossed_far = seq_permute(nb_both, 2)
    qkv_sums = qkv_grads(d_a, after(d_b, nb_both, beside))
    crossed_far = after(crossed_far, qkv_sums[0])
    if ring:
        out_both = add(out_part[0], after(out_crossed, qkv_sums[0]))
        qkv_crossed = fsdp_permute(after(qkv_sums[1], out_both), 1)
        up_share = add(*all_after(up_sent, qkv_sums[0]))
        out_sent = fsdp_send(after(out_both, up_share))
        beside = after(beside, up_share)
        units_sent = jnp.concatenate([gate_share, up_share, down_share], axis=0)
        units_far = seq_permute(units_sent, 2)
    (tokens_grad,) = vmem_call(
        final_kernel,
        "final",
        [((rows, d), F32)],
        me,
        [beside, crossed_far, d_a, d_b, w_qkv, t0, gains, mback],
        cost(0, 6e6),
    )
    if ring:
        units_far = after(units_far, tokens_grad)
        qkv_both = add(qkv_sums[0], after(qkv_crossed, tokens_grad))
        out_share = add(*all_after(out_sent, tokens_grad))
        qkv_sent = fsdp_send(after(qkv_both, out_share))
    else:
        gate_share, up_share, down_share, qkv_share = (
            scatter_whole(v[0]) for v in (gate_part, up_part, down_part, qkv_sums)
        )
        mixed_rows = jnp.zeros((rows, d), BF16)
        for r in range(4):
            mixed_rows = lax.dynamic_update_slice(mixed_rows, m[r], (0, (s ^ r) * width))
        out_part = tn(mlow, mixed_rows)
        halves = [lax.dynamic_slice_in_dim(out_part, (core ^ j) * (d // 2), d // 2) for j in range(2)]
        keep = jnp.concatenate([halves[0], ggrad_second]).reshape(d // 2 + 8, n, share)
        send = jnp.pad(halves[1], ((0, 8), (0, 0))).astype(BF16).reshape(d // 2 + 8, n, share)
        whole = (keep + seq_permute(send, 1).astype(F32)).astype(BF16)
        out_share = scatter_whole(jnp.transpose(whole, (1, 0, 2)))
        units_sent = jnp.concatenate([gate_share, up_share, down_share], axis=0)
    if not ring:
        units_far = seq_permute(units_sent, 2)
    units_all = [units_sent, seq_permute(units_sent, 1), units_far, seq_permute(units_far, 1)]
    v_all = lax.all_to_all(after(v_b, tokens_grad, *units_all), "seq", split_axis=0, concat_axis=0)
    output = add(middle, o[0], o1, o2)[None]
    (values_grad,) = vmem_call(
        place_values_kernel, "place_values", [((rows, d), F32)], me, [v_all], cost(0, 3e6)
    )
    gate_grad, up_grad, down_grad = vmem_call(
        place_units_kernel,
        "place_units",
        [((share, 4 * units), F32)] * 3,
        me,
        units_all,
        cost(0, 3e6),
        [pltpu.VMEM((4, 3 * units, share), F32)],
    )
    if ring:
        out_far = after(seq_permute(after(out_share, qkv_both), 2), gate_grad)
    else:
        out_far = seq_permute(out_share, 2)
    out_share = add(out_share, out_far)
    out_grad, second_gain_grad = vmem_call(
        place_out_kernel,
        "place_out",
        [((share, d), F32), ((1, share), F32)],
        me,
        [out_share, seq_permute(out_share, 1)],
        cost(0, 1e6),
    )
    if ring:
        qkv_share = add(*all_after(qkv_sent, out_grad, gate_grad))
    qkv_far = after(seq_permute(qkv_share, 2), values_grad, output)
    qkv_all = [qkv_share, seq_permute(qkv_share, 1), qkv_far, seq_permute(qkv_far, 1)]
    query_grad, key_grad, value_grad, gain_grad = vmem_call(
        place_qkv_kernel,
        "place_qkv",
        [((share, d), F32)] * 3 + [((1, share), F32)],
        me,
        qkv_all,
        cost(0, 3e6),
    )
    return (
        output,
        tokens_grad[None],
        values_grad[None],
        gain_grad.reshape(share),
        query_grad,
        key_grad,
        value_grad,
        out_grad,
        second_gain_grad.reshape(share),
        gate_grad,
        up_grad,
        down_grad,
    )


def solution(mesh):
    rows = P("fsdp", "seq", None)
    weight = P("fsdp", None)
    gain = P("fsdp")
    in_specs = (rows,) * 3 + (gain,) + (weight,) * 4 + (gain,) + (weight,) * 3
    out_specs = (rows,) * 3 + (gain,) + (weight,) * 4 + (gain,) + (weight,) * 3
    return jax.shard_map(
        per_device, mesh=mesh, in_specs=in_specs, out_specs=out_specs, check_vma=False
    )
```

```python
import functools
import math

import jax
import jax.numpy as jnp
from jax import lax
from jax.experimental import pallas as pl
from jax.experimental.pallas import tpu as pltpu
from jax.sharding import PartitionSpec as P

HEADS = 16
HEAD_DIM = 64
GROUPS = 4
EPSILON = 1e-06
NEGATIVE = -1e30
F32 = jnp.float32
BF16 = jnp.bfloat16
PARAMS = pltpu.CompilerParams(vmem_limit_bytes=56 * 2**20)


def nn(a, b):
    return lax.dot_general(a, b, (((1,), (0,)), ((), ())), preferred_element_type=F32)


def nt(a, b):
    return lax.dot_general(a, b, (((1,), (1,)), ((), ())), preferred_element_type=F32)


def tn(a, b):
    return lax.dot_general(a, b, (((0,), (0,)), ((), ())), preferred_element_type=F32)


def cost(flops, nbytes, trans=0):
    flops, nbytes, trans = 1, 1, 0
    return pl.CostEstimate(flops=int(flops), bytes_accessed=int(nbytes), transcendentals=int(trans))


def turn(u, cosine, sine):
    lane = lax.broadcasted_iota(jnp.int32, (u.shape[0], 128), 1)
    first = lane % HEAD_DIM < HEAD_DIM // 2
    parts = []
    for j in range(u.shape[1] // 128):
        part = u[:, 128 * j : 128 * (j + 1)]
        other = jnp.where(first, pltpu.roll(part, 96, 1), pltpu.roll(part, 32, 1))
        parts.append(part * cosine + other * sine)
    return jnp.concatenate(parts, axis=1)


def inverse_rms(v):
    return lax.rsqrt(jnp.mean(v * v, axis=-1, keepdims=True) + EPSILON)


ANY = pl.BlockSpec(memory_space=pl.ANY)


def qkv_kernel(count, me, t0, f0, p1, p2, p3, *refs):
    pieces, rest = refs[:count], refs[count:]
    cosine, sine, q, k, v, n, w, wo, tv, fv, sems = rest
    width = q.shape[-1]
    d = tv.shape[-1]
    share = d // count
    first, last = [], []
    for i, piece in enumerate(pieces):
        at = pl.ds(pl.multiple_of((me[0] ^ i) * share, share), share)
        first.append(pltpu.make_async_copy(piece.at[: w.shape[0]], w.at[:, at], sems.at[8 + i]))
        last.append(pltpu.make_async_copy(piece.at[w.shape[0] :], wo.at[:, at], sems.at[16 + i]))
    loads = [(t0, f0)] + [(p.at[:, :d], p.at[:, d : d + width]) for p in (p1, p2, p3)]
    copies = []
    for i, (t, f) in enumerate(loads):
        copies.append(pltpu.make_async_copy(t, tv.at[i], sems.at[2 * i]))
        copies.append(pltpu.make_async_copy(f, fv.at[i], sems.at[2 * i + 1]))
    for copy in copies[:2] + first + copies[2:] + last:
        copy.start()
    for i in range(4):
        copies[2 * i].wait()
        if i == 0:
            for copy in first:
                copy.wait()
        gain = w[3 * width : 3 * width + 1].astype(F32)
        x = tv[i].astype(F32)
        normed = (x * inverse_rms(x) * gain).astype(BF16)
        n[i] = normed
        u = nt(normed, w[: 3 * width])
        c, s = cosine[i], sine[i]
        q[i] = (turn(u[:, :width], c, s).astype(BF16).astype(F32) * 0.125).astype(BF16)
        k[i] = turn(u[:, width : 2 * width], c, s).astype(BF16)
        copies[2 * i + 1].wait()
        v[i] = (0.5 * u[:, 2 * width :] + 0.5 * fv[i].astype(F32)).astype(BF16)
    for copy in last:
        copy.wait()


def qkv(where, t, f, packed, pieces, cosine, sine):
    rows, d = t.shape
    width = f.shape[1]
    full = lambda *shape: pl.BlockSpec(shape, lambda i, me: (0,) * len(shape))
    main = 3 * width + 8
    shapes = [(4, rows, width)] * 3 + [(4, rows, d), (main, d), (pieces[0].shape[0] - main, d)]
    return pl.pallas_call(
        functools.partial(qkv_kernel, len(pieces)),
        grid_spec=pltpu.PrefetchScalarGridSpec(
            num_scalar_prefetch=1,
            grid=(1,),
            in_specs=[ANY] * (5 + len(pieces)) + [full(4, rows, 128)] * 2,
            out_specs=[full(*s) for s in shapes],
            scratch_shapes=[
                pltpu.VMEM((4, rows, d), BF16),
                pltpu.VMEM((4, rows, width), BF16),
                pltpu.SemaphoreType.DMA((24,)),
            ],
        ),
        out_shape=[jax.ShapeDtypeStruct(s, BF16) for s in shapes],
        compiler_params=PARAMS,
        cost_estimate=cost(2 * 4 * rows * d * 3 * width, 12e6),
        name="qkv",
    )(where.reshape(1), t, f, *packed, *pieces, cosine, sine)


def attn_kernel(me, q, k, v, *refs):
    before, (o0, o1, o2, o3, lse, o) = refs[:-6], refs[-6:]
    h = pl.program_id(0)
    rows, width = q.shape[1:]
    mine = lax.broadcasted_iota(jnp.int32, (1, width), 1) // HEAD_DIM == h
    row = lax.broadcasted_iota(jnp.int32, (rows, rows), 0)
    col = lax.broadcasted_iota(jnp.int32, (rows, rows), 1)
    s = me[0]
    for i in range(GROUPS):
        ri = i ^ s
        qi = jnp.where(mine, q[ri], jnp.zeros((), BF16))
        tiles = []
        for j in range(i + 1):
            tile = nt(qi, k[j ^ s])
            if j == i:
                tile = jnp.where(col <= row, tile, NEGATIVE)
            tiles.append(tile)
        largest = tiles[0].max(axis=1, keepdims=True)
        for tile in tiles[1:]:
            largest = jnp.maximum(largest, tile.max(axis=1, keepdims=True))
        tiles = [jnp.exp(tile - largest) for tile in tiles]
        total = tiles[0].sum(axis=1, keepdims=True)
        for tile in tiles[1:]:
            total = total + tile.sum(axis=1, keepdims=True)
        inverse = 1.0 / total
        acc = jnp.zeros((rows, width), F32)
        for j in range(i + 1):
            acc = acc + nn((tiles[j] * inverse).astype(BF16), v[j ^ s])
        o[ri] = jnp.where(mine, acc.astype(BF16), o[ri])
        stat = jnp.broadcast_to(largest + jnp.log(total), (rows, 128))
        lse[0, i] = jnp.transpose(stat)[:8]

    @pl.when(h == pl.num_programs(0) - 1)
    def _():
        for r, out in enumerate((o0, o1, o2, o3)):
            if before:
                out[:, :width] = before[r][...]
                out[:, width:] = o[r]
            else:
                out[...] = o[r]


def attention(part, me, q, k, v, *before):
    rows = q.shape[1]
    width = 2 * HEAD_DIM
    full = lambda *shape: pl.BlockSpec(shape, lambda h, me: (0,) * len(shape))
    pair = pl.BlockSpec((4, rows, width), lambda h, me: (0, 0, part))
    both = (rows, 2 * width if before else width)
    return pl.pallas_call(
        attn_kernel,
        grid_spec=pltpu.PrefetchScalarGridSpec(
            num_scalar_prefetch=1,
            grid=(2,),
            in_specs=[pair] * 3 + [full(*one.shape) for one in before],
            out_specs=[full(*both)] * 4
            + [pl.BlockSpec((1, 4, 8, rows), lambda h, me: (h, 0, 0, 0))],
            scratch_shapes=[pltpu.VMEM((4, rows, width), BF16)],
        ),
        out_shape=[jax.ShapeDtypeStruct(both, BF16)] * 4
        + [jax.ShapeDtypeStruct((2, 4, 8, rows), F32)],
        compiler_params=PARAMS,
        cost_estimate=cost(2 * 2 * 10 * rows * rows * width * 4, 4e6, 20 * rows * rows),
        name="attention",
    )(me, q, k, v, *before)


def attn_back_kernel(me, q, k, v, b0, b1, b2, b3, lse, cosine, sine, *rest):
    before, (out, vout, do, dq, dk, dv) = rest[:-6], rest[-6:]
    h = pl.program_id(0)
    rows, width = q.shape[1:]
    mine = lax.broadcasted_iota(jnp.int32, (1, width), 1) // HEAD_DIM == h
    key = lax.broadcasted_iota(jnp.int32, (rows, rows), 0)
    query = lax.broadcasted_iota(jnp.int32, (rows, rows), 1)
    s = me[0]
    zero = jnp.zeros((), BF16)

    @pl.when(h == 0)
    def _():
        for r, b in enumerate((b0, b1, b2, b3)):
            do[r] = b[...]
        dq[...] = jnp.zeros_like(dq)
        dk[...] = jnp.zeros_like(dk)
        dv[...] = jnp.zeros_like(dv)

    for i in range(GROUPS):
        qi = jnp.where(mine, q[i ^ s], zero)
        doi = jnp.where(mine, do[i ^ s], zero)
        stat = lse[0, i][:1]
        soft, back = [], []
        dot = jnp.zeros((1, rows), F32)
        for j in range(i + 1):
            tile = nt(k[j ^ s], qi)
            if j == i:
                tile = jnp.where(key <= query, tile, NEGATIVE)
            p = jnp.exp(tile - stat)
            dp = nt(v[j ^ s], doi)
            dot = dot + jnp.sum(p * dp, axis=0, keepdims=True)
            soft.append(p)
            back.append(dp)
        acc = jnp.zeros((rows, width), F32)
        for j in range(i + 1):
            ds = (soft[j] * (back[j] - dot)).astype(BF16)
            dk[j] += nn(ds, qi)
            dv[j] += nn(soft[j].astype(BF16), doi)
            acc = acc + tn(ds, jnp.where(mine, k[j ^ s], zero))
        dq[i] += acc

    @pl.when(h == pl.num_programs(0) - 1)
    def _():
        for i in range(GROUPS):
            ri = i ^ s
            c, n = cosine[ri], -sine[ri]
            out[ri, :, :width] = turn(dq[i] * 0.125, c, n).astype(BF16)
            out[ri, :, width : 2 * width] = turn(dk[i], c, n).astype(BF16)
            half = (0.5 * dv[i]).astype(BF16)
            out[ri, :, 2 * width :] = half
            vout[i, :, len(before) * width :] = half
            if before:
                vout[i, :, :width] = before[0][i]


def attention_back(part, me, q, k, v, b, lse, cosine, sine, *before):
    rows = q.shape[1]
    width = 2 * HEAD_DIM
    full = lambda *shape: pl.BlockSpec(shape, lambda h, me: (0,) * len(shape))
    pair = pl.BlockSpec((4, rows, width), lambda h, me: (0, 0, part))
    return pl.pallas_call(
        attn_back_kernel,
        grid_spec=pltpu.PrefetchScalarGridSpec(
            num_scalar_prefetch=1,
            grid=(2,),
            in_specs=[pair] * 3
            + [pl.BlockSpec((rows, width), lambda h, me: (0, part))] * 4
            + [pl.BlockSpec((1, 4, 8, rows), lambda h, me: (h, 0, 0, 0))]
            + [full(4, rows, 128)] * 2
            + [full(*one.shape) for one in before],
            out_specs=[full(4, rows, 3 * width), full(4, rows, (1 + len(before)) * width)],
            scratch_shapes=[pltpu.VMEM((4, rows, width), BF16)]
            + [pltpu.VMEM((4, rows, width), F32)] * 3,
        ),
        out_shape=[
            jax.ShapeDtypeStruct((4, rows, 3 * width), BF16),
            jax.ShapeDtypeStruct((4, rows, (1 + len(before)) * width), BF16),
        ],
        compiler_params=PARAMS,
        cost_estimate=cost(5 * 2 * 10 * rows * rows * width * 4, 4e6, 20 * rows * rows),
        name="attention_back",
    )(me, q, k, v, *b, lse, cosine, sine, *before)


def out_kernel(me, m0, m1, m2, m3, w0, x0, x1, x2, x3, t, gains, middle, lo, hi):
    s = me[0]
    width = m0.shape[1]
    quarter = x0.shape[0]
    first = w0.shape[0] - 4 * quarter
    ws = [[w0.at[first + i * quarter : first + (i + 1) * quarter] for i in range(4)], [x0, x1, x2, x3]]
    for j in range(2):
        for i, w in enumerate(ws[j]):
            start = ((s % 2) ^ j) * 4 * quarter + i * quarter
            cols = pl.ds(pl.multiple_of(start, quarter), quarter)
            part = None
            for r, m in enumerate((m0, m1, m2, m3)):
                one = nt(m[...], w[:, pl.ds(pl.multiple_of((s ^ r) * width, width), width)])
                part = one if part is None else part + one
            middle[:, cols] = t[:, cols].astype(F32) + part
    acc = middle[...]
    second = (acc * inverse_rms(acc) * gains[1:2].astype(F32)).astype(BF16)
    lo[...] = second[: lo.shape[0]]
    hi[...] = second[lo.shape[0] :]


def vmem_call(kernel, name, shapes, me, args, estimate, scratch=()):
    full = lambda shape: pl.BlockSpec(shape, lambda i, me: (0,) * len(shape))
    outs = [jax.ShapeDtypeStruct(s, t) for s, t in shapes]
    return pl.pallas_call(
        kernel,
        grid_spec=pltpu.PrefetchScalarGridSpec(
            num_scalar_prefetch=1,
            grid=(1,),
            in_specs=[full(a.shape) for a in args],
            out_specs=[full(s) for s, _ in shapes],
            scratch_shapes=scratch,
        ),
        out_shape=outs,
        compiler_params=PARAMS,
        cost_estimate=estimate,
        name=name,
    )(me, *args)


def mlp_kernel(count, me, sa0, sa1, sb0, sb1, ga, gb, *refs):
    pieces, outs = refs[: 3 * count], refs[3 * count : 3 * count + 5]
    sv, gv, wv, hid, gback, uback, sback, sems = refs[3 * count + 5 :]
    _, units, d = wv.shape
    rows = ga.shape[0]
    copies = [pltpu.make_async_copy(sa0, sv.at[0, : rows // 2], sems.at[0])]
    copies.append(pltpu.make_async_copy(sa1, sv.at[0, rows // 2 :], sems.at[1]))
    parts = []
    for h in range(3):
        loads = []
        if count == 1:
            loads.append((pieces[h], wv.at[h]))
        else:
            share = d // 8
            for k in range(4):
                mine, other = pieces[h * count + k], pieces[h * count + 4].at[k * units : (k + 1) * units]
                for piece, flip in ((mine, 2 * k), (other, 2 * k + 1)):
                    at = pl.ds(pl.multiple_of((me[0] ^ flip) * share, share), share)
                    loads.append((piece, wv.at[h, :, at]))
        sem = lambda i, h=h: sems.at[15 + 8 * h + i]
        parts.append([pltpu.make_async_copy(a, b, sem(i)) for i, (a, b) in enumerate(loads)])
    copies.append(pltpu.make_async_copy(ga, gv.at[0], sems.at[4]))
    copies.append(pltpu.make_async_copy(sb0, sv.at[1, : rows // 2], sems.at[2]))
    copies.append(pltpu.make_async_copy(sb1, sv.at[1, rows // 2 :], sems.at[5]))
    copies.append(pltpu.make_async_copy(gb, gv.at[1], sems.at[6]))
    for copy in copies[:2] + parts[0] + parts[1] + copies[2:3] + parts[2] + copies[3:]:
        copy.start()
    writes = []

    def write(buf, out):
        copy = pltpu.make_async_copy(buf, out, sems.at[7 + len(writes)])
        copy.start()
        writes.append(copy)

    for i in range(2):
        copies[3 if i else 0].wait()
        copies[4 if i else 1].wait()
        if i == 0:
            for copy in parts[0]:
                copy.wait()
        gate = nt(sv[i], wv[0])
        if i == 0:
            for copy in parts[1]:
                copy.wait()
        up = nt(sv[i], wv[1])
        sg = jax.nn.sigmoid(gate)
        act = gate * sg
        hid[i] = (act * up).astype(BF16)
        at = slice(i * rows, (i + 1) * rows)
        write(hid.at[i], outs[0].at[at])
        copies[5 if i else 2].wait()
        if i == 0:
            for copy in parts[2]:
                copy.wait()
        hb = nt(gv[i], wv[2])
        gate_back = (hb * up * sg * (1.0 + gate * (1.0 - sg))).astype(BF16)
        up_back = (hb * act).astype(BF16)
        gback[i] = gate_back
        write(gback.at[i], outs[1].at[at])
        uback[i] = up_back
        write(uback.at[i], outs[2].at[at])
        sback[i] = (nn(gate_back, wv[0]) + nn(up_back, wv[1])).astype(BF16)
        write(sback.at[i], outs[3 + i])
    for copy in writes:
        copy.wait()


def any_call(kernel, name, shapes, me, args, estimate, scratch):
    return pl.pallas_call(
        kernel,
        grid_spec=pltpu.PrefetchScalarGridSpec(
            num_scalar_prefetch=1,
            grid=(1,),
            in_specs=[ANY] * len(args),
            out_specs=[ANY] * len(shapes),
            scratch_shapes=scratch,
        ),
        out_shape=[jax.ShapeDtypeStruct(s, t) for s, t in shapes],
        compiler_params=PARAMS,
        cost_estimate=estimate,
        name=name,
    )(me, *args)


def mlp(where, sa, sb, ga, gb, pieces):
    rows, d = ga.shape
    units = pieces[0][0].shape[0]
    part = ((2 * rows, units), BF16)
    return any_call(
        functools.partial(mlp_kernel, len(pieces[0])),
        "mlp",
        [part] * 3 + [((rows, d), BF16)] * 2,
        where.reshape(1),
        [*sa, *sb, ga, gb] + [one for some in pieces for one in some],
        cost(2 * 5 * 2 * rows * d * units, 12e6, 2 * rows * units),
        [pltpu.VMEM((2, rows, d), BF16)] * 2
        + [pltpu.VMEM((3, units, d), BF16)]
        + [pltpu.VMEM((2, rows, units), BF16)] * 3
        + [pltpu.VMEM((2, rows, d), BF16), pltpu.SemaphoreType.DMA((39,))],
    )


def mlp_out_kernel(count, me, hn, hf, *refs):
    pieces, outs, w = refs[:count], refs[count : count + 4], refs[-1]
    units, d = w.shape
    rows = outs[0].shape[0]
    if count == 1:
        w[...] = pieces[0][...]
    else:
        share = d // 8
        for k in range(4):
            for piece, flip in ((pieces[k], 2 * k), (pieces[4].at[k * units : (k + 1) * units], 2 * k + 1)):
                w[:, pl.ds(pl.multiple_of((me[0] ^ flip) * share, share), share)] = piece[...]
    for h, pair in ((hn, outs[:2]), (hf, outs[2:])):
        for i, out in enumerate(pair):
            out[...] = nn(h[i * rows : (i + 1) * rows], w[...]).astype(BF16)


def unit_grad_kernel(count, me, *refs):
    ins, outs, acc = refs[: -1 - 2 * count], refs[-1 - 2 * count : -1], refs[-1]
    blocks = [block[...] for block in ins[2 * count :]]
    y = me[0] % 2
    near = jnp.concatenate(blocks[: len(blocks) // 2], axis=0)
    far = jnp.concatenate(blocks[len(blocks) // 2 :], axis=0)
    share = outs[0].shape[2]
    for i in range(count):
        acc[...] = tn(ins[2 * i][...], near) + tn(ins[2 * i + 1][...], far)
        for z in range(outs[0].shape[0]):
            for j in range(2):
                at = pl.multiple_of((2 * z + (y ^ j)) * share, share)
                outs[2 * i + j][z] = acc[:, pl.ds(at, share)].astype(BF16)


def unit_grads(pairs, blocks):
    n = lax.axis_size("fsdp")
    units, d = pairs[0][0].shape[1], blocks[0].shape[1]
    if n != 8:
        half = len(blocks) // 2
        near, far = jnp.concatenate(blocks[:half]), jnp.concatenate(blocks[half:])
        outs = [(tn(a, near) + tn(b, far)).astype(BF16) for a, b in pairs]
        return [(jnp.transpose(o.reshape(units, n, d // n), (1, 0, 2)),) for o in outs]
    me = lax.axis_index("fsdp").astype(jnp.int32).reshape(1)
    outs = vmem_call(
        functools.partial(unit_grad_kernel, len(pairs)),
        "unit_grads",
        [((n // 2, units, d // n), BF16)] * (2 * len(pairs)),
        me,
        [a for pair in pairs for a in pair] + list(blocks),
        cost(1, 1),
        [pltpu.VMEM((units, d), F32)],
    )
    return [outs[2 * i : 2 * i + 2] for i in range(len(pairs))]


def out_grad_kernel(me, m0, m1, m2, m3, beside, low, low_beside, gain, mine, other, acc):
    s, y = me[0], me[1] % 2
    width = m0.shape[1]
    half = acc.shape[0]
    low_here = low[:, pl.ds(pl.multiple_of((s % 2) * half, half), half)]
    for r, m in enumerate((m0, m1, m2, m3)):
        cols = pl.ds(pl.multiple_of((s ^ r) * width, width), width)
        theirs = beside[:, (r ^ 1) * width : ((r ^ 1) + 1) * width]
        acc[:, cols] = tn(low_here, m[...]) + tn(low_beside[...], theirs)
    share = mine.shape[2]
    for j, out in enumerate((mine, other)):
        for z in range(out.shape[0]):
            cols = pl.ds(pl.multiple_of((2 * z + (y ^ j)) * share, share), share)
            out[z, :half] = acc[:, cols].astype(BF16)
            out[z, half:] = gain[:, cols].astype(BF16)


def qkv_grad_kernel(me, normed, da, db, w, mine, other, acc):
    y = me[1] % 2
    share = mine.shape[2]
    pair = da.shape[1] // 3
    total = jnp.zeros((1, acc.shape[1]), F32)
    for part, dd in enumerate((da, db)):
        acc[3 * part * pair : 3 * (part + 1) * pair] = tn(dd[...], normed[...])
        for i in range(3):
            one = acc[(3 * part + i) * pair : (3 * part + i + 1) * pair]
            rows = w[(2 * i + part) * pair : (2 * i + part + 1) * pair].astype(F32)
            total = total + jnp.sum(one * rows, axis=0, keepdims=True)
    total = total / w[6 * pair : 6 * pair + 1].astype(F32)
    for j, out in enumerate((mine, other)):
        for z in range(mine.shape[0]):
            cols = pl.ds(pl.multiple_of((2 * z + (y ^ j)) * share, share), share)
            out[z, : 6 * pair] = acc[:, cols].astype(BF16)
    for f in range(acc.shape[1] // share):
        row = jnp.broadcast_to(total[:, f * share : (f + 1) * share], (8, share)).astype(BF16)
        for j, out in enumerate((mine, other)):

            @pl.when((f % 2) == (y ^ j))
            def _():
                out[f // 2, 6 * pair :] = row


def joined(r, da, db):
    pair = da.shape[2] // 3
    parts = [d[r, :, j * pair : (j + 1) * pair] for j in range(3) for d in (da, db)]
    return jnp.concatenate(parts, axis=1)


def normed_back_kernel(me, da, db, w, n3, n2, n1):
    for r, out in ((3, n3), (2, n2), (1, n1)):
        out[...] = nn(joined(r, da, db), w[: 2 * da.shape[2]]).astype(BF16)


def place_values_kernel(me, v, out):
    width = v.shape[2]
    for j in range(GROUPS):
        out[:, j * width : (j + 1) * width] = v[j].astype(F32)


def place_qkv_kernel(me, p0, p1, p2, p3, oq, ok, ov, gain):
    s = me[0]
    size = (p0.shape[0] - 8) // 6
    share = p0.shape[1]
    total = jnp.zeros((8, share), F32)
    for r, piece in enumerate((p0, p1, p2, p3)):
        for p in range(2):
            start = p * 3 * size
            at = pl.multiple_of((s ^ r) * 2 * size + p * size, size)
            for i, out in enumerate((oq, ok, ov)):
                block = piece[start + i * size : start + (i + 1) * size]
                out[:, pl.ds(at, size)] = jnp.transpose(block.astype(F32))
        total = total + piece[6 * size :].astype(F32)
    gain[...] = total[:1]


def place_units_kernel(me, p0, p1, p2, p3, *refs):
    outs, buf = refs[:-1], refs[-1]
    s = me[0]
    units = p0.shape[0] // len(outs)
    for r, p in enumerate((p0, p1, p2, p3)):
        buf[s ^ r] = p[...].astype(F32)
    for i, out in enumerate(outs):
        for j in range(GROUPS):
            out[:, j * units : (j + 1) * units] = jnp.transpose(buf[j, i * units : (i + 1) * units])


def place_out_kernel(me, own, other, out, gain):
    core = me[0] % 2
    half = own.shape[0] - 8
    for j, piece in enumerate((own, other)):
        at = pl.multiple_of((core ^ j) * half, half)
        out[:, pl.ds(at, half)] = jnp.transpose(piece[:half].astype(F32))
    gain[...] = own[half : half + 1].astype(F32) + other[half : half + 1].astype(F32)


def middle_kernel(me, p0, p1, p2, middle, g, gains, w0, x0, x1, x2, x3, mback, mlow, mhalf, b0, b1, b2, b3, ggrad):
    s = me[0]
    width = b0.shape[1]
    dn = p0[...].astype(F32) + p1[...].astype(F32) + p2[...].astype(F32)
    v = middle[...]
    r = inverse_rms(v)
    x = v * r
    ggrad[...] = jnp.broadcast_to(jnp.sum(dn * x, axis=0, keepdims=True), ggrad.shape)
    dx = dn * gains[1:2].astype(F32)
    total = g[...].astype(F32) + r * (dx - x * jnp.mean(dx * x, axis=-1, keepdims=True))
    mback[...] = total
    mlow[...] = total.astype(BF16)
    half = 4 * x0.shape[0]
    lows = [mlow[:, pl.ds(pl.multiple_of(((s % 2) ^ j) * half, half), half)] for j in range(2)]
    mhalf[...] = lows[1]
    for i, b in enumerate((b0, b1, b2, b3)):
        cols = pl.ds(pl.multiple_of((s ^ i) * width, width), width)
        w1 = jnp.concatenate([x[:, cols] for x in (x0, x1, x2, x3)], axis=0)
        b[...] = (nn(lows[0], w0[w0.shape[0] - half :, cols]) + nn(lows[1], w1)).astype(BF16)


def final_kernel(me, p1, p2, da, db, w, t, gains, mback, out):
    dn = nn(joined(0, da, db), w[: 2 * da.shape[2]])
    dn = dn + p1[...].astype(F32) + p2[...].astype(F32)
    v = t[...].astype(F32)
    r = inverse_rms(v)
    x = v * r
    dx = dn * gains[:1].astype(F32)
    out[...] = mback[...] + r * (dx - x * jnp.mean(dx * x, axis=-1, keepdims=True))


def after(value, *others):
    return lax.optimization_barrier((value,) + others)[0]


def all_after(values, *others):
    return list(lax.optimization_barrier(tuple(values) + others)[: len(values)])


def add(*terms):
    return sum((term.astype(F32) for term in terms[1:]), terms[0].astype(F32)).astype(BF16)


def seq_permute(value, flip):
    return lax.ppermute(value, "seq", [(i, i ^ flip) for i in range(GROUPS)])


def gather_four(own):
    near = seq_permute(own, 1)
    far = seq_permute(own, 2)
    return own, near, far, seq_permute(far, 1)


def exchange_four(pieces):
    return [pieces[0]] + [seq_permute(pieces[r], r) for r in (1, 2, 3)]


def fsdp_permute(value, flip):
    n = lax.axis_size("fsdp")
    return lax.ppermute(value, "fsdp", [(i, i ^ flip) for i in range(n)])


def fsdp_send(both):
    z = lax.axis_index("fsdp") // 2
    parts = [lax.dynamic_index_in_dim(both, z ^ k, 0, keepdims=False) for k in range(both.shape[0])]
    return [parts[0]] + [fsdp_permute(parts[k], 2 * k) for k in range(1, len(parts))]


def scatter_whole(parts):
    return lax.psum_scatter(parts, "fsdp", scatter_dimension=0, tiled=False)


def per_device(
    tokens,
    first_values,
    cotangent,
    first_gain,
    query_weight,
    key_weight,
    value_weight,
    out_weight,
    second_gain,
    gate_weight,
    up_weight,
    down_weight,
):
    n = lax.axis_size("fsdp")
    s = lax.axis_index("seq").astype(jnp.int32)
    me = s.reshape(1)
    place3 = [jnp.stack([s, lax.axis_index("fsdp").astype(jnp.int32), jnp.int32(p)]) for p in (0, 1)]
    t0, g0, f0 = tokens[0], cotangent[0], first_values[0]
    rows, d = t0.shape
    width = d // GROUPS
    pair = width // 2
    units = gate_weight.shape[1] // GROUPS
    share = d // n
    core = s % 2
    ring = n == 8

    def columns(v, which, size):
        return lax.dynamic_slice_in_dim(v, which * size, size, 1)

    here = lax.axis_index("fsdp").astype(jnp.int32)
    gains = jnp.concatenate([first_gain[None], second_gain[None], jnp.zeros((6, share), BF16)])
    qkv_weights = (query_weight, key_weight, value_weight)
    own_qkv = [columns(w, s, width).T for w in qkv_weights]
    own_qkv += [gains, columns(out_weight, core, d // 2).T]
    own_qkv = jnp.concatenate(own_qkv, axis=0)
    own_units = [columns(w, s, units).T for w in (gate_weight, up_weight, down_weight)]
    places = (jnp.arange(4, dtype=jnp.int32) ^ s)[:, None] * rows + jnp.arange(rows, dtype=jnp.int32)
    half_dim = HEAD_DIM // 2
    freqs = jnp.exp(jnp.arange(half_dim, dtype=F32) * (-2.0 * math.log(10000.0) / HEAD_DIM))
    angles = places.astype(F32)[:, :, None] * jnp.tile(freqs, 4)
    sign = jnp.tile(jnp.repeat(jnp.array([-1.0, 1.0], F32), half_dim), 2)
    cosine, sine = jnp.cos(angles), jnp.sin(angles) * sign
    f = [columns(f0, s ^ r, width) for r in range(4)]
    if ring:
        first = [fsdp_permute(own_qkv, flip) for flip in (6, 4, 2)][::-1]
        first_y = fsdp_permute(own_qkv, 1)
    packed2 = seq_permute(jnp.concatenate([t0, f[2], f[3]], axis=1), 2)
    if ring:
        pieces = [own_qkv, first_y]
        for i in range(3):
            one = after(first[i], cosine, sine, *own_units) if i == 0 else first[i]
            pieces += [one, fsdp_permute(one, 1)]
    else:
        pieces = [lax.all_gather(own_qkv, "fsdp", axis=1, tiled=True)]
        unit_pieces = [[lax.all_gather(w, "fsdp", axis=1, tiled=True)] for w in own_units]
    where = here if ring else jnp.int32(0)
    packed1 = seq_permute(jnp.concatenate([t0, f[1]], axis=1), 1)
    crossing = jnp.concatenate([packed2[:, :d], packed2[:, d + width :]], axis=1)
    if ring:
        def pair_send(own, *waits):
            own = after(own, *waits)
            return [own] + [fsdp_permute(own, flip) for flip in (2, 4, 6)]

        gate_w = pair_send(own_units[0], *first, pieces[1], pieces[3])
        crossing = after(crossing, *pieces[1::2], *gate_w)
    packed3 = seq_permute(crossing, 1)

    if ring:
        gate_w.append(fsdp_permute(jnp.concatenate(gate_w, axis=0), 1))
        up_w = pair_send(own_units[1], gate_w[1])
    g2 = seq_permute(after(g0, packed2, *pieces[1::2]), 2)

    q, k, v, normed, w_qkv, w_out = qkv(where, t0, f[0], (packed1, packed2, packed3), pieces, cosine, sine)
    gains = w_qkv[3 * width : 3 * width + 8]
    w_out_sent = w_out
    *m, lse_a = attention(0, me, q, k, v)
    g2 = after(g2, m[0])
    q = after(q, g2)
    g1, g3 = seq_permute(after(g0, g2), 1), seq_permute(g2, 1)
    if ring:
        up_w[1:] = all_after(up_w[1:], m[0])
        gate_w[4] = after(gate_w[4], m[0])
        up_w.append(fsdp_permute(jnp.concatenate(up_w, axis=0), 1))
        down_w = pair_send(own_units[2], *up_w[:4])
        q = after(q, gate_w[4])
    *m, lse_b = attention(1, me, q, k, v, *m)
    if ring:
        up_w[4] = after(up_w[4], m[0])
        down_w[1:] = all_after(down_w[1:], m[0])
        down_w.append(fsdp_permute(jnp.concatenate(down_w, axis=0), 1))
        m = all_after(m, up_w[4])
    m = exchange_four(m)
    if ring:
        m = all_after(m, *down_w[:4])
    w_out_sent = after(w_out_sent, m[2], m[3])
    w_out_other = [
        seq_permute(lax.slice_in_dim(w_out_sent, i * (d // 8), (i + 1) * (d // 8)), 1) for i in range(4)
    ]
    if ring:
        unit_pieces = [gate_w, up_w, down_w]
    m = all_after(m, *w_out_other)
    middle, *s0 = vmem_call(
        out_kernel,
        "out",
        [((rows, d), F32)] + [((rows // 2, d), BF16)] * 2,
        me,
        [*m, w_out, *w_out_other, t0, gains],
        cost(2 * rows * d * d, 8e6),
    )
    s1 = [seq_permute(one, 1) for one in s0]
    s2 = [seq_permute(one, 2) for one in s0]
    hid_near, gate_near, up_near, sb0, sb1 = mlp(where, s0, s1, g0, g1, unit_pieces)
    s2 = all_after(s2, sb0)
    s3 = [seq_permute(one, 1) for one in s2]
    hid_far, gate_far, up_far, sb2, sb3 = mlp(where, s2, s3, g2, g3, unit_pieces)
    sb_both = add(sb2, seq_permute(sb3, 1))
    p = [sb0, seq_permute(after(sb1, sb_both), 1), seq_permute(sb_both, 2)]

    (down_part,) = unit_grads([(hid_near, after(hid_far, p[1]))], (g0, g1, g2, g3))
    if ring:
        down_crossed = fsdp_permute(down_part[1], 1)
    o = vmem_call(
        functools.partial(mlp_out_kernel, len(unit_pieces[2])),
        "mlp_out",
        [((rows, d), BF16)] * 4,
        where.reshape(1),
        [hid_near, after(hid_far, down_part[0]), *unit_pieces[2]],
        cost(2 * 4 * rows * d * units, 8e6),
        [pltpu.VMEM((units, d), BF16)],
    )
    (gate_part,) = unit_grads([(gate_near, after(gate_far, o[0]))], (*s0, *s1, *s2, *s3))
    o1, o3 = all_after([seq_permute(o[1], 1), seq_permute(o[3], 1)], gate_part[0])
    p[2] = after(p[2], gate_part[0])
    p[0] = after(p[0], o3, o1)
    if ring:
        down_both = add(down_part[0], after(down_crossed, p[2]))
        p[2] = after(p[2], down_both)
        gate_crossed = fsdp_permute(after(gate_part[1], down_both), 1)
        mixed_beside = seq_permute(jnp.concatenate(m, axis=1), 1)
        p[0] = after(p[0], mixed_beside)
    mback, mlow, mhalf, b0, b1, b2, b3, ggrad_second = vmem_call(
        middle_kernel,
        "middle",
        [((rows, d), F32), ((rows, d), BF16), ((rows, d // 2), BF16)]
        + [((rows, width), BF16)] * 4
        + [((8, d), F32)],
        me,
        [*p, middle, g0, gains, w_out, *w_out_other],
        cost(2 * rows * d * d, 12e6),
    )
    b = exchange_four([b0, b1, b2, b3])
    o_both = add(o[2], after(o3, mlow))
    flat = lambda x: x.reshape(4 * rows, -1)
    qb = q
    if ring:
        low_beside = seq_permute(mhalf, 1)
        out_part = vmem_call(
            out_grad_kernel,
            "out_grad",
            [((n // 2, d // 2 + 8, share), BF16)] * 2,
            place3[0],
            [*m, mixed_beside, mlow, low_beside, ggrad_second],
            cost(2 * rows * d * d, 6e6),
            [pltpu.VMEM((d // 2, d), F32)],
        )
        (up_part,) = unit_grads([(up_near, after(up_far, out_part[0]))], (*s0, *s1, *s2, *s3))
        b[1:] = all_after(b[1:], up_part[0], o_both)
        down_sent = fsdp_send(after(down_both, b[2], b[3]))
    else:
        (up_part,) = unit_grads([(up_near, up_far)], (*s0, *s1, *s2, *s3))

    def qkv_grads(d_a, d_b):
        if ring:
            return vmem_call(
                qkv_grad_kernel,
                "qkv_grad",
                [((n // 2, 6 * pair + 8, share), BF16)] * 2,
                place3[0],
                [flat(normed), flat(d_a), flat(d_b), w_qkv],
                cost(2 * 4 * rows * d * 6 * pair, 6e6),
                [pltpu.VMEM((6 * pair, d), F32)],
            )
        whole = tn(jnp.concatenate([flat(d_a), flat(d_b)], axis=1), flat(normed))
        starts = [i * width + part * pair for part in range(2) for i in range(3)]
        w = jnp.concatenate([w_qkv[i : i + pair] for i in starts]).astype(F32)
        gain_part = jnp.sum(whole * w, axis=0, keepdims=True) / gains[:1].astype(F32)
        whole = jnp.concatenate([whole, gain_part, jnp.zeros((7, d), F32)]).astype(BF16)
        return (jnp.transpose(whole.reshape(6 * pair + 8, n, share), (1, 0, 2)),)

    d_a, v_a = attention_back(0, me, qb, k, v, b, lse_a, cosine, sine)
    o2 = seq_permute(after(o_both, d_a), 2)
    qb = after(qb, d_a)
    if ring:
        gate_both = add(gate_part[0], after(gate_crossed, d_a))
        down_share = add(*all_after(down_sent, d_a))
        gate_sent = fsdp_send(after(gate_both, down_share))
        up_crossed = fsdp_permute(after(up_part[1], gate_both), 1)
        qb = after(qb, gate_both, down_share)
    d_b, v_b = attention_back(1, me, qb, k, v, b, lse_b, cosine, sine, v_a)
    o2 = after(o2, d_b)
    d_b = after(d_b, o2)
    if ring:
        up_crossed, *gate_sent = all_after([up_crossed] + gate_sent, d_b)
        up_both = add(up_part[0], up_crossed)
        gate_share = add(*gate_sent)
        up_sent = fsdp_send(after(up_both, gate_share))
        out_crossed = fsdp_permute(after(out_part[1], up_both), 1)
        d_b = after(d_b, up_both, gate_share)

    nb3, nb2, nb1 = vmem_call(
        normed_back_kernel,
        "normed_back",
        [((rows, d), BF16)] * 3,
        me,
        [d_a, d_b, w_qkv],
        cost(2 * 3 * rows * d * 3 * width, 8e6),
    )
    nb_both = add(nb2, seq_permute(nb3, 1))
    beside = seq_permute(nb1, 1)
    crossed_far = seq_permute(nb_both, 2)
    qkv_sums = qkv_grads(d_a, after(d_b, nb_both, beside))
    output = add(middle, o[0], o1, o2)[None]
    crossed_far = after(crossed_far, qkv_sums[0], output)
    if ring:
        out_both = add(out_part[0], after(out_crossed, qkv_sums[0]))
        qkv_crossed = fsdp_permute(after(qkv_sums[1], out_both), 1)
        up_share = add(*all_after(up_sent, qkv_sums[0]))
        out_sent = fsdp_send(after(out_both, up_share))
        beside = after(beside, up_share)
        units_sent = jnp.concatenate([gate_share, up_share, down_share], axis=0)
        units_far = seq_permute(units_sent, 2)
    (tokens_grad,) = vmem_call(
        final_kernel,
        "final",
        [((rows, d), F32)],
        me,
        [beside, crossed_far, d_a, d_b, w_qkv, t0, gains, mback],
        cost(0, 6e6),
    )
    if ring:
        units_far = after(units_far, tokens_grad)
        qkv_both = add(qkv_sums[0], after(qkv_crossed, tokens_grad))
        out_share = add(*all_after(out_sent, tokens_grad))
        qkv_sent = fsdp_send(after(qkv_both, out_share))
    else:
        gate_share, up_share, down_share, qkv_share = (
            scatter_whole(v[0]) for v in (gate_part, up_part, down_part, qkv_sums)
        )
        mixed_rows = jnp.zeros((rows, d), BF16)
        for r in range(4):
            mixed_rows = lax.dynamic_update_slice(mixed_rows, m[r], (0, (s ^ r) * width))
        out_part = tn(mlow, mixed_rows)
        halves = [lax.dynamic_slice_in_dim(out_part, (core ^ j) * (d // 2), d // 2) for j in range(2)]
        keep = jnp.concatenate([halves[0], ggrad_second]).reshape(d // 2 + 8, n, share)
        send = jnp.pad(halves[1], ((0, 8), (0, 0))).astype(BF16).reshape(d // 2 + 8, n, share)
        whole = (keep + seq_permute(send, 1).astype(F32)).astype(BF16)
        out_share = scatter_whole(jnp.transpose(whole, (1, 0, 2)))
        units_sent = jnp.concatenate([gate_share, up_share, down_share], axis=0)
    if not ring:
        units_far = seq_permute(units_sent, 2)
    units_all = [units_sent, seq_permute(units_sent, 1), units_far, seq_permute(units_far, 1)]
    v_all = lax.all_to_all(after(v_b, tokens_grad), "seq", split_axis=0, concat_axis=0)
    (values_grad,) = vmem_call(
        place_values_kernel, "place_values", [((rows, d), F32)], me, [v_all], cost(0, 3e6)
    )
    gate_grad, up_grad, down_grad = vmem_call(
        place_units_kernel,
        "place_units",
        [((share, 4 * units), F32)] * 3,
        me,
        units_all,
        cost(0, 3e6),
        [pltpu.VMEM((4, 3 * units, share), F32)],
    )
    if ring:
        out_far = after(seq_permute(after(out_share, qkv_both), 2), gate_grad)
    else:
        out_far = seq_permute(out_share, 2)
    out_share = add(out_share, out_far)
    out_grad, second_gain_grad = vmem_call(
        place_out_kernel,
        "place_out",
        [((share, d), F32), ((1, share), F32)],
        me,
        [out_share, seq_permute(out_share, 1)],
        cost(0, 1e6),
    )
    if ring:
        qkv_share = add(*all_after(qkv_sent, out_grad, gate_grad, values_grad))
    qkv_far = seq_permute(qkv_share, 2)
    qkv_all = [qkv_share, seq_permute(qkv_share, 1), qkv_far, seq_permute(qkv_far, 1)]
    query_grad, key_grad, value_grad, gain_grad = vmem_call(
        place_qkv_kernel,
        "place_qkv",
        [((share, d), F32)] * 3 + [((1, share), F32)],
        me,
        qkv_all,
        cost(0, 3e6),
    )
    return (
        output,
        tokens_grad[None],
        values_grad[None],
        gain_grad.reshape(share),
        query_grad,
        key_grad,
        value_grad,
        out_grad,
        second_gain_grad.reshape(share),
        gate_grad,
        up_grad,
        down_grad,
    )


def solution(mesh):
    rows = P("fsdp", "seq", None)
    weight = P("fsdp", None)
    gain = P("fsdp")
    in_specs = (rows,) * 3 + (gain,) + (weight,) * 4 + (gain,) + (weight,) * 3
    out_specs = (rows,) * 3 + (gain,) + (weight,) * 4 + (gain,) + (weight,) * 3
    return jax.shard_map(
        per_device, mesh=mesh, in_specs=in_specs, out_specs=out_specs, check_vma=False
    )
```

```python
import functools
import math

import jax
import jax.numpy as jnp
from jax import lax
from jax.experimental import pallas as pl
from jax.experimental.pallas import tpu as pltpu
from jax.sharding import PartitionSpec as P

HEADS = 16
HEAD_DIM = 64
GROUPS = 4
EPSILON = 1e-06
NEGATIVE = -1e30
F32 = jnp.float32
BF16 = jnp.bfloat16
PARAMS = pltpu.CompilerParams(vmem_limit_bytes=56 * 2**20)


def nn(a, b):
    return lax.dot_general(a, b, (((1,), (0,)), ((), ())), preferred_element_type=F32)


def nt(a, b):
    return lax.dot_general(a, b, (((1,), (1,)), ((), ())), preferred_element_type=F32)


def tn(a, b):
    return lax.dot_general(a, b, (((0,), (0,)), ((), ())), preferred_element_type=F32)


def cost(flops, nbytes, trans=0):
    flops, nbytes, trans = 1, 1, 0
    return pl.CostEstimate(flops=int(flops), bytes_accessed=int(nbytes), transcendentals=int(trans))


def turn(u, cosine, sine):
    lane = lax.broadcasted_iota(jnp.int32, (u.shape[0], 128), 1)
    first = lane % HEAD_DIM < HEAD_DIM // 2
    parts = []
    for j in range(u.shape[1] // 128):
        part = u[:, 128 * j : 128 * (j + 1)]
        other = jnp.where(first, pltpu.roll(part, 96, 1), pltpu.roll(part, 32, 1))
        parts.append(part * cosine + other * sine)
    return jnp.concatenate(parts, axis=1)


def inverse_rms(v):
    return lax.rsqrt(jnp.mean(v * v, axis=-1, keepdims=True) + EPSILON)


ANY = pl.BlockSpec(memory_space=pl.ANY)


def qkv_kernel(count, me, t0, f0, p1, p2, p3, *refs):
    pieces, rest = refs[:count], refs[count:]
    cosine, sine, q, k, v, n, w, wo, tv, fv, sems = rest
    width = q.shape[-1]
    d = tv.shape[-1]
    share = d // count
    first, last = [], []
    for i, piece in enumerate(pieces):
        at = pl.ds(pl.multiple_of((me[0] ^ i) * share, share), share)
        first.append(pltpu.make_async_copy(piece.at[: w.shape[0]], w.at[:, at], sems.at[8 + i]))
        last.append(pltpu.make_async_copy(piece.at[w.shape[0] :], wo.at[:, at], sems.at[16 + i]))
    loads = [(t0, f0)] + [(p.at[:, :d], p.at[:, d : d + width]) for p in (p1, p2, p3)]
    copies = []
    for i, (t, f) in enumerate(loads):
        copies.append(pltpu.make_async_copy(t, tv.at[i], sems.at[2 * i]))
        copies.append(pltpu.make_async_copy(f, fv.at[i], sems.at[2 * i + 1]))
    for copy in copies[:2] + first + copies[2:] + last:
        copy.start()
    for i in range(4):
        copies[2 * i].wait()
        if i == 0:
            for copy in first:
                copy.wait()
        gain = w[3 * width : 3 * width + 1].astype(F32)
        x = tv[i].astype(F32)
        normed = (x * inverse_rms(x) * gain).astype(BF16)
        n[i] = normed
        u = nt(normed, w[: 3 * width])
        c, s = cosine[i], sine[i]
        q[i] = (turn(u[:, :width], c, s).astype(BF16).astype(F32) * 0.125).astype(BF16)
        k[i] = turn(u[:, width : 2 * width], c, s).astype(BF16)
        copies[2 * i + 1].wait()
        v[i] = (0.5 * u[:, 2 * width :] + 0.5 * fv[i].astype(F32)).astype(BF16)
    for copy in last:
        copy.wait()


def qkv(where, t, f, packed, pieces, cosine, sine):
    rows, d = t.shape
    width = f.shape[1]
    full = lambda *shape: pl.BlockSpec(shape, lambda i, me: (0,) * len(shape))
    main = 3 * width + 8
    shapes = [(4, rows, width)] * 3 + [(4, rows, d), (main, d), (pieces[0].shape[0] - main, d)]
    return pl.pallas_call(
        functools.partial(qkv_kernel, len(pieces)),
        grid_spec=pltpu.PrefetchScalarGridSpec(
            num_scalar_prefetch=1,
            grid=(1,),
            in_specs=[ANY] * (5 + len(pieces)) + [full(4, rows, 128)] * 2,
            out_specs=[full(*s) for s in shapes],
            scratch_shapes=[
                pltpu.VMEM((4, rows, d), BF16),
                pltpu.VMEM((4, rows, width), BF16),
                pltpu.SemaphoreType.DMA((24,)),
            ],
        ),
        out_shape=[jax.ShapeDtypeStruct(s, BF16) for s in shapes],
        compiler_params=PARAMS,
        cost_estimate=cost(2 * 4 * rows * d * 3 * width, 12e6),
        name="qkv",
    )(where.reshape(1), t, f, *packed, *pieces, cosine, sine)


def attn_kernel(me, q, k, v, *refs):
    before, (o0, o1, o2, o3, lse, o) = refs[:-6], refs[-6:]
    h = pl.program_id(0)
    rows, width = q.shape[1:]
    mine = lax.broadcasted_iota(jnp.int32, (1, width), 1) // HEAD_DIM == h
    row = lax.broadcasted_iota(jnp.int32, (rows, rows), 0)
    col = lax.broadcasted_iota(jnp.int32, (rows, rows), 1)
    s = me[0]
    for i in range(GROUPS):
        ri = i ^ s
        qi = jnp.where(mine, q[ri], jnp.zeros((), BF16))
        tiles = []
        for j in range(i + 1):
            tile = nt(qi, k[j ^ s])
            if j == i:
                tile = jnp.where(col <= row, tile, NEGATIVE)
            tiles.append(tile)
        largest = tiles[0].max(axis=1, keepdims=True)
        for tile in tiles[1:]:
            largest = jnp.maximum(largest, tile.max(axis=1, keepdims=True))
        tiles = [jnp.exp(tile - largest) for tile in tiles]
        total = tiles[0].sum(axis=1, keepdims=True)
        for tile in tiles[1:]:
            total = total + tile.sum(axis=1, keepdims=True)
        inverse = 1.0 / total
        acc = jnp.zeros((rows, width), F32)
        for j in range(i + 1):
            acc = acc + nn((tiles[j] * inverse).astype(BF16), v[j ^ s])
        o[ri] = jnp.where(mine, acc.astype(BF16), o[ri])
        stat = jnp.broadcast_to(largest + jnp.log(total), (rows, 128))
        lse[0, i] = jnp.transpose(stat)[:8]

    @pl.when(h == pl.num_programs(0) - 1)
    def _():
        for r, out in enumerate((o0, o1, o2, o3)):
            if before:
                out[:, :width] = before[r][...]
                out[:, width:] = o[r]
            else:
                out[...] = o[r]


def attention(part, me, q, k, v, *before):
    rows = q.shape[1]
    width = 2 * HEAD_DIM
    full = lambda *shape: pl.BlockSpec(shape, lambda h, me: (0,) * len(shape))
    pair = pl.BlockSpec((4, rows, width), lambda h, me: (0, 0, part))
    both = (rows, 2 * width if before else width)
    return pl.pallas_call(
        attn_kernel,
        grid_spec=pltpu.PrefetchScalarGridSpec(
            num_scalar_prefetch=1,
            grid=(2,),
            in_specs=[pair] * 3 + [full(*one.shape) for one in before],
            out_specs=[full(*both)] * 4
            + [pl.BlockSpec((1, 4, 8, rows), lambda h, me: (h, 0, 0, 0))],
            scratch_shapes=[pltpu.VMEM((4, rows, width), BF16)],
        ),
        out_shape=[jax.ShapeDtypeStruct(both, BF16)] * 4
        + [jax.ShapeDtypeStruct((2, 4, 8, rows), F32)],
        compiler_params=PARAMS,
        cost_estimate=cost(2 * 2 * 10 * rows * rows * width * 4, 4e6, 20 * rows * rows),
        name="attention",
    )(me, q, k, v, *before)


def attn_back_kernel(me, q, k, v, b0, b1, b2, b3, lse, cosine, sine, *rest):
    before, (out, vout, do, dq, dk, dv) = rest[:-6], rest[-6:]
    h = pl.program_id(0)
    rows, width = q.shape[1:]
    mine = lax.broadcasted_iota(jnp.int32, (1, width), 1) // HEAD_DIM == h
    key = lax.broadcasted_iota(jnp.int32, (rows, rows), 0)
    query = lax.broadcasted_iota(jnp.int32, (rows, rows), 1)
    s = me[0]
    zero = jnp.zeros((), BF16)

    @pl.when(h == 0)
    def _():
        for r, b in enumerate((b0, b1, b2, b3)):
            do[r] = b[...]
        dq[...] = jnp.zeros_like(dq)
        dk[...] = jnp.zeros_like(dk)
        dv[...] = jnp.zeros_like(dv)

    for i in range(GROUPS):
        qi = jnp.where(mine, q[i ^ s], zero)
        doi = jnp.where(mine, do[i ^ s], zero)
        stat = lse[0, i][:1]
        soft, back = [], []
        dot = jnp.zeros((1, rows), F32)
        for j in range(i + 1):
            tile = nt(k[j ^ s], qi)
            if j == i:
                tile = jnp.where(key <= query, tile, NEGATIVE)
            p = jnp.exp(tile - stat)
            dp = nt(v[j ^ s], doi)
            dot = dot + jnp.sum(p * dp, axis=0, keepdims=True)
            soft.append(p)
            back.append(dp)
        acc = jnp.zeros((rows, width), F32)
        for j in range(i + 1):
            ds = (soft[j] * (back[j] - dot)).astype(BF16)
            dk[j] += nn(ds, qi)
            dv[j] += nn(soft[j].astype(BF16), doi)
            acc = acc + tn(ds, jnp.where(mine, k[j ^ s], zero))
        dq[i] += acc

    @pl.when(h == pl.num_programs(0) - 1)
    def _():
        for i in range(GROUPS):
            ri = i ^ s
            c, n = cosine[ri], -sine[ri]
            out[ri, :, :width] = turn(dq[i] * 0.125, c, n).astype(BF16)
            out[ri, :, width : 2 * width] = turn(dk[i], c, n).astype(BF16)
            half = (0.5 * dv[i]).astype(BF16)
            out[ri, :, 2 * width :] = half
            vout[i, :, len(before) * width :] = half
            if before:
                vout[i, :, :width] = before[0][i]


def attention_back(part, me, q, k, v, b, lse, cosine, sine, *before):
    rows = q.shape[1]
    width = 2 * HEAD_DIM
    full = lambda *shape: pl.BlockSpec(shape, lambda h, me: (0,) * len(shape))
    pair = pl.BlockSpec((4, rows, width), lambda h, me: (0, 0, part))
    return pl.pallas_call(
        attn_back_kernel,
        grid_spec=pltpu.PrefetchScalarGridSpec(
            num_scalar_prefetch=1,
            grid=(2,),
            in_specs=[pair] * 3
            + [pl.BlockSpec((rows, width), lambda h, me: (0, part))] * 4
            + [pl.BlockSpec((1, 4, 8, rows), lambda h, me: (h, 0, 0, 0))]
            + [full(4, rows, 128)] * 2
            + [full(*one.shape) for one in before],
            out_specs=[full(4, rows, 3 * width), full(4, rows, (1 + len(before)) * width)],
            scratch_shapes=[pltpu.VMEM((4, rows, width), BF16)]
            + [pltpu.VMEM((4, rows, width), F32)] * 3,
        ),
        out_shape=[
            jax.ShapeDtypeStruct((4, rows, 3 * width), BF16),
            jax.ShapeDtypeStruct((4, rows, (1 + len(before)) * width), BF16),
        ],
        compiler_params=PARAMS,
        cost_estimate=cost(5 * 2 * 10 * rows * rows * width * 4, 4e6, 20 * rows * rows),
        name="attention_back",
    )(me, q, k, v, *b, lse, cosine, sine, *before)


def out_kernel(me, m0, m1, m2, m3, w0, x0, x1, x2, x3, t, gains, middle, lo, hi):
    s = me[0]
    width = m0.shape[1]
    quarter = x0.shape[0]
    first = w0.shape[0] - 4 * quarter
    ws = [[w0.at[first + i * quarter : first + (i + 1) * quarter] for i in range(4)], [x0, x1, x2, x3]]
    for j in range(2):
        for i, w in enumerate(ws[j]):
            start = ((s % 2) ^ j) * 4 * quarter + i * quarter
            cols = pl.ds(pl.multiple_of(start, quarter), quarter)
            part = None
            for r, m in enumerate((m0, m1, m2, m3)):
                one = nt(m[...], w[:, pl.ds(pl.multiple_of((s ^ r) * width, width), width)])
                part = one if part is None else part + one
            middle[:, cols] = t[:, cols].astype(F32) + part
    acc = middle[...]
    second = (acc * inverse_rms(acc) * gains[1:2].astype(F32)).astype(BF16)
    lo[...] = second[: lo.shape[0]]
    hi[...] = second[lo.shape[0] :]


def vmem_call(kernel, name, shapes, me, args, estimate, scratch=()):
    full = lambda shape: pl.BlockSpec(shape, lambda i, me: (0,) * len(shape))
    outs = [jax.ShapeDtypeStruct(s, t) for s, t in shapes]
    return pl.pallas_call(
        kernel,
        grid_spec=pltpu.PrefetchScalarGridSpec(
            num_scalar_prefetch=1,
            grid=(1,),
            in_specs=[full(a.shape) for a in args],
            out_specs=[full(s) for s, _ in shapes],
            scratch_shapes=scratch,
        ),
        out_shape=outs,
        compiler_params=PARAMS,
        cost_estimate=estimate,
        name=name,
    )(me, *args)


def mlp_kernel(count, me, sa0, sa1, sb0, sb1, ga, gb, *refs):
    pieces, outs = refs[: 3 * count], refs[3 * count : 3 * count + 5]
    sv, gv, wv, hid, gback, uback, sback, sems = refs[3 * count + 5 :]
    _, units, d = wv.shape
    rows = ga.shape[0]
    copies = [pltpu.make_async_copy(sa0, sv.at[0, : rows // 2], sems.at[0])]
    copies.append(pltpu.make_async_copy(sa1, sv.at[0, rows // 2 :], sems.at[1]))
    parts = []
    for h in range(3):
        loads = []
        if count == 1:
            loads.append((pieces[h], wv.at[h]))
        else:
            share = d // 8
            for k in range(4):
                mine, other = pieces[h * count + k], pieces[h * count + 4].at[k * units : (k + 1) * units]
                for piece, flip in ((mine, 2 * k), (other, 2 * k + 1)):
                    at = pl.ds(pl.multiple_of((me[0] ^ flip) * share, share), share)
                    loads.append((piece, wv.at[h, :, at]))
        sem = lambda i, h=h: sems.at[15 + 8 * h + i]
        parts.append([pltpu.make_async_copy(a, b, sem(i)) for i, (a, b) in enumerate(loads)])
    copies.append(pltpu.make_async_copy(ga, gv.at[0], sems.at[4]))
    copies.append(pltpu.make_async_copy(sb0, sv.at[1, : rows // 2], sems.at[2]))
    copies.append(pltpu.make_async_copy(sb1, sv.at[1, rows // 2 :], sems.at[5]))
    copies.append(pltpu.make_async_copy(gb, gv.at[1], sems.at[6]))
    for copy in copies[:2] + parts[0] + parts[1] + copies[2:3] + parts[2] + copies[3:]:
        copy.start()
    writes = []

    def write(buf, out):
        copy = pltpu.make_async_copy(buf, out, sems.at[7 + len(writes)])
        copy.start()
        writes.append(copy)

    for i in range(2):
        copies[3 if i else 0].wait()
        copies[4 if i else 1].wait()
        if i == 0:
            for copy in parts[0]:
                copy.wait()
        gate = nt(sv[i], wv[0])
        if i == 0:
            for copy in parts[1]:
                copy.wait()
        up = nt(sv[i], wv[1])
        sg = jax.nn.sigmoid(gate)
        act = gate * sg
        hid[i] = (act * up).astype(BF16)
        at = slice(i * rows, (i + 1) * rows)
        write(hid.at[i], outs[0].at[at])
        copies[5 if i else 2].wait()
        if i == 0:
            for copy in parts[2]:
                copy.wait()
        hb = nt(gv[i], wv[2])
        gate_back = (hb * up * sg * (1.0 + gate * (1.0 - sg))).astype(BF16)
        up_back = (hb * act).astype(BF16)
        gback[i] = gate_back
        write(gback.at[i], outs[1].at[at])
        uback[i] = up_back
        write(uback.at[i], outs[2].at[at])
        sback[i] = (nn(gate_back, wv[0]) + nn(up_back, wv[1])).astype(BF16)
        write(sback.at[i], outs[3 + i])
    for copy in writes:
        copy.wait()


def any_call(kernel, name, shapes, me, args, estimate, scratch):
    return pl.pallas_call(
        kernel,
        grid_spec=pltpu.PrefetchScalarGridSpec(
            num_scalar_prefetch=1,
            grid=(1,),
            in_specs=[ANY] * len(args),
            out_specs=[ANY] * len(shapes),
            scratch_shapes=scratch,
        ),
        out_shape=[jax.ShapeDtypeStruct(s, t) for s, t in shapes],
        compiler_params=PARAMS,
        cost_estimate=estimate,
        name=name,
    )(me, *args)


def mlp(where, sa, sb, ga, gb, pieces):
    rows, d = ga.shape
    units = pieces[0][0].shape[0]
    part = ((2 * rows, units), BF16)
    return any_call(
        functools.partial(mlp_kernel, len(pieces[0])),
        "mlp",
        [part] * 3 + [((rows, d), BF16)] * 2,
        where.reshape(1),
        [*sa, *sb, ga, gb] + [one for some in pieces for one in some],
        cost(2 * 5 * 2 * rows * d * units, 12e6, 2 * rows * units),
        [pltpu.VMEM((2, rows, d), BF16)] * 2
        + [pltpu.VMEM((3, units, d), BF16)]
        + [pltpu.VMEM((2, rows, units), BF16)] * 3
        + [pltpu.VMEM((2, rows, d), BF16), pltpu.SemaphoreType.DMA((39,))],
    )


def mlp_out_kernel(count, me, hn, hf, *refs):
    pieces, outs, w = refs[:count], refs[count : count + 4], refs[-1]
    units, d = w.shape
    rows = outs[0].shape[0]
    if count == 1:
        w[...] = pieces[0][...]
    else:
        share = d // 8
        for k in range(4):
            for piece, flip in ((pieces[k], 2 * k), (pieces[4].at[k * units : (k + 1) * units], 2 * k + 1)):
                w[:, pl.ds(pl.multiple_of((me[0] ^ flip) * share, share), share)] = piece[...]
    for h, pair in ((hn, outs[:2]), (hf, outs[2:])):
        for i, out in enumerate(pair):
            out[...] = nn(h[i * rows : (i + 1) * rows], w[...]).astype(BF16)


def unit_grad_kernel(count, me, *refs):
    ins, outs, acc = refs[: -1 - 2 * count], refs[-1 - 2 * count : -1], refs[-1]
    blocks = [block[...] for block in ins[2 * count :]]
    y = me[0] % 2
    near = jnp.concatenate(blocks[: len(blocks) // 2], axis=0)
    far = jnp.concatenate(blocks[len(blocks) // 2 :], axis=0)
    share = outs[0].shape[2]
    for i in range(count):
        acc[...] = tn(ins[2 * i][...], near) + tn(ins[2 * i + 1][...], far)
        for z in range(outs[0].shape[0]):
            for j in range(2):
                at = pl.multiple_of((2 * z + (y ^ j)) * share, share)
                outs[2 * i + j][z] = acc[:, pl.ds(at, share)].astype(BF16)


def unit_grads(pairs, blocks):
    n = lax.axis_size("fsdp")
    units, d = pairs[0][0].shape[1], blocks[0].shape[1]
    if n != 8:
        half = len(blocks) // 2
        near, far = jnp.concatenate(blocks[:half]), jnp.concatenate(blocks[half:])
        outs = [(tn(a, near) + tn(b, far)).astype(BF16) for a, b in pairs]
        return [(jnp.transpose(o.reshape(units, n, d // n), (1, 0, 2)),) for o in outs]
    me = lax.axis_index("fsdp").astype(jnp.int32).reshape(1)
    outs = vmem_call(
        functools.partial(unit_grad_kernel, len(pairs)),
        "unit_grads",
        [((n // 2, units, d // n), BF16)] * (2 * len(pairs)),
        me,
        [a for pair in pairs for a in pair] + list(blocks),
        cost(1, 1),
        [pltpu.VMEM((units, d), F32)],
    )
    return [outs[2 * i : 2 * i + 2] for i in range(len(pairs))]


def out_grad_kernel(me, m0, m1, m2, m3, beside, low, low_beside, gain, mine, other, acc):
    s, y = me[0], me[1] % 2
    width = m0.shape[1]
    half = acc.shape[0]
    low_here = low[:, pl.ds(pl.multiple_of((s % 2) * half, half), half)]
    for r, m in enumerate((m0, m1, m2, m3)):
        cols = pl.ds(pl.multiple_of((s ^ r) * width, width), width)
        theirs = beside[:, (r ^ 1) * width : ((r ^ 1) + 1) * width]
        acc[:, cols] = tn(low_here, m[...]) + tn(low_beside[...], theirs)
    share = mine.shape[2]
    for j, out in enumerate((mine, other)):
        for z in range(out.shape[0]):
            cols = pl.ds(pl.multiple_of((2 * z + (y ^ j)) * share, share), share)
            out[z, :half] = acc[:, cols].astype(BF16)
            out[z, half:] = gain[:, cols].astype(BF16)


def qkv_grad_kernel(me, normed, da, db, w, mine, other, acc):
    y = me[1] % 2
    share = mine.shape[2]
    pair = da.shape[1] // 3
    total = jnp.zeros((1, acc.shape[1]), F32)
    for part, dd in enumerate((da, db)):
        acc[3 * part * pair : 3 * (part + 1) * pair] = tn(dd[...], normed[...])
        for i in range(3):
            one = acc[(3 * part + i) * pair : (3 * part + i + 1) * pair]
            rows = w[(2 * i + part) * pair : (2 * i + part + 1) * pair].astype(F32)
            total = total + jnp.sum(one * rows, axis=0, keepdims=True)
    total = total / w[6 * pair : 6 * pair + 1].astype(F32)
    for j, out in enumerate((mine, other)):
        for z in range(mine.shape[0]):
            cols = pl.ds(pl.multiple_of((2 * z + (y ^ j)) * share, share), share)
            out[z, : 6 * pair] = acc[:, cols].astype(BF16)
    for f in range(acc.shape[1] // share):
        row = jnp.broadcast_to(total[:, f * share : (f + 1) * share], (8, share)).astype(BF16)
        for j, out in enumerate((mine, other)):

            @pl.when((f % 2) == (y ^ j))
            def _():
                out[f // 2, 6 * pair :] = row


def joined(r, da, db):
    pair = da.shape[2] // 3
    parts = [d[r, :, j * pair : (j + 1) * pair] for j in range(3) for d in (da, db)]
    return jnp.concatenate(parts, axis=1)


def normed_back_kernel(me, da, db, w, n3, n2, n1):
    for r, out in ((3, n3), (2, n2), (1, n1)):
        out[...] = nn(joined(r, da, db), w[: 2 * da.shape[2]]).astype(BF16)


def place_values_kernel(me, v, out):
    width = v.shape[2]
    for j in range(GROUPS):
        out[:, j * width : (j + 1) * width] = v[j].astype(F32)


def place_qkv_kernel(me, p0, p1, p2, p3, oq, ok, ov, gain):
    s = me[0]
    size = (p0.shape[0] - 8) // 6
    share = p0.shape[1]
    total = jnp.zeros((8, share), F32)
    for r, piece in enumerate((p0, p1, p2, p3)):
        for p in range(2):
            start = p * 3 * size
            at = pl.multiple_of((s ^ r) * 2 * size + p * size, size)
            for i, out in enumerate((oq, ok, ov)):
                block = piece[start + i * size : start + (i + 1) * size]
                out[:, pl.ds(at, size)] = jnp.transpose(block.astype(F32))
        total = total + piece[6 * size :].astype(F32)
    gain[...] = total[:1]


def place_units_kernel(me, p0, p1, p2, p3, *refs):
    outs, buf = refs[:-1], refs[-1]
    s = me[0]
    units = p0.shape[0] // len(outs)
    for r, p in enumerate((p0, p1, p2, p3)):
        buf[s ^ r] = p[...].astype(F32)
    for i, out in enumerate(outs):
        for j in range(GROUPS):
            out[:, j * units : (j + 1) * units] = jnp.transpose(buf[j, i * units : (i + 1) * units])


def place_out_kernel(me, own, other, out, gain):
    core = me[0] % 2
    half = own.shape[0] - 8
    for j, piece in enumerate((own, other)):
        at = pl.multiple_of((core ^ j) * half, half)
        out[:, pl.ds(at, half)] = jnp.transpose(piece[:half].astype(F32))
    gain[...] = own[half : half + 1].astype(F32) + other[half : half + 1].astype(F32)


def middle_kernel(me, p0, p1, p2, middle, g, gains, w0, x0, x1, x2, x3, mback, mlow, mhalf, b0, b1, b2, b3, ggrad):
    s = me[0]
    width = b0.shape[1]
    dn = p0[...].astype(F32) + p1[...].astype(F32) + p2[...].astype(F32)
    v = middle[...]
    r = inverse_rms(v)
    x = v * r
    ggrad[...] = jnp.broadcast_to(jnp.sum(dn * x, axis=0, keepdims=True), ggrad.shape)
    dx = dn * gains[1:2].astype(F32)
    total = g[...].astype(F32) + r * (dx - x * jnp.mean(dx * x, axis=-1, keepdims=True))
    mback[...] = total
    mlow[...] = total.astype(BF16)
    half = 4 * x0.shape[0]
    lows = [mlow[:, pl.ds(pl.multiple_of(((s % 2) ^ j) * half, half), half)] for j in range(2)]
    mhalf[...] = lows[1]
    for i, b in enumerate((b0, b1, b2, b3)):
        cols = pl.ds(pl.multiple_of((s ^ i) * width, width), width)
        w1 = jnp.concatenate([x[:, cols] for x in (x0, x1, x2, x3)], axis=0)
        b[...] = (nn(lows[0], w0[w0.shape[0] - half :, cols]) + nn(lows[1], w1)).astype(BF16)


def final_kernel(me, p1, p2, da, db, w, t, gains, mback, out):
    dn = nn(joined(0, da, db), w[: 2 * da.shape[2]])
    dn = dn + p1[...].astype(F32) + p2[...].astype(F32)
    v = t[...].astype(F32)
    r = inverse_rms(v)
    x = v * r
    dx = dn * gains[:1].astype(F32)
    out[...] = mback[...] + r * (dx - x * jnp.mean(dx * x, axis=-1, keepdims=True))


def after(value, *others):
    return lax.optimization_barrier((value,) + others)[0]


def all_after(values, *others):
    return list(lax.optimization_barrier(tuple(values) + others)[: len(values)])


def add(*terms):
    return sum((term.astype(F32) for term in terms[1:]), terms[0].astype(F32)).astype(BF16)


def seq_permute(value, flip):
    return lax.ppermute(value, "seq", [(i, i ^ flip) for i in range(GROUPS)])


def gather_four(own):
    near = seq_permute(own, 1)
    far = seq_permute(own, 2)
    return own, near, far, seq_permute(far, 1)


def exchange_four(pieces):
    return [pieces[0]] + [seq_permute(pieces[r], r) for r in (1, 2, 3)]


def fsdp_permute(value, flip):
    n = lax.axis_size("fsdp")
    return lax.ppermute(value, "fsdp", [(i, i ^ flip) for i in range(n)])


def fsdp_send(both):
    z = lax.axis_index("fsdp") // 2
    parts = [lax.dynamic_index_in_dim(both, z ^ k, 0, keepdims=False) for k in range(both.shape[0])]
    return [parts[0]] + [fsdp_permute(parts[k], 2 * k) for k in range(1, len(parts))]


def scatter_whole(parts):
    return lax.psum_scatter(parts, "fsdp", scatter_dimension=0, tiled=False)


def per_device(
    tokens,
    first_values,
    cotangent,
    first_gain,
    query_weight,
    key_weight,
    value_weight,
    out_weight,
    second_gain,
    gate_weight,
    up_weight,
    down_weight,
):
    n = lax.axis_size("fsdp")
    s = lax.axis_index("seq").astype(jnp.int32)
    me = s.reshape(1)
    place3 = [jnp.stack([s, lax.axis_index("fsdp").astype(jnp.int32), jnp.int32(p)]) for p in (0, 1)]
    t0, g0, f0 = tokens[0], cotangent[0], first_values[0]
    rows, d = t0.shape
    width = d // GROUPS
    pair = width // 2
    units = gate_weight.shape[1] // GROUPS
    share = d // n
    core = s % 2
    ring = n == 8

    def columns(v, which, size):
        return lax.dynamic_slice_in_dim(v, which * size, size, 1)

    here = lax.axis_index("fsdp").astype(jnp.int32)
    gains = jnp.concatenate([first_gain[None], second_gain[None], jnp.zeros((6, share), BF16)])
    qkv_weights = (query_weight, key_weight, value_weight)
    own_qkv = [columns(w, s, width).T for w in qkv_weights]
    own_qkv += [gains, columns(out_weight, core, d // 2).T]
    own_qkv = jnp.concatenate(own_qkv, axis=0)
    own_units = [columns(w, s, units).T for w in (gate_weight, up_weight, down_weight)]
    places = (jnp.arange(4, dtype=jnp.int32) ^ s)[:, None] * rows + jnp.arange(rows, dtype=jnp.int32)
    half_dim = HEAD_DIM // 2
    freqs = jnp.exp(jnp.arange(half_dim, dtype=F32) * (-2.0 * math.log(10000.0) / HEAD_DIM))
    angles = places.astype(F32)[:, :, None] * jnp.tile(freqs, 4)
    sign = jnp.tile(jnp.repeat(jnp.array([-1.0, 1.0], F32), half_dim), 2)
    cosine, sine = jnp.cos(angles), jnp.sin(angles) * sign
    f = [columns(f0, s ^ r, width) for r in range(4)]
    if ring:
        first = [fsdp_permute(own_qkv, flip) for flip in (6, 4, 2)][::-1]
        first_y = fsdp_permute(own_qkv, 1)
    packed2 = seq_permute(jnp.concatenate([t0, f[2], f[3]], axis=1), 2)
    if ring:
        pieces = [own_qkv, first_y]
        for i in range(3):
            one = after(first[i], cosine, sine, *own_units) if i == 0 else first[i]
            pieces += [one, fsdp_permute(one, 1)]
    else:
        pieces = [lax.all_gather(own_qkv, "fsdp", axis=1, tiled=True)]
        unit_pieces = [[lax.all_gather(w, "fsdp", axis=1, tiled=True)] for w in own_units]
    where = here if ring else jnp.int32(0)
    packed1 = seq_permute(jnp.concatenate([t0, f[1]], axis=1), 1)
    crossing = jnp.concatenate([packed2[:, :d], packed2[:, d + width :]], axis=1)
    if ring:
        def pair_send(own, *waits):
            own = after(own, *waits)
            return [own] + [fsdp_permute(own, flip) for flip in (2, 4, 6)]

        gate_w = pair_send(own_units[0], *first, pieces[1], pieces[3])
        crossing = after(crossing, *pieces[1::2], *gate_w)
    packed3 = seq_permute(crossing, 1)

    if ring:
        gate_w.append(fsdp_permute(jnp.concatenate(gate_w, axis=0), 1))
        up_w = pair_send(own_units[1], gate_w[1])
    g2 = seq_permute(after(g0, packed2, *pieces[1::2]), 2)

    q, k, v, normed, w_qkv, w_out = qkv(where, t0, f[0], (packed1, packed2, packed3), pieces, cosine, sine)
    gains = w_qkv[3 * width : 3 * width + 8]
    w_out_sent = w_out
    *m, lse_a = attention(0, me, q, k, v)
    g2 = after(g2, m[0])
    q = after(q, g2)
    g1, g3 = seq_permute(after(g0, g2), 1), seq_permute(g2, 1)
    if ring:
        up_w[1:] = all_after(up_w[1:], m[0])
        gate_w[4] = after(gate_w[4], m[0])
        up_w.append(fsdp_permute(jnp.concatenate(up_w, axis=0), 1))
        down_w = pair_send(own_units[2], *up_w[:4])
        q = after(q, gate_w[4])
    *m, lse_b = attention(1, me, q, k, v, *m)
    if ring:
        up_w[4] = after(up_w[4], m[0])
        down_w[1:] = all_after(down_w[1:], m[0])
        down_w.append(fsdp_permute(jnp.concatenate(down_w, axis=0), 1))
        m = all_after(m, up_w[4])
    m = exchange_four(m)
    if ring:
        m = all_after(m, *down_w[:4])
    w_out_sent = after(w_out_sent, m[2], m[3])
    w_out_other = [
        seq_permute(lax.slice_in_dim(w_out_sent, i * (d // 8), (i + 1) * (d // 8)), 1) for i in range(4)
    ]
    if ring:
        unit_pieces = [gate_w, up_w, down_w]
    m = all_after(m, *w_out_other)
    middle, *s0 = vmem_call(
        out_kernel,
        "out",
        [((rows, d), F32)] + [((rows // 2, d), BF16)] * 2,
        me,
        [*m, w_out, *w_out_other, t0, gains],
        cost(2 * rows * d * d, 8e6),
    )
    s1 = [seq_permute(one, 1) for one in s0]
    s2 = [seq_permute(one, 2) for one in s0]
    hid_near, gate_near, up_near, sb0, sb1 = mlp(where, s0, s1, g0, g1, unit_pieces)
    s2 = all_after(s2, sb0)
    s3 = [seq_permute(one, 1) for one in s2]
    hid_far, gate_far, up_far, sb2, sb3 = mlp(where, s2, s3, g2, g3, unit_pieces)
    sb_both = add(sb2, seq_permute(sb3, 1))
    p = [sb0, seq_permute(after(sb1, sb_both), 1), seq_permute(sb_both, 2)]

    (down_part,) = unit_grads([(hid_near, after(hid_far, p[1]))], (g0, g1, g2, g3))
    if ring:
        down_crossed = fsdp_permute(down_part[1], 1)
    o = vmem_call(
        functools.partial(mlp_out_kernel, len(unit_pieces[2])),
        "mlp_out",
        [((rows, d), BF16)] * 4,
        where.reshape(1),
        [hid_near, after(hid_far, down_part[0]), *unit_pieces[2]],
        cost(2 * 4 * rows * d * units, 8e6),
        [pltpu.VMEM((units, d), BF16)],
    )
    (gate_part,) = unit_grads([(gate_near, after(gate_far, o[0]))], (*s0, *s1, *s2, *s3))
    o1, o3 = all_after([seq_permute(o[1], 1), seq_permute(o[3], 1)], gate_part[0])
    p[2] = after(p[2], gate_part[0])
    p[0] = after(p[0], o3, o1)
    if ring:
        down_both = add(down_part[0], after(down_crossed, p[2]))
        p[2] = after(p[2], down_both)
        gate_crossed = fsdp_permute(after(gate_part[1], down_both), 1)
        mixed_beside = seq_permute(jnp.concatenate(m, axis=1), 1)
        p[0] = after(p[0], mixed_beside)
    mback, mlow, mhalf, b0, b1, b2, b3, ggrad_second = vmem_call(
        middle_kernel,
        "middle",
        [((rows, d), F32), ((rows, d), BF16), ((rows, d // 2), BF16)]
        + [((rows, width), BF16)] * 4
        + [((8, d), F32)],
        me,
        [*p, middle, g0, gains, w_out, *w_out_other],
        cost(2 * rows * d * d, 12e6),
    )
    b = exchange_four([b0, b1, b2, b3])
    o_both = add(o[2], after(o3, mlow))
    flat = lambda x: x.reshape(4 * rows, -1)
    qb = q
    if ring:
        low_beside = seq_permute(mhalf, 1)
        out_part = vmem_call(
            out_grad_kernel,
            "out_grad",
            [((n // 2, d // 2 + 8, share), BF16)] * 2,
            place3[0],
            [*m, mixed_beside, mlow, low_beside, ggrad_second],
            cost(2 * rows * d * d, 6e6),
            [pltpu.VMEM((d // 2, d), F32)],
        )
        (up_part,) = unit_grads([(up_near, after(up_far, out_part[0]))], (*s0, *s1, *s2, *s3))
        b[1:] = all_after(b[1:], up_part[0], o_both)
        down_sent = fsdp_send(after(down_both, b[2], b[3]))
    else:
        (up_part,) = unit_grads([(up_near, up_far)], (*s0, *s1, *s2, *s3))

    def qkv_grads(d_a, d_b):
        if ring:
            return vmem_call(
                qkv_grad_kernel,
                "qkv_grad",
                [((n // 2, 6 * pair + 8, share), BF16)] * 2,
                place3[0],
                [flat(normed), flat(d_a), flat(d_b), w_qkv],
                cost(2 * 4 * rows * d * 6 * pair, 6e6),
                [pltpu.VMEM((6 * pair, d), F32)],
            )
        whole = tn(jnp.concatenate([flat(d_a), flat(d_b)], axis=1), flat(normed))
        starts = [i * width + part * pair for part in range(2) for i in range(3)]
        w = jnp.concatenate([w_qkv[i : i + pair] for i in starts]).astype(F32)
        gain_part = jnp.sum(whole * w, axis=0, keepdims=True) / gains[:1].astype(F32)
        whole = jnp.concatenate([whole, gain_part, jnp.zeros((7, d), F32)]).astype(BF16)
        return (jnp.transpose(whole.reshape(6 * pair + 8, n, share), (1, 0, 2)),)

    d_a, v_a = attention_back(0, me, qb, k, v, b, lse_a, cosine, sine)
    o2 = seq_permute(after(o_both, d_a), 2)
    qb = after(qb, d_a)
    if ring:
        gate_both = add(gate_part[0], after(gate_crossed, d_a))
        down_share = add(*all_after(down_sent, d_a))
        gate_sent = fsdp_send(after(gate_both, down_share))
        up_crossed = fsdp_permute(after(up_part[1], gate_both), 1)
        qb = after(qb, gate_both, down_share)
    d_b, v_b = attention_back(1, me, qb, k, v, b, lse_b, cosine, sine, v_a)
    o2 = after(o2, d_b)
    d_b = after(d_b, o2)
    if ring:
        up_crossed, *gate_sent = all_after([up_crossed] + gate_sent, d_b)
        up_both = add(up_part[0], up_crossed)
        gate_share = add(*gate_sent)
        up_sent = fsdp_send(after(up_both, gate_share))
        out_crossed = fsdp_permute(after(out_part[1], up_both), 1)
        d_b = after(d_b, up_both, gate_share)

    nb3, nb2, nb1 = vmem_call(
        normed_back_kernel,
        "normed_back",
        [((rows, d), BF16)] * 3,
        me,
        [d_a, d_b, w_qkv],
        cost(2 * 3 * rows * d * 3 * width, 8e6),
    )
    nb_both = add(nb2, seq_permute(nb3, 1))
    beside = seq_permute(nb1, 1)
    crossed_far = seq_permute(nb_both, 2)
    qkv_sums = qkv_grads(d_a, after(d_b, nb_both, beside))
    output = add(middle, o[0], o1, o2)[None]
    crossed_far = after(crossed_far, qkv_sums[0], output)
    if ring:
        out_both = add(out_part[0], after(out_crossed, qkv_sums[0]))
        qkv_crossed = fsdp_permute(after(qkv_sums[1], out_both), 1)
        up_share = add(*all_after(up_sent, qkv_sums[0]))
        out_sent = fsdp_send(after(out_both, up_share))
        beside = after(beside, up_share)
        units_sent = jnp.concatenate([gate_share, up_share, down_share], axis=0)
        units_far = seq_permute(units_sent, 2)
    (tokens_grad,) = vmem_call(
        final_kernel,
        "final",
        [((rows, d), F32)],
        me,
        [beside, crossed_far, d_a, d_b, w_qkv, t0, gains, mback],
        cost(0, 6e6),
    )
    if ring:
        units_far = after(units_far, tokens_grad)
        qkv_both = add(qkv_sums[0], after(qkv_crossed, tokens_grad))
        out_share = add(*all_after(out_sent, tokens_grad))
        qkv_sent = fsdp_send(after(qkv_both, out_share))
    else:
        gate_share, up_share, down_share, qkv_share = (
            scatter_whole(v[0]) for v in (gate_part, up_part, down_part, qkv_sums)
        )
        mixed_rows = jnp.zeros((rows, d), BF16)
        for r in range(4):
            mixed_rows = lax.dynamic_update_slice(mixed_rows, m[r], (0, (s ^ r) * width))
        out_part = tn(mlow, mixed_rows)
        halves = [lax.dynamic_slice_in_dim(out_part, (core ^ j) * (d // 2), d // 2) for j in range(2)]
        keep = jnp.concatenate([halves[0], ggrad_second]).reshape(d // 2 + 8, n, share)
        send = jnp.pad(halves[1], ((0, 8), (0, 0))).astype(BF16).reshape(d // 2 + 8, n, share)
        whole = (keep + seq_permute(send, 1).astype(F32)).astype(BF16)
        out_share = scatter_whole(jnp.transpose(whole, (1, 0, 2)))
        units_sent = jnp.concatenate([gate_share, up_share, down_share], axis=0)
    if not ring:
        units_far = seq_permute(units_sent, 2)
    units_all = [units_sent, seq_permute(units_sent, 1), units_far, seq_permute(units_far, 1)]
    v_all = lax.all_to_all(after(v_b, tokens_grad), "seq", split_axis=0, concat_axis=0)
    (values_grad,) = vmem_call(
        place_values_kernel, "place_values", [((rows, d), F32)], me, [v_all], cost(0, 3e6)
    )
    gate_grad, up_grad, down_grad = vmem_call(
        place_units_kernel,
        "place_units",
        [((share, 4 * units), F32)] * 3,
        me,
        units_all,
        cost(0, 3e6),
        [pltpu.VMEM((4, 3 * units, share), F32)],
    )
    if ring:
        out_far = after(seq_permute(after(out_share, qkv_both), 2), gate_grad)
    else:
        out_far = seq_permute(out_share, 2)
    out_share = add(out_share, out_far)
    out_grad, second_gain_grad = vmem_call(
        place_out_kernel,
        "place_out",
        [((share, d), F32), ((1, share), F32)],
        me,
        [out_share, seq_permute(out_share, 1)],
        cost(0, 1e6),
    )
    if ring:
        qkv_share = add(*all_after(qkv_sent, gate_grad, values_grad))
    qkv_far = after(seq_permute(qkv_share, 2), out_grad)
    qkv_all = [qkv_share, seq_permute(qkv_share, 1), qkv_far, seq_permute(qkv_far, 1)]
    query_grad, key_grad, value_grad, gain_grad = vmem_call(
        place_qkv_kernel,
        "place_qkv",
        [((share, d), F32)] * 3 + [((1, share), F32)],
        me,
        qkv_all,
        cost(0, 3e6),
    )
    return (
        output,
        tokens_grad[None],
        values_grad[None],
        gain_grad.reshape(share),
        query_grad,
        key_grad,
        value_grad,
        out_grad,
        second_gain_grad.reshape(share),
        gate_grad,
        up_grad,
        down_grad,
    )


def solution(mesh):
    rows = P("fsdp", "seq", None)
    weight = P("fsdp", None)
    gain = P("fsdp")
    in_specs = (rows,) * 3 + (gain,) + (weight,) * 4 + (gain,) + (weight,) * 3
    out_specs = (rows,) * 3 + (gain,) + (weight,) * 4 + (gain,) + (weight,) * 3
    return jax.shard_map(
        per_device, mesh=mesh, in_specs=in_specs, out_specs=out_specs, check_vma=False
    )
```
